32 devices in a mesh: head: 4 (over z), seq: 8 (over y, x, core).
Axes of the slice: x: 2, y: 2, z: 4, core: 2. Of those that a mesh axis runs over, the one named last changes fastest.
Arguments:
- hidden_in: bfloat16 [8192, 1536], P(('seq', 'head')), may hold values from -6 to 6
- out_grad: bfloat16 [8192, 1536], P(('seq', 'head')), may hold values from -6 to 6
- doc_lengths: int32 [32], replicated, may hold values from 1 to 1024, 8192 in all
- expert_ids: int32 [8192, 8], P(('seq', 'head')), may hold values from 0 to 15, all different within a row
- attention_norm: bfloat16 [1536], P(('head', 'seq')), may hold values from 0.5 to 1.5
- query_weight: bfloat16 [1536, 1536], P(('head', 'seq')), may hold values from -0.625 to 0.625
- key_matrix: bfloat16 [1536, 512], P(('head', 'seq')), may hold values from -0.625 to 0.625
- value_matrix: bfloat16 [1536, 512], P(('head', 'seq')), may hold values from -0.15625 to 0.15625
- output_weight: bfloat16 [1536, 1536], P(('head', 'seq')), may hold values from -2.5 to 2.5
- expert_norm: bfloat16 [1536], P(('head', 'seq')), may hold values from 0.5 to 1.5
- router_weight: bfloat16 [1536, 16], P(('head', 'seq')), may hold values from -0.078125 to 0.078125
- expert_input: bfloat16 [1536, 16, 1024], P(('head', 'seq')), may hold values from -0.15625 to 0.15625
- expert_output: bfloat16 [1536, 16, 512], P(('head', 'seq')), may hold values from -6 to 6
Outputs:
- block_out: bfloat16 [8192, 1536], P(('seq', 'head'))
- input_grad: float32 [8192, 1536], P(('seq', 'head'))
- attention_norm_grad: float32 [1536], P(('head', 'seq'))
- query_grad: float32 [1536, 1536], P(('head', 'seq'))
- key_grad: float32 [1536, 512], P(('head', 'seq'))
- value_grad: float32 [1536, 512], P(('head', 'seq'))
- output_grad: float32 [1536, 1536], P(('head', 'seq'))
- expert_norm_grad: float32 [1536], P(('head', 'seq'))
- router_grad: float32 [1536, 16], P(('head', 'seq'))
- expert_input_grad: float32 [1536, 16, 1024], P(('head', 'seq'))
- expert_output_grad: float32 [1536, 16, 512], P(('head', 'seq'))
The draws below stay inside these ranges and needn't reach their ends.
Inputs may be any that keep to these rules, and one draw needn't show every extreme that they name: `doc_lengths`: the lengths sum to 8192; one document has exactly 1024 tokens. `expert_ids`: the 8 experts of a token are different.
All inputs are finite; a program needn't handle non-finite values.
Results may differ from the reference program's by a relative error of at most 0.017.
The reference program's roundings to bfloat16 on the way count: a program that leaves them out, or rounds other values in their place, can miss the bound.
Values may be sent and summed in bfloat16 or wider, within the bound.
No kernel may reach another device: no remote copies, remote signals or barrier semaphores. Data moves between devices by JAX's collectives and lax.ppermute only.
A program may use at most 576 MiB of HBM per device.

```python
import math
import jax
import jax.numpy as jnp
import numpy as np
from jax import lax

MODEL_WIDTH = 1536
QUERY_HEADS = 24
KEY_VALUE_HEADS = 8
HEAD_WIDTH = 64
FF = 512
TOPK = 8
EXPERTS = 16
QUERY_BLOCK_ROWS = 512
TOK_DEV = 256
DOCUMENT_SPAN = 1024
TOKENS = 8192
NDOCS = 32
CAP = 160


def spiked(array, stream_key, source, target, shards_of, factor):
    def block_of(dim):
        return (jnp.arange(array.shape[dim]) // (array.shape[dim] // shards_of)).reshape((-1,) + (1,) * (array.ndim - 1 - dim))

    one_side = jax.random.permutation(stream_key, shards_of)[block_of(target)]
    far = (block_of(target) + shards_of // 2) % shards_of
    return jnp.where((block_of(source) == one_side) | (block_of(source) == far), factor * array, array)


def level_of(stream_key, dims, shards, least, top_value):
    level = 1.0
    for position, blocks in shards:
        steps = jax.random.uniform(jax.random.fold_in(jax.random.fold_in(stream_key, 6), position), (blocks,), jnp.float32, least / len(shards), top_value / len(shards))
        level = level * jnp.repeat(jnp.exp(steps), dims[position] // blocks).reshape((-1,) + (1,) * (len(dims) - 1 - position))
    return level


def different_ones(stream_key, rows, count, top, lift):
    ranking = jax.random.permutation(jax.random.fold_in(stream_key, 1), count)
    boost = ranking
    for power in range(3):
        boost = boost * boost // count
    boost = boost * lift // count
    chance = jax.random.randint(jax.random.fold_in(stream_key, 2), (rows, count), 0, 4096) + boost
    holders = jax.random.permutation(jax.random.fold_in(stream_key, 3), rows)[jnp.arange(count) % rows]
    chance = jnp.where(jnp.arange(rows)[:, None] == holders[None, :], 1 << 14, chance)
    priority = chance * count + jnp.arange(count)
    return lax.top_k(priority.astype(jnp.int32), top)[1].astype(jnp.int32)


def split_up(count, total, reach, lean):
    portions = [(1 << 20) // math.isqrt(grade ** lean) + 1 for grade in range(2, count + 1)]
    spare, holding = total - reach - (count - 1), [1] * (count - 1)
    while spare > 0:
        movable = [i for i in range(count - 1) if holding[i] < reach]
        pool, left = sum([portions[i] for i in movable]), spare
        for i in movable:
            extra = min(reach - holding[i], max(1, left * portions[i] // pool), spare)
            holding[i] = holding[i] + extra
            spare = spare - extra
    return np.array([reach] + holding)


def uneven(stream_key, count, total, most, slope):
    if count == 2:
        one = jax.random.randint(stream_key, (), max(1, total - most), min(most, total - 1) + 1)
        return jnp.stack([one, total - one])
    tallies = jnp.asarray(split_up(count, total, most, slope), jnp.int32)
    couples = (count - 1) // 2
    giver, sink = tallies[1:1 + 2 * couples:2], tallies[2:2 + 2 * couples:2]
    room = jnp.minimum(giver - 1, most - sink)
    moved = jax.random.randint(jax.random.fold_in(stream_key, 1), (couples,), 0, 1 << 20) % (room + 1)
    tallies = tallies.at[1:1 + 2 * couples:2].set(giver - moved).at[2:2 + 2 * couples:2].set(sink + moved)
    return tallies[jax.random.permutation(jax.random.fold_in(stream_key, 2), count)]


def centred(stream_key, extent, scale, limit, cuts=(), kind=jnp.bfloat16):
    array = scale * jax.random.normal(stream_key, extent, jnp.float32)
    if cuts:
        array = array * level_of(stream_key, extent, cuts, -0.22, 0.18)
    return jnp.clip(array, -limit, limit).astype(kind)


def heavy_noise(own_key, shape, deviation, most, cuts, heavy, kind=jnp.bfloat16):
    values = deviation * jax.random.normal(own_key, shape, jnp.float32)
    if cuts:
        values = values * level_of(own_key, shape, cuts, -0.22, 0.18)
    return jnp.clip(spiked(values, jax.random.fold_in(own_key, 3), *heavy), -most, most).astype(kind)


def setup_inputs(seed: int = 0) -> dict:
    keys = jax.random.split(jax.random.key(seed), 14)
    return {
        "hidden_in": centred(keys[0], (TOKENS, MODEL_WIDTH), 1.0, 6.0, ((0, 32),)),
        "out_grad": heavy_noise(keys[1], (TOKENS, MODEL_WIDTH), 1.0, 6.0, ((0, 32),), (0, 1, 32, 2.75)),
        "doc_lengths": uneven(keys[2], NDOCS, TOKENS, DOCUMENT_SPAN, 2).astype(jnp.int32),
        "expert_ids": different_ones(keys[3], TOKENS, EXPERTS, TOPK, 4096),
        "attention_norm": jnp.clip(1.0 + 0.1 * jax.random.normal(keys[4], (MODEL_WIDTH,), jnp.float32), 0.5, 1.5).astype(jnp.bfloat16),
        "query_weight": centred(keys[5], (MODEL_WIDTH, QUERY_HEADS * HEAD_WIDTH), (MODEL_WIDTH // 16) ** -0.5, 0.625, ((0, 32),)),
        "key_matrix": centred(keys[6], (MODEL_WIDTH, KEY_VALUE_HEADS * HEAD_WIDTH), (MODEL_WIDTH // 16) ** -0.5, 0.625, ((0, 32),)),
        "value_matrix": centred(keys[7], (MODEL_WIDTH, KEY_VALUE_HEADS * HEAD_WIDTH), MODEL_WIDTH ** -0.5, 0.15625, ((0, 32),)),
        "output_weight": centred(keys[8], (MODEL_WIDTH, QUERY_HEADS * HEAD_WIDTH), (max(MODEL_WIDTH // 256, 1)) ** -0.5, 2.5, ((0, 32),)),
        "expert_norm": jnp.clip(1.0 + 0.1 * jax.random.normal(keys[9], (MODEL_WIDTH,), jnp.float32), 0.5, 1.5).astype(jnp.bfloat16),
        "router_weight": centred(keys[10], (MODEL_WIDTH, EXPERTS), (4 * MODEL_WIDTH) ** -0.5, 0.078125, ((0, 32),)),
        "expert_input": centred(keys[11], (MODEL_WIDTH, EXPERTS, 2 * FF), MODEL_WIDTH ** -0.5, 0.15625, ((0, 32),)),
        "expert_output": centred(keys[12], (MODEL_WIDTH, EXPERTS, FF), (max(FF // 512, 1)) ** -0.5, 6.0, ((0, 32),)),
    }


EPS = 1e-06
ATTN_SCALE = 1.0 / 64.0
RESIDUAL_SCALE = 0.22
MASKED = -1e+30
HIGHEST = lax.Precision.HIGHEST

@jax.custom_vjp
def lower_bound(v):
    return lax.optimization_barrier(v.astype(jnp.bfloat16)).astype(jnp.float32)

@jax.custom_vjp
def low_back(v):
    return v

def low_keep(v):
    return (lower_bound(v), None)

def low_pass(kept, grad):
    return (grad,)

def back_keep(v):
    return (v, None)

def back_low(kept, grad):
    return (lower_bound(grad),)
lower_bound.defvjp(low_keep, low_pass)
low_back.defvjp(back_keep, back_low)

def rms_norm(values, gain):
    return values * lax.rsqrt(lax.optimization_barrier(jnp.mean(values * values, axis=-1, keepdims=True)) + EPS) * gain

def doc_start(doc_lengths, places):
    starts = jnp.cumsum(doc_lengths) - doc_lengths
    earlier = starts[None, :] <= places[:, None]
    return lax.optimization_barrier(jnp.max(jnp.where(earlier, starts[None, :], 0), axis=1)).astype(jnp.int32)

def rope_tables(places):
    frequency = jnp.exp(-jnp.log(10000.0) * 2.0 * jnp.arange(HEAD_WIDTH // 2).astype(jnp.float32) / HEAD_WIDTH)
    angles = places.astype(jnp.float32)[:, None] * frequency[None, :]
    return (jnp.cos(angles), jnp.sin(angles))

def apply_rotation(values, cosine_lookup, sine_lookup, head_count):
    shaped = values.reshape(values.shape[0], head_count, 2, HEAD_WIDTH // 2)
    first_half = shaped[:, :, 0, :]
    second_half = shaped[:, :, 1, :]
    cos_part = cosine_lookup[:, None, :]
    sin_part = sine_lookup[:, None, :]
    turned = jnp.stack([first_half * cos_part - second_half * sin_part, second_half * cos_part + first_half * sin_part], axis=2)
    return turned.reshape(values.shape)

def assign_slots(identities):
    flat_ids = identities.reshape(-1).astype(jnp.int32)
    claims = flat_ids.shape[0]
    chosen_hot = (flat_ids[:, None] == jnp.arange(EXPERTS).astype(jnp.int32)[None, :]).astype(jnp.int32)
    earlier = jnp.cumsum(chosen_hot, axis=0) - chosen_hot
    slot_of = lax.optimization_barrier(jnp.sum(earlier * chosen_hot, axis=1)).astype(jnp.int32)
    destination = jnp.where(slot_of < CAP, flat_ids * CAP + slot_of, EXPERTS * CAP).astype(jnp.int32)
    ordinal = jnp.arange(claims).astype(jnp.int32)
    token_of = jnp.full((EXPERTS * CAP + 1,), claims // TOPK, jnp.int32).at[destination].set(ordinal // TOPK)
    claim_of = jnp.full((EXPERTS * CAP + 1,), claims, jnp.int32).at[destination].set(ordinal)
    return (destination, token_of[:-1], claim_of[:-1])

def attention(query_rows, key_row_list, value_row_list, starts):
    group_width = QUERY_HEADS // KEY_VALUE_HEADS
    width_extent = DOCUMENT_SPAN + QUERY_BLOCK_ROWS
    key_padding = jnp.concatenate([jnp.zeros((DOCUMENT_SPAN, KEY_VALUE_HEADS * HEAD_WIDTH), key_row_list.dtype), key_row_list], axis=0)
    value_padding = jnp.concatenate([jnp.zeros((DOCUMENT_SPAN, KEY_VALUE_HEADS * HEAD_WIDTH), value_row_list.dtype), value_row_list], axis=0)

    def one_block(block_id):
        leading_row = (block_id * QUERY_BLOCK_ROWS).astype(jnp.int32)
        query_tile_block = lax.dynamic_slice_in_dim(query_rows, leading_row, QUERY_BLOCK_ROWS, 0).reshape(QUERY_BLOCK_ROWS, KEY_VALUE_HEADS, group_width, HEAD_WIDTH)
        key_tile_block = lax.dynamic_slice_in_dim(key_padding, leading_row, width_extent, 0).reshape(width_extent, KEY_VALUE_HEADS, HEAD_WIDTH)
        value_tile_block = lax.dynamic_slice_in_dim(value_padding, leading_row, width_extent, 0).reshape(width_extent, KEY_VALUE_HEADS, HEAD_WIDTH)
        start_block = lax.dynamic_slice_in_dim(starts, leading_row, QUERY_BLOCK_ROWS, 0)
        query_place = leading_row + jnp.arange(QUERY_BLOCK_ROWS).astype(jnp.int32)
        key_place = leading_row - DOCUMENT_SPAN + jnp.arange(width_extent).astype(jnp.int32)
        visible = (key_place[None, :] >= start_block[:, None]) & (key_place[None, :] <= query_place[:, None])
        raw_scores = low_back(jnp.einsum('qhgd,khd->hgqk', query_tile_block, key_tile_block, precision=HIGHEST))
        scaled = jnp.where(visible[None, None], raw_scores * ATTN_SCALE, MASKED)
        soft_weights = jax.nn.softmax(scaled, axis=-1)
        mixture = jnp.einsum('hgqk,khd->qhgd', lower_bound(soft_weights), value_tile_block, precision=HIGHEST)
        return mixture.reshape(QUERY_BLOCK_ROWS, QUERY_HEADS * HEAD_WIDTH)
    block_ids = jnp.arange(TOKENS // QUERY_BLOCK_ROWS).astype(jnp.int32)
    return lax.map(jax.checkpoint(one_block), block_ids).reshape(TOKENS, QUERY_HEADS * HEAD_WIDTH)

def experts(normed_two, gates, identities, inner_weight, outer_weight):
    groups = TOKENS // TOK_DEV

    def one_group(pieces):
        row_block, gate_rows, id_rows = pieces
        destination, token_of, claim_of = assign_slots(id_rows)
        padded = jnp.concatenate([row_block, jnp.zeros((1, MODEL_WIDTH), row_block.dtype)], axis=0)
        dispatched = padded[token_of].reshape(EXPERTS, CAP, MODEL_WIDTH)
        gate_up = low_back(jnp.einsum('ecd,dej->ecj', dispatched, inner_weight, precision=HIGHEST))
        activation = lower_bound(jax.nn.silu(gate_up[..., :FF]) * gate_up[..., FF:])
        returned = lower_bound(low_back(jnp.einsum('ecf,def->ecd', activation, outer_weight, precision=HIGHEST)))
        flat_out = jnp.concatenate([returned.reshape(EXPERTS * CAP, MODEL_WIDTH), jnp.zeros((1, MODEL_WIDTH), returned.dtype)], axis=0)
        picked = flat_out[destination].reshape(TOK_DEV, TOPK, MODEL_WIDTH)
        return lax.optimization_barrier(jnp.sum(picked * gate_rows[:, :, None], axis=1))
    mixed = lax.map(jax.checkpoint(one_group), (normed_two.reshape(groups, TOK_DEV, MODEL_WIDTH), gates.reshape(groups, TOK_DEV, TOPK), identities.reshape(groups, TOK_DEV, TOPK)))
    return mixed.reshape(TOKENS, MODEL_WIDTH)

def reference(hidden_in, out_grad, doc_lengths, expert_ids, attention_norm, query_weight, key_matrix, value_matrix, output_weight, expert_norm, router_weight, expert_input, expert_output):
    places = jnp.arange(TOKENS).astype(jnp.int32)
    starts = doc_start(doc_lengths, places)
    cosine_lookup, sine_lookup = rope_tables(places - starts)
    chosen_hot = (expert_ids[:, :, None] == jnp.arange(EXPERTS).astype(jnp.int32)[None, None, :]).astype(jnp.float32)

    def forward(stream, attn_gain, w_query, w_key, w_value, w_output, second_gain, w_router, w_inner, w_outer):
        normed = lower_bound(rms_norm(stream, attn_gain))
        query_lin = low_back(jnp.dot(normed, w_query, precision=HIGHEST))
        key_linear = low_back(jnp.dot(normed, w_key, precision=HIGHEST))
        value_row_list = lower_bound(low_back(jnp.dot(normed, w_value, precision=HIGHEST)))
        query_rows = lower_bound(apply_rotation(query_lin, cosine_lookup, sine_lookup, QUERY_HEADS))
        key_row_list = lower_bound(apply_rotation(key_linear, cosine_lookup, sine_lookup, KEY_VALUE_HEADS))
        mixture = lower_bound(low_back(attention(query_rows, key_row_list, value_row_list, starts)))
        branch = low_back(jnp.dot(mixture, w_output.T, precision=HIGHEST))
        middle = stream + RESIDUAL_SCALE * branch
        normed_two = lower_bound(rms_norm(middle, second_gain))
        logits = low_back(jnp.dot(normed_two, w_router, precision=HIGHEST))
        chosen = lax.optimization_barrier(jnp.sum(chosen_hot * logits[:, None, :], axis=-1))
        gates = jax.nn.softmax(chosen, axis=-1)
        return middle + RESIDUAL_SCALE * experts(normed_two, gates, expert_ids, w_inner, w_outer)
    primals = (hidden_in.astype(jnp.float32), attention_norm.astype(jnp.float32), query_weight.astype(jnp.float32), key_matrix.astype(jnp.float32), value_matrix.astype(jnp.float32), output_weight.astype(jnp.float32), expert_norm.astype(jnp.float32), router_weight.astype(jnp.float32), expert_input.astype(jnp.float32), expert_output.astype(jnp.float32))
    result, pull_back = jax.vjp(forward, *primals)
    grads = pull_back(out_grad.astype(jnp.float32))
    return (result.astype(jnp.bfloat16), grads[0], grads[1], grads[2], grads[3], grads[4], grads[5], grads[6], grads[7], grads[8], grads[9])
```

```python
import functools

import jax
import jax.numpy as jnp
from jax import lax
from jax.experimental import pallas as pl
from jax.experimental.pallas import tpu as pltpu
from jax.sharding import PartitionSpec as P

MODEL_WIDTH = 1536
QUERY_HEADS = 24
KEY_VALUE_HEADS = 8
HEAD_WIDTH = 64
FF = 512
EXPERTS = 16
CAP = 160

EPS = 1e-06
ATTN_SCALE = 1.0 / 64.0
RESIDUAL_SCALE = 0.22
MASKED = -1e30

GROUP = QUERY_HEADS // KEY_VALUE_HEADS
QUERY_COLS = QUERY_HEADS * HEAD_WIDTH
PAIR_COLS = KEY_VALUE_HEADS * HEAD_WIDTH
LANES = 128
HALF = HEAD_WIDTH // 2
PAIRED = LANES // HEAD_WIDTH
EXPERT_COLS = 3 * FF

bf16 = jnp.bfloat16
f32 = jnp.float32

NT = (((1,), (1,)), ((), ()))
TN = (((0,), (0,)), ((), ()))
VMEM_BYTES = 56 * 1024 * 1024


def dot(left, right, dims=(((1,), (0,)), ((), ()))):
    return lax.dot_general(left, right, dims, preferred_element_type=f32)


def swap(block, mask):
    count = lax.axis_size("seq")
    return lax.ppermute(block, "seq", [(i, i ^ mask) for i in range(count)])


def around(block, distance):
    count = lax.axis_size("head")
    return lax.ppermute(block, "head", [(i, (i + distance) % count) for i in range(count)])


def along_stream(block, distance):
    heads, groups = lax.axis_size("head"), lax.axis_size("seq")
    route = []
    for group in range(groups):
        for head in range(heads):
            target = group * heads + head + distance
            if 0 <= target < heads * groups:
                route.append((head * groups + group, (target % heads) * groups + target // heads))
    return lax.ppermute(block, ("head", "seq"), route)


def side(mask):
    return (lax.axis_index("seq") // mask) % 2


def far_masks():
    masks, mask = [], 2
    while mask < lax.axis_size("seq"):
        masks.append(mask)
        mask = mask * 2
    return masks


def join(own, other, bit, axis):
    return jnp.where(
        bit == 0, jnp.stack([own, other], axis=axis), jnp.stack([other, own], axis=axis)
    )


def swap_head(block, mask):
    count = lax.axis_size("head")
    return lax.ppermute(block, "head", [(i, i ^ mask) for i in range(count)])


def head_side(mask):
    return (lax.axis_index("head") // mask) % 2


def after(value, *others):
    return lax.optimization_barrier((value,) + others)[0]


class Flow:
    def __init__(self, steps):
        self.steps = steps
        self.value = None
        self.moves = []
        self.done = False
        self.feed(None)

    def feed(self, results):
        try:
            self.moves = self.steps.send(results)
        except StopIteration as stop:
            self.value, self.moves, self.done = stop.value, [], True


class Clock:
    def __init__(self):
        self.last = ()

    def begin(self, *flows, ready=()):
        flows = [flow for flow in flows if not flow.done]
        blocks = tuple(block for flow in flows for block, _ in flow.moves)
        if not blocks:
            return [], []
        tied = lax.optimization_barrier(blocks + tuple(self.last) + tuple(ready))
        movers = [move for flow in flows for _, move in flow.moves]
        return flows, [move(block) for move, block in zip(movers, tied)]

    def end(self, pending, *held):
        flows, results = pending
        if not results:
            return
        if held:
            results = list(lax.optimization_barrier(tuple(results) + held)[: len(results)])
        self.last = tuple(results)
        for flow in flows:
            count = len(flow.moves)
            flow.feed(results[:count])
            results = results[count:]

    def tick(self, *flows, ready=()):
        self.end(self.begin(*flows, ready=ready))

    def finish(self, *flows):
        while not all(flow.done for flow in flows):
            self.tick(*flows)
        return flows[0].value if len(flows) == 1 else [flow.value for flow in flows]


def by_seq(mask):
    return lambda block: swap(block, mask)


def by_head(mask):
    return lambda block: swap_head(block, mask)


def one_move(block, move):
    (result,) = yield [(block, move)]
    return result


def line_gather(block):
    heads = lax.axis_size("head")
    here = lax.axis_index("head")
    whole = jnp.zeros((heads,) + block.shape, block.dtype)
    whole = lax.dynamic_update_index_in_dim(whole, block, here, 0)
    results = yield [
        (block, functools.partial(around, distance=distance)) for distance in range(1, heads)
    ]
    for distance, result in enumerate(results, 1):
        whole = lax.dynamic_update_index_in_dim(whole, result, (here - distance) % heads, 0)
    return whole


def rows_gather(block):
    lines = yield from line_gather(block)
    masks = far_masks()
    middle = lines.shape[0] // 2
    parts = [(lines[:middle], masks), (lines[middle:], masks[::-1])]
    for step in range(len(masks)):
        results = yield [(part, by_seq(order[step])) for part, order in parts]
        parts = [
            (
                join(
                    part,
                    result,
                    side(order[step]),
                    1 + sum(1 for other in order[:step] if other > order[step]),
                ),
                order,
            )
            for (part, order), result in zip(parts, results)
        ]
    whole = jnp.concatenate([part for part, _ in parts], axis=0)
    (result,) = yield [(whole, by_seq(1))]
    whole = join(whole, result, side(1), 1 + len(masks))
    return whole.reshape(MODEL_WIDTH, block.shape[1])


def rows_scatter(kept, sent):
    masks = far_masks()
    (result,) = yield [(sent, by_seq(1))]
    whole = (kept.astype(f32) + result.astype(f32)).astype(bf16)
    whole = whole.reshape(whole.shape[:1] + (2,) * len(masks) + whole.shape[2:])
    middle = whole.shape[0] // 2
    parts = [(whole[:middle], masks), (whole[middle:], masks[::-1])]
    for step in range(len(masks)):
        axes = [
            1 + sum(1 for other in order[step + 1 :] if other > order[step])
            for _, order in parts
        ]
        results = yield [
            (lax.index_in_dim(part, 1, axis, False), by_seq(order[step]))
            for (part, order), axis in zip(parts, axes)
        ]
        parts = [
            (
                (
                    lax.index_in_dim(part, 0, axis, False).astype(f32) + result.astype(f32)
                ).astype(bf16),
                order,
            )
            for (part, order), axis, result in zip(parts, axes, results)
        ]
    return jnp.concatenate([part for part, _ in parts], axis=0)


def line_scatter(terms):
    heads = lax.axis_size("head")
    here = lax.axis_index("head")
    results = yield [
        (
            lax.dynamic_index_in_dim(terms, (here + distance) % heads, 0, False),
            functools.partial(around, distance=distance),
        )
        for distance in range(1, heads)
    ]
    total = lax.dynamic_index_in_dim(terms, here, 0, False).astype(f32)
    for result in results:
        total = total + result.astype(f32)
    return total


def tokens_gather(block):
    masks = far_masks()
    middle = block.shape[0] // 2
    parts = [(block[:middle], masks), (block[middle:], masks[::-1])]
    for step in range(len(masks)):
        results = yield [(part, by_seq(order[step])) for part, order in parts]
        parts = [
            (
                jnp.stack(
                    [part, result],
                    axis=sum(1 for other in order[:step] if other > order[step]),
                ),
                order,
            )
            for (part, order), result in zip(parts, results)
        ]
    whole = jnp.concatenate([part for part, _ in parts], axis=len(masks))
    return whole.reshape((lax.axis_size("seq") // 2 * block.shape[0],) + block.shape[1:])


def tokens_scatter(own, other):
    masks = far_masks()
    blocks = lax.axis_size("seq") // 2
    (result,) = yield [(other, by_seq(1))]
    whole = (own.astype(f32) + result.astype(f32)).astype(bf16)
    whole = whole.reshape((2,) * len(masks) + (own.shape[0] // blocks, own.shape[1]))
    middle = whole.shape[-2] // 2
    parts = [(whole[..., :middle, :], masks), (whole[..., middle:, :], masks[::-1])]
    for step in range(len(masks)):
        axes = [sum(1 for other in order[step + 1 :] if other > order[step]) for _, order in parts]
        results = yield [
            (lax.index_in_dim(part, 1, axis, False), by_seq(order[step]))
            for (part, order), axis in zip(parts, axes)
        ]
        last = step == len(masks) - 1
        parts = [
            (
                (
                    lax.index_in_dim(part, 0, axis, False).astype(f32) + result.astype(f32)
                ).astype(f32 if last else bf16),
                order,
            )
            for (part, order), axis, result in zip(parts, axes, results)
        ]
    return jnp.concatenate([part for part, _ in parts], axis=0)


def doc_start(doc_lengths, places):
    starts = jnp.cumsum(doc_lengths) - doc_lengths
    earlier = starts[None, :] <= places[:, None]
    return jnp.max(jnp.where(earlier, starts[None, :], 0), axis=1)


def rope_tables(places):
    frequency = jnp.exp(
        -jnp.log(10000.0) * 2.0 * jnp.arange(HALF).astype(f32) / HEAD_WIDTH
    )
    angles = places.astype(f32)[:, None] * frequency[None, :]
    cosine, sine = jnp.cos(angles), jnp.sin(angles)
    return (
        jnp.concatenate([cosine] * (LANES // HALF), axis=1),
        jnp.concatenate([-sine, sine] * PAIRED, axis=1),
    )


def turn(values, cosine, sine, sign):
    lane = lax.broadcasted_iota(jnp.int32, (values.shape[0], LANES), 1) % HEAD_WIDTH
    pieces = []
    for first in range(0, values.shape[1], LANES):
        piece = values[:, first : first + LANES]
        swapped = jnp.where(
            lane < HALF, pltpu.roll(piece, LANES - HALF, 1), pltpu.roll(piece, HALF, 1)
        )
        pieces.append(piece * cosine + (sign * swapped) * sine)
    return jnp.concatenate(pieces, axis=1)


def whole_block(shape):
    return pl.BlockSpec(shape, lambda *_: (0,) * len(shape), pipeline_mode=pl.Buffered(1))


def params():
    return pltpu.CompilerParams(vmem_limit_bytes=VMEM_BYTES)


def cost(flops, moved, transcendentals=0, weight=1):
    return pl.CostEstimate(
        flops=weight * flops,
        bytes_accessed=weight * moved,
        transcendentals=weight * transcendentals,
    )


def rms_inverse(values):
    return lax.rsqrt(jnp.mean(values * values, axis=1, keepdims=True) + EPS)


def norm_backward(values, inverse, gain, incoming):
    scaled = incoming * gain
    mean_term = jnp.mean(scaled * values, axis=1, keepdims=True)
    values_grad = inverse * scaled - values * (inverse * inverse * inverse * mean_term)
    gain_grad = jnp.sum(incoming * values * inverse, axis=0, keepdims=True)
    return (values_grad, gain_grad)


def enter(hidden_in, w_small, cosine, sine):
    tokens = hidden_in.shape[0]
    small_cols = w_small.shape[1]

    def kernel(hidden_ref, weight_ref, cosine_ref, sine_ref, normed_ref, kv_ref, gain_ref):
        extras = jnp.transpose(weight_ref[:, 2 * PAIR_COLS :].astype(f32))
        gains = extras[EXPERTS : EXPERTS + 8]
        gain_ref[...] = gains
        values = hidden_ref[...].astype(f32)
        normed = (values * rms_inverse(values) * gains[:1]).astype(bf16)
        normed_ref[...] = normed
        keys = dot(normed, weight_ref[:, :PAIR_COLS])
        kv_ref[0] = turn(keys, cosine_ref[...], sine_ref[...], 1.0).astype(bf16)
        kv_ref[1] = dot(normed, weight_ref[:, PAIR_COLS : 2 * PAIR_COLS]).astype(bf16)

    return pl.pallas_call(
        kernel,
        out_shape=[
            jax.ShapeDtypeStruct((tokens, MODEL_WIDTH), bf16),
            jax.ShapeDtypeStruct((2, tokens, PAIR_COLS), bf16),
            jax.ShapeDtypeStruct((8, MODEL_WIDTH), f32),
        ],
        compiler_params=params(),
        cost_estimate=cost(
            4 * tokens * MODEL_WIDTH * PAIR_COLS, 2 * MODEL_WIDTH * (small_cols + 2 * tokens)
        ),
        name="enter",
    )(hidden_in, w_small, cosine, sine)


def project_queries(normed, w_square, cosine, sine):
    tokens = normed.shape[0]
    width = 512

    def kernel(normed_ref, weight_ref, cosine_ref, sine_ref, out_ref):
        product = dot(normed_ref[...], weight_ref[...])
        out_ref[...] = turn(product, cosine_ref[...], sine_ref[...], 1.0).astype(bf16)

    return pl.pallas_call(
        kernel,
        grid=(QUERY_COLS // width,),
        in_specs=[
            whole_block((tokens, MODEL_WIDTH)),
            pl.BlockSpec((MODEL_WIDTH, width), lambda i: (0, i)),
            whole_block((tokens, LANES)),
            whole_block((tokens, LANES)),
        ],
        out_specs=pl.BlockSpec((tokens, width), lambda i: (0, i)),
        out_shape=jax.ShapeDtypeStruct((tokens, QUERY_COLS), bf16),
        compiler_params=params(),
        cost_estimate=cost(
            2 * tokens * MODEL_WIDTH * QUERY_COLS, 2 * MODEL_WIDTH * (QUERY_COLS + 2 * tokens)
        ),
        name="project_queries",
    )(normed, w_square, cosine, sine)


def square_block(index):
    return pl.BlockSpec(
        (MODEL_WIDTH, MODEL_WIDTH), lambda *_: (0, index), pipeline_mode=pl.Buffered(1)
    )


def leave_attention(mixture, w_square, hidden_in, gains):
    tokens = mixture.shape[0]

    def kernel(mixture_ref, weight_ref, hidden_ref, gain_ref, middle_ref, normed_ref):
        branch = dot(mixture_ref[...], weight_ref[...], NT)
        middle = hidden_ref[...].astype(f32) + RESIDUAL_SCALE * branch
        middle_ref[...] = middle
        normed_ref[...] = (middle * rms_inverse(middle) * gain_ref[1:2]).astype(bf16)

    return pl.pallas_call(
        kernel,
        grid=(1,),
        in_specs=[
            whole_block((tokens, QUERY_COLS)),
            square_block(1),
            whole_block((tokens, MODEL_WIDTH)),
            whole_block((8, MODEL_WIDTH)),
        ],
        out_specs=[whole_block((tokens, MODEL_WIDTH))] * 2,
        out_shape=[
            jax.ShapeDtypeStruct((tokens, MODEL_WIDTH), f32),
            jax.ShapeDtypeStruct((tokens, MODEL_WIDTH), bf16),
        ],
        compiler_params=params(),
        cost_estimate=cost(
            2 * tokens * MODEL_WIDTH * QUERY_COLS, 2 * MODEL_WIDTH * (QUERY_COLS + 5 * tokens)
        ),
        name="leave_attention",
    )(mixture, w_square, hidden_in, gains)


def return_to_attention(back, back_parts, code, normed_two, middle, out_grad, w_small, w_square, gains):
    tokens = middle.shape[0]
    parts = len(back_parts)

    def kernel(
        back_ref,
        code_ref,
        normed_ref,
        middle_ref,
        grad_ref,
        router_ref,
        weight_ref,
        gain_ref,
        *refs,
    ):
        logits_grad_ref, middle_grad_ref, branch_grad_ref, mixture_grad_ref, gain_grad_ref = refs[
            parts:
        ]
        total = back_ref[...]
        for ref in refs[:parts]:
            total = total + ref[...].astype(f32)
        code = code_ref[...].astype(f32)
        lane = lax.broadcasted_iota(jnp.int32, (tokens, LANES), 1)
        router = jnp.where(
            lax.broadcasted_iota(jnp.int32, (MODEL_WIDTH, LANES), 1) < EXPERTS,
            router_ref[...],
            jnp.asarray(0.0, bf16),
        )
        logits = jnp.where(code > 0.5, dot(normed_ref[...], router), MASKED)
        raised = jnp.exp(logits - jnp.max(logits, axis=1, keepdims=True))
        raised = jnp.where(code > 0.5, raised, 0.0)
        gates = raised / jnp.sum(raised, axis=1, keepdims=True)
        extra = total[:, MODEL_WIDTH:]
        gate_grad = extra + pltpu.roll(extra, LANES - EXPERTS, 1)
        gate_grad = jnp.where((lane < EXPERTS) & (code > 0.5) & (code < 1.5), gate_grad, 0.0)
        inner = jnp.sum(gates * gate_grad, axis=1, keepdims=True)
        logits_grad = (gates * (gate_grad - inner)).astype(bf16)
        logits_grad_ref[...] = logits_grad
        incoming = total[:, :MODEL_WIDTH] + dot(logits_grad, router, NT)
        middle = middle_ref[...]
        norm_grad, gain_grad = norm_backward(
            middle, rms_inverse(middle), gain_ref[1:2], incoming
        )
        middle_grad = grad_ref[...].astype(f32) + norm_grad
        middle_grad_ref[...] = middle_grad
        branch_grad = (RESIDUAL_SCALE * middle_grad).astype(bf16)
        branch_grad_ref[...] = branch_grad
        mixture_grad_ref[...] = dot(branch_grad, weight_ref[...]).astype(bf16)
        gain_grad_ref[...] = jnp.broadcast_to(gain_grad, (8, MODEL_WIDTH))

    wide = MODEL_WIDTH + LANES
    return pl.pallas_call(
        kernel,
        grid=(1,),
        in_specs=[
            whole_block((tokens, wide)),
            whole_block((tokens, LANES)),
            whole_block((tokens, MODEL_WIDTH)),
            whole_block((tokens, MODEL_WIDTH)),
            whole_block((tokens, MODEL_WIDTH)),
            pl.BlockSpec(
                (MODEL_WIDTH, LANES),
                lambda *_: (0, 2 * PAIR_COLS // LANES),
                pipeline_mode=pl.Buffered(1),
            ),
            square_block(1),
            whole_block((8, MODEL_WIDTH)),
        ]
        + [whole_block((tokens, wide))] * parts,
        out_specs=[
            whole_block((tokens, LANES)),
            whole_block((tokens, MODEL_WIDTH)),
            whole_block((tokens, MODEL_WIDTH)),
            whole_block((tokens, QUERY_COLS)),
            whole_block((8, MODEL_WIDTH)),
        ],
        out_shape=[
            jax.ShapeDtypeStruct((tokens, LANES), bf16),
            jax.ShapeDtypeStruct((tokens, MODEL_WIDTH), f32),
            jax.ShapeDtypeStruct((tokens, MODEL_WIDTH), bf16),
            jax.ShapeDtypeStruct((tokens, QUERY_COLS), bf16),
            jax.ShapeDtypeStruct((8, MODEL_WIDTH), f32),
        ],
        compiler_params=params(),
        cost_estimate=cost(
            2 * tokens * MODEL_WIDTH * QUERY_COLS, 2 * MODEL_WIDTH * (QUERY_COLS + 12 * tokens)
        ),
        name="return_to_attention",
    )(back, code, normed_two, middle, out_grad, w_small, w_square, gains, *back_parts)


def store_rows(product, columns, place, core, kept_ref, sent_ref):
    heads, far, rows = kept_ref.shape[:3]
    for mine in range(2):

        @pl.when(core == mine)
        def _():
            for head in range(heads):
                for group in range(2 * far):
                    first = (head * 2 * far + group) * rows
                    piece = product[first : first + rows]
                    target = kept_ref if group % 2 == mine else sent_ref
                    target[head, (group // 2) ^ place, :, columns] = piece


def weight_terms(lefts, rights):
    tokens = lefts[0].shape[0]
    tile = 384
    operands, in_specs, runs = [], [], []
    first = 0
    for left, parts in zip(lefts, rights):
        left_at = len(operands)
        operands.append(left)
        in_specs.append(whole_block((tokens, MODEL_WIDTH)))
        for right in parts:
            steps = right.shape[1] // tile
            runs.append((first, steps, left_at, len(operands)))
            operands.append(right)
            in_specs.append(
                pl.BlockSpec(
                    (tokens, tile),
                    functools.partial(
                        lambda i, first, steps: (0, jnp.clip(i - first, 0, steps - 1)),
                        first=first,
                        steps=steps,
                    ),
                )
            )
            first = first + steps
    width = first * tile

    def kernel(*refs):
        step = pl.program_id(0)
        for start, steps, left_at, right_at in runs:

            @pl.when((step >= start) & (step < start + steps))
            def _():
                refs[-1][...] = dot(refs[left_at][...], refs[right_at][...], TN).astype(bf16)

    return pl.pallas_call(
        kernel,
        grid=(first,),
        in_specs=in_specs,
        out_specs=pl.BlockSpec((MODEL_WIDTH, tile), lambda i: (0, i)),
        out_shape=jax.ShapeDtypeStruct((MODEL_WIDTH, width), bf16),
        compiler_params=params(),
        cost_estimate=cost(
            2 * tokens * MODEL_WIDTH * width,
            2 * width * (MODEL_WIDTH + tokens),
        ),
        name="weight_terms",
    )(*operands)


def leave(
    place,
    heads,
    groups,
    terms,
    query_grads,
    cosine,
    sine,
    hidden_in,
    normed,
    middle_grad,
    normed_two,
    logits_grad,
    gain_grad_two,
    w_small,
    w_query,
    gains,
):
    tokens = hidden_in.shape[0]
    parts = len(terms)
    count = len(terms[0])
    part_cols = PAIR_COLS // parts
    query_cols = QUERY_COLS // parts
    small_cols = w_small.shape[1]
    part_shape = (heads, groups // 2, MODEL_WIDTH // (heads * groups), small_cols)

    def kernel(
        place_ref,
        cosine_ref,
        sine_ref,
        hidden_ref,
        normed_ref,
        middle_grad_ref,
        normed_two_ref,
        logits_grad_ref,
        gain_two_ref,
        small_ref,
        query_weight_ref,
        gain_ref,
        *refs,
    ):
        query_grad_refs, term_refs = refs[:parts], refs[parts:-3]
        input_grad_ref, kept_ref, sent_ref = refs[-3:]

        def store(product, columns):
            store_rows(
                product.astype(bf16), columns, place_ref[0], place_ref[1], kept_ref, sent_ref
            )

        keys, lists = [], []
        for part in range(parts):
            total = term_refs[part * count][...]
            for ref in term_refs[part * count + 1 : (part + 1) * count]:
                total = total + ref[...].astype(f32)
            keys.append(turn(total[0], cosine_ref[...], sine_ref[...], -1.0).astype(bf16))
            lists.append(total[1].astype(bf16))
        keys = jnp.concatenate(keys, axis=1)
        lists = jnp.concatenate(lists, axis=1)
        incoming = dot(keys, small_ref[:, :PAIR_COLS], NT) + dot(
            lists, small_ref[:, PAIR_COLS : 2 * PAIR_COLS], NT
        )
        for part in range(parts):
            columns = slice(part * query_cols, (part + 1) * query_cols)
            incoming = incoming + dot(
                query_grad_refs[part][...], query_weight_ref[:, columns], NT
            )
        values = hidden_ref[...].astype(f32)
        norm_grad, gain_grad = norm_backward(
            values, rms_inverse(values), gain_ref[:1], incoming
        )
        input_grad_ref[...] = middle_grad_ref[...] + norm_grad
        normed = normed_ref[...]
        store(dot(normed, keys, TN), slice(0, PAIR_COLS))
        store(dot(normed, lists, TN), slice(PAIR_COLS, 2 * PAIR_COLS))
        two = gain_two_ref[:1]
        first_high = gain_grad.astype(bf16).astype(f32)
        second_high = two.astype(bf16).astype(f32)
        rows = jnp.concatenate(
            [
                jnp.zeros((EXPERTS, MODEL_WIDTH), f32),
                first_high,
                second_high,
                gain_grad - first_high,
                two - second_high,
                jnp.zeros((LANES - EXPERTS - 4, MODEL_WIDTH), f32),
            ],
            axis=0,
        )
        extras = dot(normed_two_ref[...], logits_grad_ref[...], TN) + jnp.transpose(rows)
        store(extras, slice(2 * PAIR_COLS, small_cols))

    return pl.pallas_call(
        kernel,
        grid=(1,),
        in_specs=[
            pl.BlockSpec(memory_space=pltpu.SMEM),
            whole_block((tokens, LANES)),
            whole_block((tokens, LANES)),
            whole_block((tokens, MODEL_WIDTH)),
            whole_block((tokens, MODEL_WIDTH)),
            whole_block((tokens, MODEL_WIDTH)),
            whole_block((tokens, MODEL_WIDTH)),
            whole_block((tokens, LANES)),
            whole_block((8, MODEL_WIDTH)),
            whole_block((MODEL_WIDTH, small_cols)),
            square_block(0),
            whole_block((8, MODEL_WIDTH)),
        ]
        + [whole_block((tokens, query_cols))] * parts
        + [whole_block((2, tokens, part_cols))] * (parts * count),
        out_specs=[
            whole_block((tokens, MODEL_WIDTH)),
            whole_block(part_shape),
            whole_block(part_shape),
        ],
        out_shape=[
            jax.ShapeDtypeStruct((tokens, MODEL_WIDTH), f32),
            jax.ShapeDtypeStruct(part_shape, bf16),
            jax.ShapeDtypeStruct(part_shape, bf16),
        ],
        compiler_params=params(),
        cost_estimate=cost(
            2 * tokens * MODEL_WIDTH * (QUERY_COLS + 4 * PAIR_COLS),
            2 * MODEL_WIDTH * (QUERY_COLS + 2 * small_cols + 8 * tokens),
        ),
        name="leave",
    )(
        place,
        cosine,
        sine,
        hidden_in,
        normed,
        middle_grad,
        normed_two,
        logits_grad,
        gain_grad_two,
        w_small,
        w_query,
        gains,
        *query_grads,
        *[array for part in terms for array in part],
    )


def stacked_heads(block, pair):
    first = pair * GROUP * HEAD_WIDTH
    return jnp.concatenate(
        [
            block[:, first + j * HEAD_WIDTH : first + (j + 1) * HEAD_WIDTH]
            for j in range(GROUP)
        ],
        axis=0,
    )


def masked_scores(keys, queries, starts, offset, causal):
    tokens = keys.shape[0]
    scores = dot(keys, queries, NT)
    key_place = lax.broadcasted_iota(jnp.int32, (tokens, tokens), 0)
    visible = key_place + offset >= starts
    if causal:
        visible = visible & (key_place <= lax.broadcasted_iota(jnp.int32, (tokens, tokens), 1))
    parts = [
        jnp.where(visible, scores[:, j * tokens : (j + 1) * tokens], MASKED) for j in range(GROUP)
    ]
    return jnp.concatenate(parts, axis=1)


def kv_spec(tokens):
    return pl.BlockSpec((2, tokens, LANES), lambda i: (0, 0, i))


def attend(queries, key_values, starts, name):
    tokens = queries.shape[0]
    blocks = len(key_values)
    pairs = KEY_VALUE_HEADS // PAIRED
    width = PAIRED * GROUP * HEAD_WIDTH

    def kernel(starts_ref, query_ref, *refs):
        kv_refs, (out_ref, lse_ref) = refs[:blocks], refs[blocks:]
        starts_row = starts_ref[...]
        turned = []
        lse_rows = []
        for pair in range(PAIRED):
            lanes = slice(pair * HEAD_WIDTH, (pair + 1) * HEAD_WIDTH)
            stacked = stacked_heads(query_ref[...], pair) * jnp.asarray(ATTN_SCALE, bf16)
            scores = [
                masked_scores(
                    kv_refs[b][0, :, lanes],
                    stacked,
                    starts_row,
                    (b - blocks + 1) * tokens,
                    b == blocks - 1,
                )
                for b in range(blocks)
            ]
            top = functools.reduce(
                jnp.maximum, [jnp.max(s, axis=0, keepdims=True) for s in scores]
            )
            total = jnp.zeros_like(top)
            mixed = jnp.zeros((HEAD_WIDTH, GROUP * tokens), f32)
            for b in range(blocks):
                weights = jnp.exp(scores[b] - top)
                total = total + jnp.sum(weights, axis=0, keepdims=True)
                mixed = mixed + dot(kv_refs[b][1, :, lanes], weights.astype(bf16), TN)
            mixed = mixed / total
            lse = top + jnp.log(total)
            for j in range(GROUP):
                columns = slice(j * tokens, (j + 1) * tokens)
                turned.append(mixed[:, columns])
                lse_rows.append(lse[:, columns])
        out_ref[...] = jnp.transpose(jnp.concatenate(turned, axis=0)).astype(bf16)
        lse_rows = lse_rows + [jnp.zeros((1, tokens), f32)] * (8 - len(lse_rows))
        lse_ref[0] = jnp.concatenate(lse_rows, axis=0)

    scores_count = QUERY_HEADS * tokens * tokens * blocks
    return pl.pallas_call(
        kernel,
        grid=(pairs,),
        in_specs=[
            whole_block((1, tokens)),
            pl.BlockSpec((tokens, width), lambda i: (0, i)),
        ]
        + [kv_spec(tokens)] * blocks,
        out_specs=[
            pl.BlockSpec((tokens, width), lambda i: (0, i)),
            pl.BlockSpec((1, 8, tokens), lambda i: (i, 0, 0)),
        ],
        out_shape=[
            jax.ShapeDtypeStruct((tokens, QUERY_COLS), bf16),
            jax.ShapeDtypeStruct((pairs, 8, tokens), f32),
        ],
        compiler_params=pltpu.CompilerParams(vmem_limit_bytes=VMEM_BYTES),
        cost_estimate=pl.CostEstimate(
            flops=4 * scores_count * HEAD_WIDTH,
            bytes_accessed=4 * tokens * (QUERY_COLS + blocks * PAIR_COLS),
            transcendentals=scores_count,
        ),
        name=name,
    )(starts, queries, *key_values)


def attend_backward(
    queries, key_values, starts, mixture_grad, lse, cosine, sine, part, parts, name
):
    tokens = queries.shape[0]
    blocks = len(key_values)
    pairs = KEY_VALUE_HEADS // PAIRED // parts
    first = part * pairs
    width = PAIRED * GROUP * HEAD_WIDTH

    def kernel(starts_ref, query_ref, grad_ref, lse_ref, cosine_ref, sine_ref, *refs):
        kv_refs = refs[:blocks]
        dq_ref = refs[blocks]
        dkv_refs = refs[blocks + 1 : 2 * blocks + 1]
        probs_ref, prob_grad_ref = refs[2 * blocks + 1 :]
        starts_row = starts_ref[...]
        turned = []
        for pair in range(PAIRED):
            lanes = slice(pair * HEAD_WIDTH, (pair + 1) * HEAD_WIDTH)
            stacked = stacked_heads(query_ref[...], pair) * jnp.asarray(ATTN_SCALE, bf16)
            incoming = stacked_heads(grad_ref[...], pair)
            lse_row = jnp.concatenate(
                [lse_ref[0, pair * GROUP + j : pair * GROUP + j + 1, :] for j in range(GROUP)],
                axis=1,
            )
            delta = jnp.zeros((1, GROUP * tokens), f32)
            for b in range(blocks):
                scores = masked_scores(
                    kv_refs[b][0, :, lanes],
                    stacked,
                    starts_row,
                    (b - blocks + 1) * tokens,
                    b == blocks - 1,
                )
                probs = jnp.exp(scores - lse_row)
                prob_grad = dot(kv_refs[b][1, :, lanes], incoming, NT)
                delta = delta + jnp.sum(probs * prob_grad, axis=0, keepdims=True)
                probs_ref[b] = probs
                prob_grad_ref[b] = prob_grad
            query_grad = jnp.zeros((HEAD_WIDTH, GROUP * tokens), f32)
            for b in range(blocks):
                probs = probs_ref[b]
                score_grad = (probs * (prob_grad_ref[b] - delta)).astype(bf16)
                query_grad = query_grad + dot(kv_refs[b][0, :, lanes], score_grad, TN)
                key_part = dot(score_grad, stacked)
                value_part = dot(probs.astype(bf16), incoming)
                dkv_refs[b][0, :, lanes] = key_part.astype(dkv_refs[b].dtype)
                dkv_refs[b][1, :, lanes] = value_part.astype(dkv_refs[b].dtype)
            query_grad = query_grad * ATTN_SCALE
            for j in range(GROUP):
                turned.append(query_grad[:, j * tokens : (j + 1) * tokens])
        query_grad = jnp.transpose(jnp.concatenate(turned, axis=0))
        dq_ref[...] = turn(query_grad, cosine_ref[...], sine_ref[...], -1.0).astype(bf16)

    scores_count = QUERY_HEADS // parts * tokens * tokens * blocks
    return pl.pallas_call(
        kernel,
        grid=(pairs,),
        in_specs=[
            whole_block((1, tokens)),
            pl.BlockSpec((tokens, width), lambda i: (0, first + i)),
            pl.BlockSpec((tokens, width), lambda i: (0, first + i)),
            pl.BlockSpec((1, 8, tokens), lambda i: (first + i, 0, 0)),
            whole_block((tokens, LANES)),
            whole_block((tokens, LANES)),
        ]
        + [pl.BlockSpec((2, tokens, LANES), lambda i: (0, 0, first + i))] * blocks,
        out_specs=[pl.BlockSpec((tokens, width), lambda i: (0, i))] + [kv_spec(tokens)] * blocks,
        out_shape=[jax.ShapeDtypeStruct((tokens, QUERY_COLS // parts), bf16)]
        + [jax.ShapeDtypeStruct((2, tokens, PAIR_COLS // parts), bf16)] * (blocks - 1)
        + [jax.ShapeDtypeStruct((2, tokens, PAIR_COLS // parts), f32)],
        scratch_shapes=[pltpu.VMEM((blocks, tokens, GROUP * tokens), f32)] * 2,
        compiler_params=pltpu.CompilerParams(vmem_limit_bytes=VMEM_BYTES),
        cost_estimate=pl.CostEstimate(
            flops=10 * scores_count * HEAD_WIDTH,
            bytes_accessed=4 * tokens * (2 * QUERY_COLS + 2 * blocks * PAIR_COLS),
            transcendentals=scores_count,
        ),
        name=name,
    )(starts, queries, mixture_grad, lse, cosine, sine, *key_values)


def expert_block(index):
    return pl.BlockSpec((MODEL_WIDTH, FF), lambda *_: (0, index), pipeline_mode=pl.Buffered(1))


def experts(order, inputs, grads, scaled, w_small, w_expert, expert, tokens):
    rows = inputs.shape[0]
    wide = MODEL_WIDTH + LANES
    fresh = scaled is None

    def kernel(
        order_ref, expert_ref, input_ref, grad_ref, router_ref, gate_ref, up_ref, down_ref, *refs
    ):
        scaled_ref, hidden_grad_ref, input_grad_ref = refs if fresh else refs[1:]
        block = input_ref[...]
        code = grad_ref[:, MODEL_WIDTH:].astype(f32)
        lane = lax.broadcasted_iota(jnp.int32, (tokens, LANES), 1)
        logits = jnp.where(code > 0.5, dot(block, router_ref[...]), MASKED)
        raised = jnp.exp(logits - jnp.max(logits, axis=1, keepdims=True))
        raised = jnp.where(code > 0.5, raised, 0.0)
        gates = raised / jnp.sum(raised, axis=1, keepdims=True)
        kept = (lane == expert_ref[0]) & (code > 0.5) & (code < 1.5)
        gate = jnp.sum(jnp.where(kept, gates, 0.0), axis=1, keepdims=True)
        gate_part = dot(block, gate_ref[...])
        up_part = dot(block, up_ref[...])
        sigmoid = 1.0 / (1.0 + jnp.exp(-gate_part))
        silu = gate_part * sigmoid
        activation = silu * up_part
        scaled_ref[...] = (activation * gate).astype(bf16)
        pulled = dot(grad_ref[:, :MODEL_WIDTH], down_ref[...])
        gate_grad = RESIDUAL_SCALE * jnp.sum(activation * pulled, axis=1, keepdims=True)
        high = gate_grad.astype(bf16).astype(f32)
        columns = jnp.where(
            lane == expert_ref[0],
            high,
            jnp.where(lane == expert_ref[0] + EXPERTS, gate_grad - high, 0.0),
        )
        input_grad_ref[:, MODEL_WIDTH:] = columns.astype(bf16)
        activation_grad = pulled * (RESIDUAL_SCALE * gate)
        slope = sigmoid * (1.0 + gate_part * (1.0 - sigmoid))
        gate_part_grad = (activation_grad * up_part * slope).astype(bf16)
        up_part_grad = (activation_grad * silu).astype(bf16)
        hidden_grad_ref[:, :FF] = gate_part_grad
        hidden_grad_ref[:, FF:] = up_part_grad
        input_grad_ref[:, :MODEL_WIDTH] = (
            dot(gate_part_grad, gate_ref[...], NT) + dot(up_part_grad, up_ref[...], NT)
        ).astype(bf16)

    in_specs = [
        pl.BlockSpec(memory_space=pltpu.SMEM),
        pl.BlockSpec((tokens, MODEL_WIDTH), lambda i, order_ref: (i, 0)),
        pl.BlockSpec((tokens, wide), lambda i, order_ref: (order_ref[i], 0)),
        pl.BlockSpec(
            (MODEL_WIDTH, LANES),
            lambda *_: (0, 2 * PAIR_COLS // LANES),
            pipeline_mode=pl.Buffered(1),
        ),
        expert_block(0),
        expert_block(1),
        expert_block(2),
    ]
    operands = [order, expert, inputs, grads, w_small, w_expert, w_expert, w_expert]
    if not fresh:
        in_specs.append(pl.BlockSpec(memory_space=pl.ANY))
        operands.append(scaled)
    return pl.pallas_call(
        kernel,
        grid_spec=pltpu.PrefetchScalarGridSpec(
            num_scalar_prefetch=1,
            grid=(rows // tokens,),
            in_specs=in_specs,
            out_specs=[
                pl.BlockSpec((tokens, FF), lambda i, order_ref: (order_ref[i], 0)),
                pl.BlockSpec((tokens, 2 * FF), lambda i, order_ref: (i, 0)),
                pl.BlockSpec((tokens, wide), lambda i, order_ref: (i, 0)),
            ],
        ),
        out_shape=[
            jax.ShapeDtypeStruct((grads.shape[0], FF), bf16),
            jax.ShapeDtypeStruct((rows, 2 * FF), bf16),
            jax.ShapeDtypeStruct((rows, wide), bf16),
        ],
        input_output_aliases={} if fresh else {8: 0},
        compiler_params=params(),
        cost_estimate=cost(
            10 * rows * MODEL_WIDTH * FF,
            2 * MODEL_WIDTH * (3 * rows + EXPERT_COLS),
            rows * FF,
        ),
        name="experts",
    )(*operands)


def expert_shares(scaled, weights, tokens):
    rows = scaled.shape[0]

    def kernel(scaled_ref, weight_ref, out_ref):
        out_ref[...] = dot(scaled_ref[...], weight_ref[...], NT).astype(bf16)

    return pl.pallas_call(
        kernel,
        grid=(rows // (2 * tokens),),
        in_specs=[
            pl.BlockSpec((2 * tokens, FF), lambda i: (i, 0)),
            expert_block(2),
        ],
        out_specs=pl.BlockSpec((2 * tokens, MODEL_WIDTH), lambda i: (i, 0)),
        out_shape=jax.ShapeDtypeStruct((rows, MODEL_WIDTH), bf16),
        compiler_params=params(),
        cost_estimate=cost(
            2 * rows * MODEL_WIDTH * FF, 2 * MODEL_WIDTH * (rows + FF) + 2 * rows * FF,
        ),
        name="expert_shares",
    )(scaled, weights)


def expert_terms(pieces, scale, name):
    width = pieces[0][1].shape[1]
    tile = 384
    rows = sum(left.shape[0] for left, _ in pieces)

    def kernel(*refs):
        total = None
        for k in range(len(pieces)):
            term = dot(refs[2 * k][...], refs[2 * k + 1][...], TN)
            total = term if total is None else total + term
        refs[-1][...] = (scale * total).astype(bf16)

    in_specs = []
    for left, right in pieces:
        in_specs.append(pl.BlockSpec((left.shape[0], tile), lambda i: (0, i)))
        in_specs.append(whole_block(right.shape))
    return pl.pallas_call(
        kernel,
        grid=(MODEL_WIDTH // tile,),
        in_specs=in_specs,
        out_specs=pl.BlockSpec((tile, width), lambda i: (i, 0)),
        out_shape=jax.ShapeDtypeStruct((MODEL_WIDTH, width), bf16),
        compiler_params=params(),
        cost_estimate=cost(
            2 * rows * MODEL_WIDTH * width, 2 * (rows + width) * MODEL_WIDTH + 2 * rows * width
        ),
        name=name,
    )(*[array for piece in pieces for array in piece])


def shards(
    hidden_in,
    out_grad,
    doc_lengths,
    expert_ids,
    attention_norm,
    query_weight,
    key_matrix,
    value_matrix,
    output_weight,
    expert_norm,
    router_weight,
    expert_input,
    expert_output,
):
    tokens = hidden_in.shape[0]
    heads = lax.axis_size("head")
    groups = lax.axis_size("seq")
    own_rows = query_weight.shape[0]
    head_index = lax.axis_index("head")
    seq_index = lax.axis_index("seq")
    shared = EXPERTS // groups
    first_row = (seq_index * heads + head_index) * tokens
    expert = (seq_index * shared + head_index % shared).astype(jnp.int32)[None]

    places = first_row + jnp.arange(tokens)
    starts = doc_start(doc_lengths, places)
    cosine, sine = rope_tables(places - starts)
    starts_row = (starts - first_row).astype(jnp.int32)[None, :]

    hot = (expert_ids[:, :, None] == jnp.arange(EXPERTS)[None, None, :]).astype(f32)
    chosen = jnp.sum(hot, axis=1)
    before = (jnp.arange(tokens)[:, None] > jnp.arange(tokens)[None, :]).astype(bf16)
    earlier = dot(before, chosen.astype(bf16))
    code = jnp.where(chosen > 0.5, jnp.where(earlier < CAP - 0.5, 1.0, 2.0), 0.0)
    code = jnp.concatenate(
        [code.astype(bf16), jnp.zeros((tokens, LANES - EXPERTS), bf16)], axis=1
    )
    coded_grad = jnp.concatenate([out_grad, code], axis=1)

    def spread(block, axes):
        return lax.all_to_all(block, axes, split_axis=0, concat_axis=0, tiled=True)

    clock = Clock()
    small = jnp.concatenate(
        [
            key_matrix,
            value_matrix,
            router_weight,
            attention_norm[:, None],
            expert_norm[:, None],
            jnp.zeros((own_rows, LANES - EXPERTS - 2), bf16),
        ],
        axis=1,
    )
    w_small = lax.all_gather(small, ("head", "seq"), axis=0, tiled=True)

    mine = jnp.concatenate(
        [
            expert_input.reshape(own_rows, groups, shared, 2 * FF),
            expert_output.reshape(own_rows, groups, shared, FF),
        ],
        axis=3,
    )
    mine = jnp.tile(jnp.transpose(mine, (2, 1, 0, 3)), (heads // shared, 1, 1, 1))
    mine = mine.reshape(heads * groups, own_rows, EXPERT_COLS)
    mine_flow = Flow(one_move(mine, functools.partial(spread, axes=("head", "seq"))))
    pending = clock.begin(mine_flow)

    normed, own_kv, gains = enter(hidden_in, w_small, cosine, sine)
    clock.end(pending, own_kv)
    kv_flows = [
        Flow(one_move(own_kv, functools.partial(along_stream, distance=distance)))
        for distance in range(1, heads + 1)
    ]
    w_large = lax.all_gather(
        jnp.concatenate([query_weight, output_weight], axis=1),
        ("head", "seq"),
        axis=0,
        tiled=True,
    )
    far_grads = [Flow(one_move(coded_grad, by_head(step))) for step in range(1, shared)]
    clock.tick(*kv_flows)
    key_values = [flow.value for flow in kv_flows[::-1]] + [own_kv]
    w_expert = mine_flow.value.reshape(MODEL_WIDTH, EXPERT_COLS)
    queries = project_queries(normed, w_large, cosine, sine)
    mixture, lse = attend(queries, key_values, starts_row, "attend")
    middle, normed_two = leave_attention(mixture, w_large, hidden_in, gains)

    input_flows = [Flow(tokens_gather(normed_two))]
    far_tokens = [Flow(one_move(normed_two, by_head(step))) for step in range(1, shared)]
    clock.tick(input_flows[0], *far_tokens)

    input_flows = input_flows + [Flow(tokens_gather(flow.value)) for flow in far_tokens]
    clock.tick(input_flows[0], *far_grads)

    def seq_gather(block):
        return lax.all_gather(block, "seq", axis=0, tiled=True)

    grads = [seq_gather(after(coded_grad, *key_values))] + [
        seq_gather(flow.value) for flow in far_grads
    ]
    core_flows = [Flow(one_move(clock.finish(input_flows[0]), by_seq(1)))]
    clock.tick(core_flows[0], *input_flows[1:])

    back = []
    inputs = {}
    hidden_grads = {}
    scaled = [None] * shared
    turn_of = expert
    blocks = jnp.arange(groups // 2, dtype=jnp.int32) * 2
    for step in range(shared):
        terms = []
        for core in range(2):
            if core == 0:
                inputs[step, 0] = clock.finish(input_flows[step])
                pending = clock.begin(*input_flows[step + 1 :], *back)
            else:
                inputs[step, 1] = clock.finish(core_flows[step])
                if step + 1 < shared:
                    following = clock.finish(input_flows[step + 1])
                    core_flows.append(Flow(one_move(following, by_seq(1))))
                pending = clock.begin(*core_flows[step + 1 :], *back)
            order = (blocks + core) ^ seq_index
            scaled[step], hidden_grads[step, core], input_grad = experts(
                order.astype(jnp.int32),
                inputs[step, core],
                grads[step],
                scaled[step],
                w_small,
                w_expert,
                turn_of,
                tokens,
            )
            turn_of = after(expert, input_grad)
            terms.append(input_grad)
            clock.end(pending, turn_of)
        back.append(Flow(tokens_scatter(*terms)))

    work = [
        lambda first: expert_shares(after(scaled[0], first), w_expert, tokens),
        lambda first: expert_terms(
            [(inputs[key], after(hidden_grads[key], first)) for key in inputs], 1.0, "up_terms"
        ),
        lambda first: expert_terms(
            [(grad, after(part, first)) for grad, part in zip(grads, scaled)],
            RESIDUAL_SCALE,
            "down_terms",
        ),
    ] + [
        functools.partial(
            lambda first, part: expert_shares(after(part, first), w_expert, tokens), part=part
        )
        for part in scaled[1:]
    ]
    made = []
    while not all(flow.done for flow in back):
        pending = clock.begin(*back)
        held = ()
        if len(made) < len(work):
            made.append(work[len(made)](after(turn_of, *clock.last)))
            turn_of = after(expert, made[-1])
            held = (turn_of,)
        clock.end(pending, *held)
    back_parts = [
        Flow(one_move(back[step].value.astype(bf16), by_head(step))) for step in range(1, shared)
    ]
    pending = clock.begin(*back_parts)
    while len(made) < len(work):
        made.append(work[len(made)](after(turn_of, *clock.last)))
        turn_of = after(expert, made[-1])
    clock.end(pending, turn_of)
    up_part, down_part = made[1:3]
    shares = made[:1] + made[3:]
    shares = [lax.psum_scatter(part, "seq", scatter_dimension=0, tiled=True) for part in shares]
    expert_part = jnp.concatenate([up_part, down_part], axis=1)
    expert_part = expert_part.reshape(heads * groups, own_rows, EXPERT_COLS)
    expert_flow = Flow(
        one_move(expert_part, functools.partial(spread, axes=("head", "seq")))
    )
    pending = clock.begin(expert_flow)
    logits_grad, middle_grad, branch_grad, mixture_grad, gain_grad_two = return_to_attention(
        back[0].value,
        [flow.value for flow in back_parts],
        code,
        normed_two,
        middle,
        out_grad,
        w_small,
        w_large,
        gains,
    )

    place = jnp.stack([seq_index // 2, seq_index % 2]).astype(jnp.int32)
    query_grad, *kv_terms = attend_backward(
        queries,
        key_values,
        starts_row,
        mixture_grad,
        lse,
        cosine,
        sine,
        0,
        1,
        "attend_backward",
    )
    query_grads = [query_grad]
    large_part = weight_terms(
        [normed, after(branch_grad, query_grad)], [query_grads, [mixture]]
    )
    clock.end(pending, large_part)
    large_part = lax.psum_scatter(large_part, ("head", "seq"), scatter_dimension=0, tiled=True)
    kv_flows = [
        Flow(one_move(term, functools.partial(along_stream, distance=-distance)))
        for term, distance in zip(kv_terms[:-1], range(heads, 0, -1))
    ]
    clock.tick(*kv_flows)
    terms = [(kv_terms[-1], kv_flows)]
    input_grad, *small_parts = leave(
        place,
        heads,
        groups,
        [[own] + [flow.value for flow in flows] for own, flows in terms],
        query_grads,
        cosine,
        sine,
        after(hidden_in, *shares),
        normed,
        middle_grad,
        normed_two,
        logits_grad,
        gain_grad_two,
        w_small,
        w_large,
        gains,
    )

    small_flow = Flow(rows_scatter(*small_parts))
    share_flows = [
        Flow(one_move(shares[step], by_head(step))) for step in range(1, shared)
    ]
    clock.tick(small_flow)
    clock.tick(small_flow, *share_flows)
    small_flow = Flow(line_scatter(clock.finish(small_flow)))
    clock.finish(small_flow)
    moe_out = shares[0].astype(f32)
    for flow in share_flows:
        moe_out = moe_out + flow.value.astype(f32)
    block_out = (middle + RESIDUAL_SCALE * moe_out).astype(bf16)

    expert_sum = expert_flow.value.reshape(
        heads // shared, shared, groups, own_rows, EXPERT_COLS
    )
    expert_sum = jnp.sum(expert_sum.astype(f32), axis=0)

    def expert_output_of(first, last):
        columns = jnp.transpose(expert_sum[..., first:last], (2, 1, 0, 3))
        return columns.reshape(own_rows, EXPERTS, last - first)

    expert_input_grad = expert_output_of(0, 2 * FF)
    expert_output_grad = expert_output_of(2 * FF, EXPERT_COLS)
    large_sum = large_part.astype(f32)
    query_weight_grad = large_sum[:, :QUERY_COLS]
    output_grad = large_sum[:, QUERY_COLS:]
    small_sum = small_flow.value
    key_grad = small_sum[:, :PAIR_COLS]
    value_grad = small_sum[:, PAIR_COLS : 2 * PAIR_COLS]
    rest = small_sum[:, 2 * PAIR_COLS :]
    router_grad = rest[:, :EXPERTS]
    attention_norm_grad = rest[:, EXPERTS] + rest[:, EXPERTS + 2]
    expert_norm_grad = rest[:, EXPERTS + 1] + rest[:, EXPERTS + 3]
    return (
        block_out,
        input_grad,
        attention_norm_grad,
        query_weight_grad,
        key_grad,
        value_grad,
        output_grad,
        expert_norm_grad,
        router_grad,
        expert_input_grad,
        expert_output_grad,
    )


def solution(mesh):
    return jax.shard_map(
        shards,
        mesh=mesh,
        in_specs=(
            P(("seq", "head"), None),
            P(("seq", "head"), None),
            P(),
            P(("seq", "head"), None),
            P(("head", "seq")),
            P(("head", "seq"), None),
            P(("head", "seq"), None),
            P(("head", "seq"), None),
            P(("head", "seq"), None),
            P(("head", "seq")),
            P(("head", "seq"), None),
            P(("head", "seq"), None, None),
            P(("head", "seq"), None, None),
        ),
        out_specs=(
            P(("seq", "head"), None),
            P(("seq", "head"), None),
            P(("head", "seq")),
            P(("head", "seq"), None),
            P(("head", "seq"), None),
            P(("head", "seq"), None),
            P(("head", "seq"), None),
            P(("head", "seq")),
            P(("head", "seq"), None),
            P(("head", "seq"), None, None),
            P(("head", "seq"), None, None),
        ),
        check_vma=False,
    )
```

```python
import functools

import jax
import jax.numpy as jnp
from jax import lax
from jax.experimental import pallas as pl
from jax.experimental.pallas import tpu as pltpu
from jax.sharding import PartitionSpec as P

MODEL_WIDTH = 1536
QUERY_HEADS = 24
KEY_VALUE_HEADS = 8
HEAD_WIDTH = 64
FF = 512
EXPERTS = 16
CAP = 160

EPS = 1e-06
ATTN_SCALE = 1.0 / 64.0
RESIDUAL_SCALE = 0.22
MASKED = -1e30

GROUP = QUERY_HEADS // KEY_VALUE_HEADS
QUERY_COLS = QUERY_HEADS * HEAD_WIDTH
PAIR_COLS = KEY_VALUE_HEADS * HEAD_WIDTH
LANES = 128
HALF = HEAD_WIDTH // 2
PAIRED = LANES // HEAD_WIDTH
EXPERT_COLS = 3 * FF

bf16 = jnp.bfloat16
f32 = jnp.float32

NT = (((1,), (1,)), ((), ()))
TN = (((0,), (0,)), ((), ()))
VMEM_BYTES = 56 * 1024 * 1024


def dot(left, right, dims=(((1,), (0,)), ((), ()))):
    return lax.dot_general(left, right, dims, preferred_element_type=f32)


def swap(block, mask):
    count = lax.axis_size("seq")
    return lax.ppermute(block, "seq", [(i, i ^ mask) for i in range(count)])


def around(block, distance):
    count = lax.axis_size("head")
    return lax.ppermute(block, "head", [(i, (i + distance) % count) for i in range(count)])


def along_stream(block, distance):
    heads, groups = lax.axis_size("head"), lax.axis_size("seq")
    route = []
    for group in range(groups):
        for head in range(heads):
            target = group * heads + head + distance
            if 0 <= target < heads * groups:
                route.append((head * groups + group, (target % heads) * groups + target // heads))
    return lax.ppermute(block, ("head", "seq"), route)


def side(mask):
    return (lax.axis_index("seq") // mask) % 2


def far_masks():
    masks, mask = [], 2
    while mask < lax.axis_size("seq"):
        masks.append(mask)
        mask = mask * 2
    return masks


def join(own, other, bit, axis):
    return jnp.where(
        bit == 0, jnp.stack([own, other], axis=axis), jnp.stack([other, own], axis=axis)
    )


def swap_head(block, mask):
    count = lax.axis_size("head")
    return lax.ppermute(block, "head", [(i, i ^ mask) for i in range(count)])


def head_side(mask):
    return (lax.axis_index("head") // mask) % 2


def after(value, *others):
    return lax.optimization_barrier((value,) + others)[0]


class Flow:
    def __init__(self, steps):
        self.steps = steps
        self.value = None
        self.moves = []
        self.done = False
        self.feed(None)

    def feed(self, results):
        try:
            self.moves = self.steps.send(results)
        except StopIteration as stop:
            self.value, self.moves, self.done = stop.value, [], True


class Clock:
    def __init__(self):
        self.last = ()

    def begin(self, *flows, ready=()):
        flows = [flow for flow in flows if not flow.done]
        blocks = tuple(block for flow in flows for block, _ in flow.moves)
        if not blocks:
            return [], []
        tied = lax.optimization_barrier(blocks + tuple(self.last) + tuple(ready))
        movers = [move for flow in flows for _, move in flow.moves]
        return flows, [move(block) for move, block in zip(movers, tied)]

    def end(self, pending, *held):
        flows, results = pending
        if not results:
            return
        if held:
            results = list(lax.optimization_barrier(tuple(results) + held)[: len(results)])
        self.last = tuple(results)
        for flow in flows:
            count = len(flow.moves)
            flow.feed(results[:count])
            results = results[count:]

    def tick(self, *flows, ready=()):
        self.end(self.begin(*flows, ready=ready))

    def finish(self, *flows):
        while not all(flow.done for flow in flows):
            self.tick(*flows)
        return flows[0].value if len(flows) == 1 else [flow.value for flow in flows]


def by_seq(mask):
    return lambda block: swap(block, mask)


def by_head(mask):
    return lambda block: swap_head(block, mask)


def one_move(block, move):
    (result,) = yield [(block, move)]
    return result


def line_gather(block):
    heads = lax.axis_size("head")
    here = lax.axis_index("head")
    whole = jnp.zeros((heads,) + block.shape, block.dtype)
    whole = lax.dynamic_update_index_in_dim(whole, block, here, 0)
    results = yield [
        (block, functools.partial(around, distance=distance)) for distance in range(1, heads)
    ]
    for distance, result in enumerate(results, 1):
        whole = lax.dynamic_update_index_in_dim(whole, result, (here - distance) % heads, 0)
    return whole


def rows_gather(block):
    lines = yield from line_gather(block)
    masks = far_masks()
    middle = lines.shape[0] // 2
    parts = [(lines[:middle], masks), (lines[middle:], masks[::-1])]
    for step in range(len(masks)):
        results = yield [(part, by_seq(order[step])) for part, order in parts]
        parts = [
            (
                join(
                    part,
                    result,
                    side(order[step]),
                    1 + sum(1 for other in order[:step] if other > order[step]),
                ),
                order,
            )
            for (part, order), result in zip(parts, results)
        ]
    whole = jnp.concatenate([part for part, _ in parts], axis=0)
    (result,) = yield [(whole, by_seq(1))]
    whole = join(whole, result, side(1), 1 + len(masks))
    return whole.reshape(MODEL_WIDTH, block.shape[1])


def rows_scatter(kept, sent):
    masks = far_masks()
    (result,) = yield [(sent, by_seq(1))]
    whole = (kept.astype(f32) + result.astype(f32)).astype(bf16)
    whole = whole.reshape(whole.shape[:1] + (2,) * len(masks) + whole.shape[2:])
    middle = whole.shape[0] // 2
    parts = [(whole[:middle], masks), (whole[middle:], masks[::-1])]
    for step in range(len(masks)):
        axes = [
            1 + sum(1 for other in order[step + 1 :] if other > order[step])
            for _, order in parts
        ]
        results = yield [
            (lax.index_in_dim(part, 1, axis, False), by_seq(order[step]))
            for (part, order), axis in zip(parts, axes)
        ]
        parts = [
            (
                (
                    lax.index_in_dim(part, 0, axis, False).astype(f32) + result.astype(f32)
                ).astype(bf16),
                order,
            )
            for (part, order), axis, result in zip(parts, axes, results)
        ]
    return jnp.concatenate([part for part, _ in parts], axis=0)


def line_scatter(terms):
    heads = lax.axis_size("head")
    here = lax.axis_index("head")
    results = yield [
        (
            lax.dynamic_index_in_dim(terms, (here + distance) % heads, 0, False),
            functools.partial(around, distance=distance),
        )
        for distance in range(1, heads)
    ]
    total = lax.dynamic_index_in_dim(terms, here, 0, False).astype(f32)
    for result in results:
        total = total + result.astype(f32)
    return total


def tokens_gather(block):
    masks = far_masks()
    middle = block.shape[0] // 2
    parts = [(block[:middle], masks), (block[middle:], masks[::-1])]
    for step in range(len(masks)):
        results = yield [(part, by_seq(order[step])) for part, order in parts]
        parts = [
            (
                jnp.stack(
                    [part, result],
                    axis=sum(1 for other in order[:step] if other > order[step]),
                ),
                order,
            )
            for (part, order), result in zip(parts, results)
        ]
    whole = jnp.concatenate([part for part, _ in parts], axis=len(masks))
    return whole.reshape((lax.axis_size("seq") // 2 * block.shape[0],) + block.shape[1:])


def tokens_scatter(own, other):
    masks = far_masks()
    blocks = lax.axis_size("seq") // 2
    (result,) = yield [(other, by_seq(1))]
    whole = (own.astype(f32) + result.astype(f32)).astype(bf16)
    whole = whole.reshape((2,) * len(masks) + (own.shape[0] // blocks, own.shape[1]))
    middle = whole.shape[-2] // 2
    parts = [(whole[..., :middle, :], masks), (whole[..., middle:, :], masks[::-1])]
    for step in range(len(masks)):
        axes = [sum(1 for other in order[step + 1 :] if other > order[step]) for _, order in parts]
        results = yield [
            (lax.index_in_dim(part, 1, axis, False), by_seq(order[step]))
            for (part, order), axis in zip(parts, axes)
        ]
        last = step == len(masks) - 1
        parts = [
            (
                (
                    lax.index_in_dim(part, 0, axis, False).astype(f32) + result.astype(f32)
                ).astype(f32 if last else bf16),
                order,
            )
            for (part, order), axis, result in zip(parts, axes, results)
        ]
    return jnp.concatenate([part for part, _ in parts], axis=0)


def doc_start(doc_lengths, places):
    starts = jnp.cumsum(doc_lengths) - doc_lengths
    earlier = starts[None, :] <= places[:, None]
    return jnp.max(jnp.where(earlier, starts[None, :], 0), axis=1)


def rope_tables(places):
    frequency = jnp.exp(
        -jnp.log(10000.0) * 2.0 * jnp.arange(HALF).astype(f32) / HEAD_WIDTH
    )
    angles = places.astype(f32)[:, None] * frequency[None, :]
    cosine, sine = jnp.cos(angles), jnp.sin(angles)
    return (
        jnp.concatenate([cosine] * (LANES // HALF), axis=1),
        jnp.concatenate([-sine, sine] * PAIRED, axis=1),
    )


def turn(values, cosine, sine, sign):
    lane = lax.broadcasted_iota(jnp.int32, (values.shape[0], LANES), 1) % HEAD_WIDTH
    pieces = []
    for first in range(0, values.shape[1], LANES):
        piece = values[:, first : first + LANES]
        swapped = jnp.where(
            lane < HALF, pltpu.roll(piece, LANES - HALF, 1), pltpu.roll(piece, HALF, 1)
        )
        pieces.append(piece * cosine + (sign * swapped) * sine)
    return jnp.concatenate(pieces, axis=1)


def whole_block(shape):
    return pl.BlockSpec(shape, lambda *_: (0,) * len(shape), pipeline_mode=pl.Buffered(1))


def params():
    return pltpu.CompilerParams(vmem_limit_bytes=VMEM_BYTES)


def cost(flops, moved, transcendentals=0, weight=1):
    return pl.CostEstimate(
        flops=weight * flops,
        bytes_accessed=weight * moved,
        transcendentals=weight * transcendentals,
    )


def rms_inverse(values):
    return lax.rsqrt(jnp.mean(values * values, axis=1, keepdims=True) + EPS)


def norm_backward(values, inverse, gain, incoming):
    scaled = incoming * gain
    mean_term = jnp.mean(scaled * values, axis=1, keepdims=True)
    values_grad = inverse * scaled - values * (inverse * inverse * inverse * mean_term)
    gain_grad = jnp.sum(incoming * values * inverse, axis=0, keepdims=True)
    return (values_grad, gain_grad)


def enter(hidden_in, w_small, cosine, sine):
    tokens = hidden_in.shape[0]
    small_cols = w_small.shape[1]

    def kernel(hidden_ref, weight_ref, cosine_ref, sine_ref, normed_ref, kv_ref, gain_ref):
        extras = jnp.transpose(weight_ref[:, 2 * PAIR_COLS :].astype(f32))
        gains = extras[EXPERTS : EXPERTS + 8]
        gain_ref[...] = gains
        values = hidden_ref[...].astype(f32)
        normed = (values * rms_inverse(values) * gains[:1]).astype(bf16)
        normed_ref[...] = normed
        keys = dot(normed, weight_ref[:, :PAIR_COLS])
        kv_ref[0] = turn(keys, cosine_ref[...], sine_ref[...], 1.0).astype(bf16)
        kv_ref[1] = dot(normed, weight_ref[:, PAIR_COLS : 2 * PAIR_COLS]).astype(bf16)

    return pl.pallas_call(
        kernel,
        out_shape=[
            jax.ShapeDtypeStruct((tokens, MODEL_WIDTH), bf16),
            jax.ShapeDtypeStruct((2, tokens, PAIR_COLS), bf16),
            jax.ShapeDtypeStruct((8, MODEL_WIDTH), f32),
        ],
        compiler_params=params(),
        cost_estimate=cost(
            4 * tokens * MODEL_WIDTH * PAIR_COLS, 2 * MODEL_WIDTH * (small_cols + 2 * tokens)
        ),
        name="enter",
    )(hidden_in, w_small, cosine, sine)


def project_queries(normed, w_square, cosine, sine):
    tokens = normed.shape[0]
    width = 512

    def kernel(normed_ref, weight_ref, cosine_ref, sine_ref, out_ref):
        product = dot(normed_ref[...], weight_ref[...])
        out_ref[...] = turn(product, cosine_ref[...], sine_ref[...], 1.0).astype(bf16)

    return pl.pallas_call(
        kernel,
        grid=(QUERY_COLS // width,),
        in_specs=[
            whole_block((tokens, MODEL_WIDTH)),
            pl.BlockSpec((MODEL_WIDTH, width), lambda i: (0, i)),
            whole_block((tokens, LANES)),
            whole_block((tokens, LANES)),
        ],
        out_specs=pl.BlockSpec((tokens, width), lambda i: (0, i)),
        out_shape=jax.ShapeDtypeStruct((tokens, QUERY_COLS), bf16),
        compiler_params=params(),
        cost_estimate=cost(
            2 * tokens * MODEL_WIDTH * QUERY_COLS, 2 * MODEL_WIDTH * (QUERY_COLS + 2 * tokens)
        ),
        name="project_queries",
    )(normed, w_square, cosine, sine)


def square_block(index):
    return pl.BlockSpec(
        (MODEL_WIDTH, MODEL_WIDTH), lambda *_: (0, index), pipeline_mode=pl.Buffered(1)
    )


def leave_attention(mixture, w_square, hidden_in, gains):
    tokens = mixture.shape[0]

    def kernel(mixture_ref, weight_ref, hidden_ref, gain_ref, middle_ref, normed_ref):
        branch = dot(mixture_ref[...], weight_ref[...], NT)
        middle = hidden_ref[...].astype(f32) + RESIDUAL_SCALE * branch
        middle_ref[...] = middle
        normed_ref[...] = (middle * rms_inverse(middle) * gain_ref[1:2]).astype(bf16)

    return pl.pallas_call(
        kernel,
        grid=(1,),
        in_specs=[
            whole_block((tokens, QUERY_COLS)),
            square_block(1),
            whole_block((tokens, MODEL_WIDTH)),
            whole_block((8, MODEL_WIDTH)),
        ],
        out_specs=[whole_block((tokens, MODEL_WIDTH))] * 2,
        out_shape=[
            jax.ShapeDtypeStruct((tokens, MODEL_WIDTH), f32),
            jax.ShapeDtypeStruct((tokens, MODEL_WIDTH), bf16),
        ],
        compiler_params=params(),
        cost_estimate=cost(
            2 * tokens * MODEL_WIDTH * QUERY_COLS, 2 * MODEL_WIDTH * (QUERY_COLS + 5 * tokens)
        ),
        name="leave_attention",
    )(mixture, w_square, hidden_in, gains)


def return_to_attention(back, back_parts, code, normed_two, middle, out_grad, w_small, w_square, gains):
    tokens = middle.shape[0]
    parts = len(back_parts)

    def kernel(
        back_ref,
        code_ref,
        normed_ref,
        middle_ref,
        grad_ref,
        router_ref,
        weight_ref,
        gain_ref,
        *refs,
    ):
        logits_grad_ref, middle_grad_ref, branch_grad_ref, mixture_grad_ref, gain_grad_ref = refs[
            parts:
        ]
        total = back_ref[...]
        for ref in refs[:parts]:
            total = total + ref[...].astype(f32)
        code = code_ref[...].astype(f32)
        lane = lax.broadcasted_iota(jnp.int32, (tokens, LANES), 1)
        router = jnp.where(
            lax.broadcasted_iota(jnp.int32, (MODEL_WIDTH, LANES), 1) < EXPERTS,
            router_ref[...],
            jnp.asarray(0.0, bf16),
        )
        logits = jnp.where(code > 0.5, dot(normed_ref[...], router), MASKED)
        raised = jnp.exp(logits - jnp.max(logits, axis=1, keepdims=True))
        raised = jnp.where(code > 0.5, raised, 0.0)
        gates = raised / jnp.sum(raised, axis=1, keepdims=True)
        extra = total[:, MODEL_WIDTH:]
        gate_grad = extra + pltpu.roll(extra, LANES - EXPERTS, 1)
        gate_grad = jnp.where((lane < EXPERTS) & (code > 0.5) & (code < 1.5), gate_grad, 0.0)
        inner = jnp.sum(gates * gate_grad, axis=1, keepdims=True)
        logits_grad = (gates * (gate_grad - inner)).astype(bf16)
        logits_grad_ref[...] = logits_grad
        incoming = total[:, :MODEL_WIDTH] + dot(logits_grad, router, NT)
        middle = middle_ref[...]
        norm_grad, gain_grad = norm_backward(
            middle, rms_inverse(middle), gain_ref[1:2], incoming
        )
        middle_grad = grad_ref[...].astype(f32) + norm_grad
        middle_grad_ref[...] = middle_grad
        branch_grad = (RESIDUAL_SCALE * middle_grad).astype(bf16)
        branch_grad_ref[...] = branch_grad
        mixture_grad_ref[...] = dot(branch_grad, weight_ref[...]).astype(bf16)
        gain_grad_ref[...] = jnp.broadcast_to(gain_grad, (8, MODEL_WIDTH))

    wide = MODEL_WIDTH + LANES
    return pl.pallas_call(
        kernel,
        grid=(1,),
        in_specs=[
            whole_block((tokens, wide)),
            whole_block((tokens, LANES)),
            whole_block((tokens, MODEL_WIDTH)),
            whole_block((tokens, MODEL_WIDTH)),
            whole_block((tokens, MODEL_WIDTH)),
            pl.BlockSpec(
                (MODEL_WIDTH, LANES),
                lambda *_: (0, 2 * PAIR_COLS // LANES),
                pipeline_mode=pl.Buffered(1),
            ),
            square_block(1),
            whole_block((8, MODEL_WIDTH)),
        ]
        + [whole_block((tokens, wide))] * parts,
        out_specs=[
            whole_block((tokens, LANES)),
            whole_block((tokens, MODEL_WIDTH)),
            whole_block((tokens, MODEL_WIDTH)),
            whole_block((tokens, QUERY_COLS)),
            whole_block((8, MODEL_WIDTH)),
        ],
        out_shape=[
            jax.ShapeDtypeStruct((tokens, LANES), bf16),
            jax.ShapeDtypeStruct((tokens, MODEL_WIDTH), f32),
            jax.ShapeDtypeStruct((tokens, MODEL_WIDTH), bf16),
            jax.ShapeDtypeStruct((tokens, QUERY_COLS), bf16),
            jax.ShapeDtypeStruct((8, MODEL_WIDTH), f32),
        ],
        compiler_params=params(),
        cost_estimate=cost(
            2 * tokens * MODEL_WIDTH * QUERY_COLS, 2 * MODEL_WIDTH * (QUERY_COLS + 12 * tokens)
        ),
        name="return_to_attention",
    )(back, code, normed_two, middle, out_grad, w_small, w_square, gains, *back_parts)


def store_rows(product, columns, place, core, kept_ref, sent_ref):
    heads, far, rows = kept_ref.shape[:3]
    for mine in range(2):

        @pl.when(core == mine)
        def _():
            for head in range(heads):
                for group in range(2 * far):
                    first = (head * 2 * far + group) * rows
                    piece = product[first : first + rows]
                    target = kept_ref if group % 2 == mine else sent_ref
                    target[head, (group // 2) ^ place, :, columns] = piece


def weight_terms(lefts, rights):
    tokens = lefts[0].shape[0]
    tile = 384
    operands, in_specs, runs = [], [], []
    first = 0
    for left, parts in zip(lefts, rights):
        left_at = len(operands)
        operands.append(left)
        in_specs.append(whole_block((tokens, MODEL_WIDTH)))
        for right in parts:
            steps = right.shape[1] // tile
            runs.append((first, steps, left_at, len(operands)))
            operands.append(right)
            in_specs.append(
                pl.BlockSpec(
                    (tokens, tile),
                    functools.partial(
                        lambda i, first, steps: (0, jnp.clip(i - first, 0, steps - 1)),
                        first=first,
                        steps=steps,
                    ),
                )
            )
            first = first + steps
    width = first * tile

    def kernel(*refs):
        step = pl.program_id(0)
        for start, steps, left_at, right_at in runs:

            @pl.when((step >= start) & (step < start + steps))
            def _():
                refs[-1][...] = dot(refs[left_at][...], refs[right_at][...], TN).astype(bf16)

    return pl.pallas_call(
        kernel,
        grid=(first,),
        in_specs=in_specs,
        out_specs=pl.BlockSpec((MODEL_WIDTH, tile), lambda i: (0, i)),
        out_shape=jax.ShapeDtypeStruct((MODEL_WIDTH, width), bf16),
        compiler_params=params(),
        cost_estimate=cost(
            2 * tokens * MODEL_WIDTH * width,
            2 * width * (MODEL_WIDTH + tokens),
        ),
        name="weight_terms",
    )(*operands)


def leave(
    place,
    heads,
    groups,
    terms,
    query_grads,
    cosine,
    sine,
    hidden_in,
    normed,
    middle_grad,
    normed_two,
    logits_grad,
    gain_grad_two,
    w_small,
    w_query,
    gains,
):
    tokens = hidden_in.shape[0]
    parts = len(terms)
    count = len(terms[0])
    part_cols = PAIR_COLS // parts
    query_cols = QUERY_COLS // parts
    small_cols = w_small.shape[1]
    part_shape = (heads, groups // 2, MODEL_WIDTH // (heads * groups), small_cols)

    def kernel(
        place_ref,
        cosine_ref,
        sine_ref,
        hidden_ref,
        normed_ref,
        middle_grad_ref,
        normed_two_ref,
        logits_grad_ref,
        gain_two_ref,
        small_ref,
        query_weight_ref,
        gain_ref,
        *refs,
    ):
        query_grad_refs, term_refs = refs[:parts], refs[parts:-3]
        input_grad_ref, kept_ref, sent_ref = refs[-3:]

        def store(product, columns):
            store_rows(
                product.astype(bf16), columns, place_ref[0], place_ref[1], kept_ref, sent_ref
            )

        keys, lists = [], []
        for part in range(parts):
            total = term_refs[part * count][...]
            for ref in term_refs[part * count + 1 : (part + 1) * count]:
                total = total + ref[...].astype(f32)
            keys.append(turn(total[0], cosine_ref[...], sine_ref[...], -1.0).astype(bf16))
            lists.append(total[1].astype(bf16))
        keys = jnp.concatenate(keys, axis=1)
        lists = jnp.concatenate(lists, axis=1)
        incoming = dot(keys, small_ref[:, :PAIR_COLS], NT) + dot(
            lists, small_ref[:, PAIR_COLS : 2 * PAIR_COLS], NT
        )
        for part in range(parts):
            columns = slice(part * query_cols, (part + 1) * query_cols)
            incoming = incoming + dot(
                query_grad_refs[part][...], query_weight_ref[:, columns], NT
            )
        values = hidden_ref[...].astype(f32)
        norm_grad, gain_grad = norm_backward(
            values, rms_inverse(values), gain_ref[:1], incoming
        )
        input_grad_ref[...] = middle_grad_ref[...] + norm_grad
        normed = normed_ref[...]
        store(dot(normed, keys, TN), slice(0, PAIR_COLS))
        store(dot(normed, lists, TN), slice(PAIR_COLS, 2 * PAIR_COLS))
        two = gain_two_ref[:1]
        first_high = gain_grad.astype(bf16).astype(f32)
        second_high = two.astype(bf16).astype(f32)
        rows = jnp.concatenate(
            [
                jnp.zeros((EXPERTS, MODEL_WIDTH), f32),
                first_high,
                second_high,
                gain_grad - first_high,
                two - second_high,
                jnp.zeros((LANES - EXPERTS - 4, MODEL_WIDTH), f32),
            ],
            axis=0,
        )
        extras = dot(normed_two_ref[...], logits_grad_ref[...], TN) + jnp.transpose(rows)
        store(extras, slice(2 * PAIR_COLS, small_cols))

    return pl.pallas_call(
        kernel,
        grid=(1,),
        in_specs=[
            pl.BlockSpec(memory_space=pltpu.SMEM),
            whole_block((tokens, LANES)),
            whole_block((tokens, LANES)),
            whole_block((tokens, MODEL_WIDTH)),
            whole_block((tokens, MODEL_WIDTH)),
            whole_block((tokens, MODEL_WIDTH)),
            whole_block((tokens, MODEL_WIDTH)),
            whole_block((tokens, LANES)),
            whole_block((8, MODEL_WIDTH)),
            whole_block((MODEL_WIDTH, small_cols)),
            square_block(0),
            whole_block((8, MODEL_WIDTH)),
        ]
        + [whole_block((tokens, query_cols))] * parts
        + [whole_block((2, tokens, part_cols))] * (parts * count),
        out_specs=[
            whole_block((tokens, MODEL_WIDTH)),
            whole_block(part_shape),
            whole_block(part_shape),
        ],
        out_shape=[
            jax.ShapeDtypeStruct((tokens, MODEL_WIDTH), f32),
            jax.ShapeDtypeStruct(part_shape, bf16),
            jax.ShapeDtypeStruct(part_shape, bf16),
        ],
        compiler_params=params(),
        cost_estimate=cost(
            2 * tokens * MODEL_WIDTH * (QUERY_COLS + 4 * PAIR_COLS),
            2 * MODEL_WIDTH * (QUERY_COLS + 2 * small_cols + 8 * tokens),
        ),
        name="leave",
    )(
        place,
        cosine,
        sine,
        hidden_in,
        normed,
        middle_grad,
        normed_two,
        logits_grad,
        gain_grad_two,
        w_small,
        w_query,
        gains,
        *query_grads,
        *[array for part in terms for array in part],
    )


def stacked_heads(block, pair):
    first = pair * GROUP * HEAD_WIDTH
    return jnp.concatenate(
        [
            block[:, first + j * HEAD_WIDTH : first + (j + 1) * HEAD_WIDTH]
            for j in range(GROUP)
        ],
        axis=0,
    )


def masked_scores(keys, queries, starts, offset, causal):
    tokens = keys.shape[0]
    scores = dot(keys, queries, NT)
    key_place = lax.broadcasted_iota(jnp.int32, (tokens, tokens), 0)
    visible = key_place + offset >= starts
    if causal:
        visible = visible & (key_place <= lax.broadcasted_iota(jnp.int32, (tokens, tokens), 1))
    parts = [
        jnp.where(visible, scores[:, j * tokens : (j + 1) * tokens], MASKED) for j in range(GROUP)
    ]
    return jnp.concatenate(parts, axis=1)


def kv_spec(tokens):
    return pl.BlockSpec((2, tokens, LANES), lambda i: (0, 0, i))


def attend(queries, key_values, starts, name):
    tokens = queries.shape[0]
    blocks = len(key_values)
    pairs = KEY_VALUE_HEADS // PAIRED
    width = PAIRED * GROUP * HEAD_WIDTH

    def kernel(starts_ref, query_ref, *refs):
        kv_refs, (out_ref, lse_ref) = refs[:blocks], refs[blocks:]
        starts_row = starts_ref[...]
        turned = []
        lse_rows = []
        for pair in range(PAIRED):
            lanes = slice(pair * HEAD_WIDTH, (pair + 1) * HEAD_WIDTH)
            stacked = stacked_heads(query_ref[...], pair) * jnp.asarray(ATTN_SCALE, bf16)
            scores = [
                masked_scores(
                    kv_refs[b][0, :, lanes],
                    stacked,
                    starts_row,
                    (b - blocks + 1) * tokens,
                    b == blocks - 1,
                )
                for b in range(blocks)
            ]
            top = functools.reduce(
                jnp.maximum, [jnp.max(s, axis=0, keepdims=True) for s in scores]
            )
            total = jnp.zeros_like(top)
            mixed = jnp.zeros((HEAD_WIDTH, GROUP * tokens), f32)
            for b in range(blocks):
                weights = jnp.exp(scores[b] - top)
                total = total + jnp.sum(weights, axis=0, keepdims=True)
                mixed = mixed + dot(kv_refs[b][1, :, lanes], weights.astype(bf16), TN)
            mixed = mixed / total
            lse = top + jnp.log(total)
            for j in range(GROUP):
                columns = slice(j * tokens, (j + 1) * tokens)
                turned.append(mixed[:, columns])
                lse_rows.append(lse[:, columns])
        out_ref[...] = jnp.transpose(jnp.concatenate(turned, axis=0)).astype(bf16)
        lse_rows = lse_rows + [jnp.zeros((1, tokens), f32)] * (8 - len(lse_rows))
        lse_ref[0] = jnp.concatenate(lse_rows, axis=0)

    scores_count = QUERY_HEADS * tokens * tokens * blocks
    return pl.pallas_call(
        kernel,
        grid=(pairs,),
        in_specs=[
            whole_block((1, tokens)),
            pl.BlockSpec((tokens, width), lambda i: (0, i)),
        ]
        + [kv_spec(tokens)] * blocks,
        out_specs=[
            pl.BlockSpec((tokens, width), lambda i: (0, i)),
            pl.BlockSpec((1, 8, tokens), lambda i: (i, 0, 0)),
        ],
        out_shape=[
            jax.ShapeDtypeStruct((tokens, QUERY_COLS), bf16),
            jax.ShapeDtypeStruct((pairs, 8, tokens), f32),
        ],
        compiler_params=pltpu.CompilerParams(vmem_limit_bytes=VMEM_BYTES),
        cost_estimate=pl.CostEstimate(
            flops=4 * scores_count * HEAD_WIDTH,
            bytes_accessed=4 * tokens * (QUERY_COLS + blocks * PAIR_COLS),
            transcendentals=scores_count,
        ),
        name=name,
    )(starts, queries, *key_values)


def attend_backward(
    queries, key_values, starts, mixture_grad, lse, cosine, sine, part, parts, name
):
    tokens = queries.shape[0]
    blocks = len(key_values)
    pairs = KEY_VALUE_HEADS // PAIRED // parts
    first = part * pairs
    width = PAIRED * GROUP * HEAD_WIDTH

    def kernel(starts_ref, query_ref, grad_ref, lse_ref, cosine_ref, sine_ref, *refs):
        kv_refs = refs[:blocks]
        dq_ref = refs[blocks]
        dkv_refs = refs[blocks + 1 : 2 * blocks + 1]
        probs_ref, prob_grad_ref = refs[2 * blocks + 1 :]
        starts_row = starts_ref[...]
        turned = []
        for pair in range(PAIRED):
            lanes = slice(pair * HEAD_WIDTH, (pair + 1) * HEAD_WIDTH)
            stacked = stacked_heads(query_ref[...], pair) * jnp.asarray(ATTN_SCALE, bf16)
            incoming = stacked_heads(grad_ref[...], pair)
            lse_row = jnp.concatenate(
                [lse_ref[0, pair * GROUP + j : pair * GROUP + j + 1, :] for j in range(GROUP)],
                axis=1,
            )
            delta = jnp.zeros((1, GROUP * tokens), f32)
            for b in range(blocks):
                scores = masked_scores(
                    kv_refs[b][0, :, lanes],
                    stacked,
                    starts_row,
                    (b - blocks + 1) * tokens,
                    b == blocks - 1,
                )
                probs = jnp.exp(scores - lse_row)
                prob_grad = dot(kv_refs[b][1, :, lanes], incoming, NT)
                delta = delta + jnp.sum(probs * prob_grad, axis=0, keepdims=True)
                probs_ref[b] = probs
                prob_grad_ref[b] = prob_grad
            query_grad = jnp.zeros((HEAD_WIDTH, GROUP * tokens), f32)
            for b in range(blocks):
                probs = probs_ref[b]
                score_grad = (probs * (prob_grad_ref[b] - delta)).astype(bf16)
                query_grad = query_grad + dot(kv_refs[b][0, :, lanes], score_grad, TN)
                key_part = dot(score_grad, stacked)
                value_part = dot(probs.astype(bf16), incoming)
                dkv_refs[b][0, :, lanes] = key_part.astype(dkv_refs[b].dtype)
                dkv_refs[b][1, :, lanes] = value_part.astype(dkv_refs[b].dtype)
            query_grad = query_grad * ATTN_SCALE
            for j in range(GROUP):
                turned.append(query_grad[:, j * tokens : (j + 1) * tokens])
        query_grad = jnp.transpose(jnp.concatenate(turned, axis=0))
        dq_ref[...] = turn(query_grad, cosine_ref[...], sine_ref[...], -1.0).astype(bf16)

    scores_count = QUERY_HEADS // parts * tokens * tokens * blocks
    return pl.pallas_call(
        kernel,
        grid=(pairs,),
        in_specs=[
            whole_block((1, tokens)),
            pl.BlockSpec((tokens, width), lambda i: (0, first + i)),
            pl.BlockSpec((tokens, width), lambda i: (0, first + i)),
            pl.BlockSpec((1, 8, tokens), lambda i: (first + i, 0, 0)),
            whole_block((tokens, LANES)),
            whole_block((tokens, LANES)),
        ]
        + [pl.BlockSpec((2, tokens, LANES), lambda i: (0, 0, first + i))] * blocks,
        out_specs=[pl.BlockSpec((tokens, width), lambda i: (0, i))] + [kv_spec(tokens)] * blocks,
        out_shape=[jax.ShapeDtypeStruct((tokens, QUERY_COLS // parts), bf16)]
        + [jax.ShapeDtypeStruct((2, tokens, PAIR_COLS // parts), bf16)] * (blocks - 1)
        + [jax.ShapeDtypeStruct((2, tokens, PAIR_COLS // parts), f32)],
        scratch_shapes=[pltpu.VMEM((blocks, tokens, GROUP * tokens), f32)] * 2,
        compiler_params=pltpu.CompilerParams(vmem_limit_bytes=VMEM_BYTES),
        cost_estimate=pl.CostEstimate(
            flops=10 * scores_count * HEAD_WIDTH,
            bytes_accessed=4 * tokens * (2 * QUERY_COLS + 2 * blocks * PAIR_COLS),
            transcendentals=scores_count,
        ),
        name=name,
    )(starts, queries, mixture_grad, lse, cosine, sine, *key_values)


def expert_block(index):
    return pl.BlockSpec((MODEL_WIDTH, FF), lambda *_: (0, index), pipeline_mode=pl.Buffered(1))


def experts(order, inputs, grads, scaled, w_small, w_up, w_down, expert, tokens):
    rows = inputs.shape[0]
    wide = MODEL_WIDTH + LANES
    fresh = scaled is None

    def kernel(
        order_ref, expert_ref, input_ref, grad_ref, router_ref, gate_ref, up_ref, down_ref, *refs
    ):
        scaled_ref, hidden_grad_ref, input_grad_ref = refs if fresh else refs[1:]
        block = input_ref[...]
        code = grad_ref[:, MODEL_WIDTH:].astype(f32)
        lane = lax.broadcasted_iota(jnp.int32, (tokens, LANES), 1)
        logits = jnp.where(code > 0.5, dot(block, router_ref[...]), MASKED)
        raised = jnp.exp(logits - jnp.max(logits, axis=1, keepdims=True))
        raised = jnp.where(code > 0.5, raised, 0.0)
        gates = raised / jnp.sum(raised, axis=1, keepdims=True)
        kept = (lane == expert_ref[0]) & (code > 0.5) & (code < 1.5)
        gate = jnp.sum(jnp.where(kept, gates, 0.0), axis=1, keepdims=True)
        gate_part = dot(block, gate_ref[...])
        up_part = dot(block, up_ref[...])
        sigmoid = 1.0 / (1.0 + jnp.exp(-gate_part))
        silu = gate_part * sigmoid
        activation = silu * up_part
        scaled_ref[...] = (activation * gate).astype(bf16)
        pulled = dot(grad_ref[:, :MODEL_WIDTH], down_ref[...])
        gate_grad = RESIDUAL_SCALE * jnp.sum(activation * pulled, axis=1, keepdims=True)
        high = gate_grad.astype(bf16).astype(f32)
        columns = jnp.where(
            lane == expert_ref[0],
            high,
            jnp.where(lane == expert_ref[0] + EXPERTS, gate_grad - high, 0.0),
        )
        input_grad_ref[:, MODEL_WIDTH:] = columns.astype(bf16)
        activation_grad = pulled * (RESIDUAL_SCALE * gate)
        slope = sigmoid * (1.0 + gate_part * (1.0 - sigmoid))
        gate_part_grad = (activation_grad * up_part * slope).astype(bf16)
        up_part_grad = (activation_grad * silu).astype(bf16)
        hidden_grad_ref[:, :FF] = gate_part_grad
        hidden_grad_ref[:, FF:] = up_part_grad
        input_grad_ref[:, :MODEL_WIDTH] = (
            dot(gate_part_grad, gate_ref[...], NT) + dot(up_part_grad, up_ref[...], NT)
        ).astype(bf16)

    in_specs = [
        pl.BlockSpec(memory_space=pltpu.SMEM),
        pl.BlockSpec((tokens, MODEL_WIDTH), lambda i, order_ref: (i, 0)),
        pl.BlockSpec((tokens, wide), lambda i, order_ref: (order_ref[i], 0)),
        pl.BlockSpec(
            (MODEL_WIDTH, LANES),
            lambda *_: (0, 2 * PAIR_COLS // LANES),
            pipeline_mode=pl.Buffered(1),
        ),
        expert_block(0),
        expert_block(1),
        expert_block(0),
    ]
    operands = [order, expert, inputs, grads, w_small, w_up, w_up, w_down]
    if not fresh:
        in_specs.append(pl.BlockSpec(memory_space=pl.ANY))
        operands.append(scaled)
    return pl.pallas_call(
        kernel,
        grid_spec=pltpu.PrefetchScalarGridSpec(
            num_scalar_prefetch=1,
            grid=(rows // tokens,),
            in_specs=in_specs,
            out_specs=[
                pl.BlockSpec((tokens, FF), lambda i, order_ref: (order_ref[i], 0)),
                pl.BlockSpec((tokens, 2 * FF), lambda i, order_ref: (i, 0)),
                pl.BlockSpec((tokens, wide), lambda i, order_ref: (i, 0)),
            ],
        ),
        out_shape=[
            jax.ShapeDtypeStruct((grads.shape[0], FF), bf16),
            jax.ShapeDtypeStruct((rows, 2 * FF), bf16),
            jax.ShapeDtypeStruct((rows, wide), bf16),
        ],
        input_output_aliases={} if fresh else {8: 0},
        compiler_params=params(),
        cost_estimate=cost(
            10 * rows * MODEL_WIDTH * FF,
            2 * MODEL_WIDTH * (3 * rows + EXPERT_COLS),
            rows * FF,
        ),
        name="experts",
    )(*operands)


def expert_shares(scaled, weights, tokens, groups):
    count = len(scaled)

    def kernel(*refs):
        weight_ref, out_ref = refs[count:]
        for k in range(count):

            @pl.when(pl.program_id(1) == k)
            def _():
                out_ref[...] = dot(refs[k][...], weight_ref[...], NT).astype(bf16)

    rows = groups * count * tokens
    return pl.pallas_call(
        kernel,
        grid=(groups, count),
        in_specs=[pl.BlockSpec((tokens, FF), lambda i, k: (i, 0))] * count + [expert_block(0)],
        out_specs=pl.BlockSpec((tokens, MODEL_WIDTH), lambda i, k: (i * count + k, 0)),
        out_shape=jax.ShapeDtypeStruct((rows, MODEL_WIDTH), bf16),
        compiler_params=params(),
        cost_estimate=cost(
            2 * rows * MODEL_WIDTH * FF, 2 * MODEL_WIDTH * (rows + FF) + 2 * rows * FF
        ),
        name="expert_shares",
    )(*scaled, weights)


def expert_terms(pieces, scale, name):
    width = pieces[0][1].shape[1]
    tile = 384
    rows = sum(left.shape[0] for left, _ in pieces)

    def kernel(*refs):
        total = None
        for k in range(len(pieces)):
            term = dot(refs[2 * k][...], refs[2 * k + 1][...], TN)
            total = term if total is None else total + term
        refs[-1][...] = (scale * total).astype(bf16)

    in_specs = []
    for left, right in pieces:
        in_specs.append(pl.BlockSpec((left.shape[0], tile), lambda i: (0, i)))
        in_specs.append(whole_block(right.shape))
    return pl.pallas_call(
        kernel,
        grid=(MODEL_WIDTH // tile,),
        in_specs=in_specs,
        out_specs=pl.BlockSpec((tile, width), lambda i: (i, 0)),
        out_shape=jax.ShapeDtypeStruct((MODEL_WIDTH, width), bf16),
        compiler_params=params(),
        cost_estimate=cost(
            2 * rows * MODEL_WIDTH * width, 2 * (rows + width) * MODEL_WIDTH + 2 * rows * width
        ),
        name=name,
    )(*[array for piece in pieces for array in piece])


def shards(
    hidden_in,
    out_grad,
    doc_lengths,
    expert_ids,
    attention_norm,
    query_weight,
    key_matrix,
    value_matrix,
    output_weight,
    expert_norm,
    router_weight,
    expert_input,
    expert_output,
):
    tokens = hidden_in.shape[0]
    heads = lax.axis_size("head")
    groups = lax.axis_size("seq")
    own_rows = query_weight.shape[0]
    head_index = lax.axis_index("head")
    seq_index = lax.axis_index("seq")
    shared = EXPERTS // groups
    first_row = (seq_index * heads + head_index) * tokens
    expert = (seq_index * shared + head_index % shared).astype(jnp.int32)[None]

    places = first_row + jnp.arange(tokens)
    starts = doc_start(doc_lengths, places)
    cosine, sine = rope_tables(places - starts)
    starts_row = (starts - first_row).astype(jnp.int32)[None, :]

    hot = (expert_ids[:, :, None] == jnp.arange(EXPERTS)[None, None, :]).astype(f32)
    chosen = jnp.sum(hot, axis=1)
    before = (jnp.arange(tokens)[:, None] > jnp.arange(tokens)[None, :]).astype(bf16)
    earlier = dot(before, chosen.astype(bf16))
    code = jnp.where(chosen > 0.5, jnp.where(earlier < CAP - 0.5, 1.0, 2.0), 0.0)
    code = jnp.concatenate(
        [code.astype(bf16), jnp.zeros((tokens, LANES - EXPERTS), bf16)], axis=1
    )
    coded_grad = jnp.concatenate([out_grad, code], axis=1)

    def spread(block, axes):
        return lax.all_to_all(block, axes, split_axis=0, concat_axis=0, tiled=True)

    clock = Clock()
    small = jnp.concatenate(
        [
            key_matrix,
            value_matrix,
            router_weight,
            attention_norm[:, None],
            expert_norm[:, None],
            jnp.zeros((own_rows, LANES - EXPERTS - 2), bf16),
        ],
        axis=1,
    )
    w_small = lax.all_gather(small, ("head", "seq"), axis=0, tiled=True)

    def expert_rows(weight):
        weight = weight.reshape(own_rows, groups, shared, weight.shape[2])
        weight = jnp.tile(jnp.transpose(weight, (2, 1, 0, 3)), (heads // shared, 1, 1, 1))
        return Flow(
            one_move(
                weight.reshape(heads * groups, own_rows, weight.shape[3]),
                functools.partial(spread, axes=("head", "seq")),
            )
        )

    up_flow = expert_rows(expert_input)
    far_grads = [Flow(one_move(coded_grad, by_head(step))) for step in range(1, shared)]
    pending = clock.begin(up_flow, *far_grads)

    normed, own_kv, gains = enter(hidden_in, w_small, cosine, sine)
    clock.end(pending, own_kv)
    kv_flows = [
        Flow(one_move(own_kv, functools.partial(along_stream, distance=distance)))
        for distance in range(1, heads + 1)
    ]
    w_large = lax.all_gather(
        jnp.concatenate([query_weight, output_weight], axis=1),
        ("head", "seq"),
        axis=0,
        tiled=True,
    )
    clock.tick(*kv_flows)
    key_values = [flow.value for flow in kv_flows[::-1]] + [own_kv]
    down_flow = expert_rows(after(expert_output, kv_flows[-1].value))
    Clock().tick(down_flow)
    w_up = up_flow.value.reshape(MODEL_WIDTH, 2 * FF)
    w_down = down_flow.value.reshape(MODEL_WIDTH, FF)
    queries = project_queries(normed, w_large, cosine, sine)
    mixture, lse = attend(queries, key_values, starts_row, "attend")
    middle, normed_two = leave_attention(mixture, w_large, hidden_in, gains)

    input_flows = [Flow(tokens_gather(normed_two))]
    far_tokens = [Flow(one_move(normed_two, by_head(step))) for step in range(1, shared)]
    clock.tick(input_flows[0], *far_tokens, ready=(down_flow.value,))

    def seq_gather(block):
        return lax.all_gather(block, "seq", axis=0, tiled=True)

    grads = [seq_gather(after(coded_grad, *key_values))] + [
        seq_gather(after(flow.value, *key_values)) for flow in far_grads
    ]
    input_flows = input_flows + [Flow(tokens_gather(flow.value)) for flow in far_tokens]
    clock.tick(input_flows[0])
    core_flows = [Flow(one_move(clock.finish(input_flows[0]), by_seq(1)))]
    clock.tick(core_flows[0], *input_flows[1:])

    back = []
    inputs = {}
    hidden_grads = {}
    scaled = [None] * shared
    turn_of = expert
    blocks = jnp.arange(groups // 2, dtype=jnp.int32) * 2
    for step in range(shared):
        terms = []
        inputs[step, 0] = clock.finish(input_flows[step])
        if step > 0:
            core_flows.append(Flow(one_move(inputs[step, 0], by_seq(1))))
        pending = clock.begin(*core_flows[step:], *input_flows[step + 1 :], *back)
        for core in range(2):
            if core == 1:
                if step > 0:
                    clock.end(pending, turn_of)
                    pending = clock.begin(*back)
                inputs[step, 1] = clock.finish(core_flows[step])
            order = (blocks + core) ^ seq_index
            scaled[step], hidden_grads[step, core], input_grad = experts(
                order.astype(jnp.int32),
                inputs[step, core],
                grads[step],
                scaled[step],
                w_small,
                w_up,
                w_down,
                turn_of,
                tokens,
            )
            turn_of = after(expert, input_grad)
            terms.append(input_grad)
        clock.end(pending, turn_of)
        back.append(Flow(tokens_scatter(*terms)))

    work = [
        lambda first: expert_shares(
            [after(part, first) for part in scaled], w_down, tokens, groups
        ),
        lambda first: expert_terms(
            [(inputs[key], after(hidden_grads[key], first)) for key in inputs], 1.0, "up_terms"
        ),
        lambda first: expert_terms(
            [(grad, after(part, first)) for grad, part in zip(grads, scaled)],
            RESIDUAL_SCALE,
            "down_terms",
        ),
    ]
    made = []
    while not all(flow.done for flow in back):
        pending = clock.begin(*back)
        held = ()
        if len(made) < len(work):
            made.append(work[len(made)](after(turn_of, *clock.last)))
            turn_of = after(expert, made[-1])
            held = (turn_of,)
        clock.end(pending, *held)
    back_parts = [
        Flow(one_move(back[step].value.astype(bf16), by_head(step))) for step in range(1, shared)
    ]
    pending = clock.begin(*back_parts)
    while len(made) < len(work):
        made.append(work[len(made)](after(turn_of, *clock.last)))
        turn_of = after(expert, made[-1])
    clock.end(pending, turn_of)
    shares, up_part, down_part = made
    shares = lax.psum_scatter(shares, "seq", scatter_dimension=0, tiled=True)
    expert_part = jnp.concatenate([up_part, down_part], axis=1)
    expert_part = expert_part.reshape(heads * groups, own_rows, EXPERT_COLS)
    expert_flow = Flow(
        one_move(expert_part, functools.partial(spread, axes=("head", "seq")))
    )
    pending = clock.begin(expert_flow)
    logits_grad, middle_grad, branch_grad, mixture_grad, gain_grad_two = return_to_attention(
        back[0].value,
        [flow.value for flow in back_parts],
        code,
        normed_two,
        middle,
        out_grad,
        w_small,
        w_large,
        gains,
    )

    place = jnp.stack([seq_index // 2, seq_index % 2]).astype(jnp.int32)
    query_grad, *kv_terms = attend_backward(
        queries,
        key_values,
        starts_row,
        mixture_grad,
        lse,
        cosine,
        sine,
        0,
        1,
        "attend_backward",
    )
    query_grads = [query_grad]
    large_part = weight_terms(
        [normed, after(branch_grad, query_grad)], [query_grads, [mixture]]
    )
    clock.end(pending, large_part)
    large_part = lax.psum_scatter(large_part, ("head", "seq"), scatter_dimension=0, tiled=True)
    kv_flows = [
        Flow(one_move(term, functools.partial(along_stream, distance=-distance)))
        for term, distance in zip(kv_terms[:-1], range(heads, 0, -1))
    ]
    share_flows = [
        Flow(one_move(shares[step * tokens : (step + 1) * tokens], by_head(step)))
        for step in range(1, shared)
    ]
    clock.tick(*kv_flows, *share_flows)
    terms = [(kv_terms[-1], kv_flows)]
    input_grad, *small_parts = leave(
        place,
        heads,
        groups,
        [[own] + [flow.value for flow in flows] for own, flows in terms],
        query_grads,
        cosine,
        sine,
        after(hidden_in, shares),
        normed,
        middle_grad,
        normed_two,
        logits_grad,
        gain_grad_two,
        w_small,
        w_large,
        gains,
    )

    small_flow = Flow(rows_scatter(*small_parts))
    small_flow = Flow(line_scatter(clock.finish(small_flow)))
    clock.finish(small_flow)
    moe_out = shares[:tokens].astype(f32)
    for flow in share_flows:
        moe_out = moe_out + flow.value.astype(f32)
    block_out = (middle + RESIDUAL_SCALE * moe_out).astype(bf16)

    expert_sum = expert_flow.value.reshape(
        heads // shared, shared, groups, own_rows, EXPERT_COLS
    )
    expert_sum = jnp.sum(expert_sum.astype(f32), axis=0)

    def expert_output_of(first, last):
        columns = jnp.transpose(expert_sum[..., first:last], (2, 1, 0, 3))
        return columns.reshape(own_rows, EXPERTS, last - first)

    expert_input_grad = expert_output_of(0, 2 * FF)
    expert_output_grad = expert_output_of(2 * FF, EXPERT_COLS)
    large_sum = after(large_part, small_flow.value).astype(f32)
    query_weight_grad = large_sum[:, :QUERY_COLS]
    output_grad = large_sum[:, QUERY_COLS:]
    small_sum = small_flow.value
    key_grad = small_sum[:, :PAIR_COLS]
    value_grad = small_sum[:, PAIR_COLS : 2 * PAIR_COLS]
    rest = small_sum[:, 2 * PAIR_COLS :]
    router_grad = rest[:, :EXPERTS]
    attention_norm_grad = rest[:, EXPERTS] + rest[:, EXPERTS + 2]
    expert_norm_grad = rest[:, EXPERTS + 1] + rest[:, EXPERTS + 3]
    return (
        block_out,
        input_grad,
        attention_norm_grad,
        query_weight_grad,
        key_grad,
        value_grad,
        output_grad,
        expert_norm_grad,
        router_grad,
        expert_input_grad,
        expert_output_grad,
    )


def solution(mesh):
    return jax.shard_map(
        shards,
        mesh=mesh,
        in_specs=(
            P(("seq", "head"), None),
            P(("seq", "head"), None),
            P(),
            P(("seq", "head"), None),
            P(("head", "seq")),
            P(("head", "seq"), None),
            P(("head", "seq"), None),
            P(("head", "seq"), None),
            P(("head", "seq"), None),
            P(("head", "seq")),
            P(("head", "seq"), None),
            P(("head", "seq"), None, None),
            P(("head", "seq"), None, None),
        ),
        out_specs=(
            P(("seq", "head"), None),
            P(("seq", "head"), None),
            P(("head", "seq")),
            P(("head", "seq"), None),
            P(("head", "seq"), None),
            P(("head", "seq"), None),
            P(("head", "seq"), None),
            P(("head", "seq")),
            P(("head", "seq"), None),
            P(("head", "seq"), None, None),
            P(("head", "seq"), None, None),
        ),
        check_vma=False,
    )
```

```python
import functools

import jax
import jax.numpy as jnp
from jax import lax
from jax.experimental import pallas as pl
from jax.experimental.pallas import tpu as pltpu
from jax.sharding import PartitionSpec as P

MODEL_WIDTH = 1536
QUERY_HEADS = 24
KEY_VALUE_HEADS = 8
HEAD_WIDTH = 64
FF = 512
EXPERTS = 16
CAP = 160

EPS = 1e-06
ATTN_SCALE = 1.0 / 64.0
RESIDUAL_SCALE = 0.22
MASKED = -1e30

GROUP = QUERY_HEADS // KEY_VALUE_HEADS
QUERY_COLS = QUERY_HEADS * HEAD_WIDTH
PAIR_COLS = KEY_VALUE_HEADS * HEAD_WIDTH
LANES = 128
HALF = HEAD_WIDTH // 2
PAIRED = LANES // HEAD_WIDTH
EXPERT_COLS = 3 * FF

bf16 = jnp.bfloat16
f32 = jnp.float32

NT = (((1,), (1,)), ((), ()))
TN = (((0,), (0,)), ((), ()))
VMEM_BYTES = 56 * 1024 * 1024


def dot(left, right, dims=(((1,), (0,)), ((), ()))):
    return lax.dot_general(left, right, dims, preferred_element_type=f32)


def swap(block, mask):
    count = lax.axis_size("seq")
    return lax.ppermute(block, "seq", [(i, i ^ mask) for i in range(count)])


def around(block, distance):
    count = lax.axis_size("head")
    return lax.ppermute(block, "head", [(i, (i + distance) % count) for i in range(count)])


def along_stream(block, distance):
    heads, groups = lax.axis_size("head"), lax.axis_size("seq")
    route = []
    for group in range(groups):
        for head in range(heads):
            target = group * heads + head + distance
            if 0 <= target < heads * groups:
                route.append((head * groups + group, (target % heads) * groups + target // heads))
    return lax.ppermute(block, ("head", "seq"), route)


def side(mask):
    return (lax.axis_index("seq") // mask) % 2


def far_masks():
    masks, mask = [], 2
    while mask < lax.axis_size("seq"):
        masks.append(mask)
        mask = mask * 2
    return masks


def join(own, other, bit, axis):
    return jnp.where(
        bit == 0, jnp.stack([own, other], axis=axis), jnp.stack([other, own], axis=axis)
    )


def swap_head(block, mask):
    count = lax.axis_size("head")
    return lax.ppermute(block, "head", [(i, i ^ mask) for i in range(count)])


def head_side(mask):
    return (lax.axis_index("head") // mask) % 2


def after(value, *others):
    return lax.optimization_barrier((value,) + others)[0]


class Flow:
    def __init__(self, steps):
        self.steps = steps
        self.value = None
        self.moves = []
        self.done = False
        self.feed(None)

    def feed(self, results):
        try:
            self.moves = self.steps.send(results)
        except StopIteration as stop:
            self.value, self.moves, self.done = stop.value, [], True


class Clock:
    def __init__(self):
        self.last = ()

    def begin(self, *flows, ready=()):
        flows = [flow for flow in flows if not flow.done]
        blocks = tuple(block for flow in flows for block, _ in flow.moves)
        if not blocks:
            return [], []
        tied = lax.optimization_barrier(blocks + tuple(self.last) + tuple(ready))
        movers = [move for flow in flows for _, move in flow.moves]
        return flows, [move(block) for move, block in zip(movers, tied)]

    def end(self, pending, *held):
        flows, results = pending
        if not results:
            return
        if held:
            results = list(lax.optimization_barrier(tuple(results) + held)[: len(results)])
        self.last = tuple(results)
        for flow in flows:
            count = len(flow.moves)
            flow.feed(results[:count])
            results = results[count:]

    def tick(self, *flows, ready=()):
        self.end(self.begin(*flows, ready=ready))

    def finish(self, *flows):
        while not all(flow.done for flow in flows):
            self.tick(*flows)
        return flows[0].value if len(flows) == 1 else [flow.value for flow in flows]


def by_seq(mask):
    return lambda block: swap(block, mask)


def by_head(mask):
    return lambda block: swap_head(block, mask)


def one_move(block, move):
    (result,) = yield [(block, move)]
    return result


def line_gather(block):
    heads = lax.axis_size("head")
    here = lax.axis_index("head")
    whole = jnp.zeros((heads,) + block.shape, block.dtype)
    whole = lax.dynamic_update_index_in_dim(whole, block, here, 0)
    results = yield [
        (block, functools.partial(around, distance=distance)) for distance in range(1, heads)
    ]
    for distance, result in enumerate(results, 1):
        whole = lax.dynamic_update_index_in_dim(whole, result, (here - distance) % heads, 0)
    return whole


def rows_gather(block):
    lines = yield from line_gather(block)
    masks = far_masks()
    middle = lines.shape[0] // 2
    parts = [(lines[:middle], masks), (lines[middle:], masks[::-1])]
    for step in range(len(masks)):
        results = yield [(part, by_seq(order[step])) for part, order in parts]
        parts = [
            (
                join(
                    part,
                    result,
                    side(order[step]),
                    1 + sum(1 for other in order[:step] if other > order[step]),
                ),
                order,
            )
            for (part, order), result in zip(parts, results)
        ]
    whole = jnp.concatenate([part for part, _ in parts], axis=0)
    (result,) = yield [(whole, by_seq(1))]
    whole = join(whole, result, side(1), 1 + len(masks))
    return whole.reshape(MODEL_WIDTH, block.shape[1])


def rows_scatter(kept, sent):
    masks = far_masks()
    (result,) = yield [(sent, by_seq(1))]
    whole = (kept.astype(f32) + result.astype(f32)).astype(bf16)
    whole = whole.reshape(whole.shape[:1] + (2,) * len(masks) + whole.shape[2:])
    middle = whole.shape[0] // 2
    parts = [(whole[:middle], masks), (whole[middle:], masks[::-1])]
    for step in range(len(masks)):
        axes = [
            1 + sum(1 for other in order[step + 1 :] if other > order[step])
            for _, order in parts
        ]
        results = yield [
            (lax.index_in_dim(part, 1, axis, False), by_seq(order[step]))
            for (part, order), axis in zip(parts, axes)
        ]
        parts = [
            (
                (
                    lax.index_in_dim(part, 0, axis, False).astype(f32) + result.astype(f32)
                ).astype(bf16),
                order,
            )
            for (part, order), axis, result in zip(parts, axes, results)
        ]
    return jnp.concatenate([part for part, _ in parts], axis=0)


def line_scatter(terms):
    heads = lax.axis_size("head")
    here = lax.axis_index("head")
    results = yield [
        (
            lax.dynamic_index_in_dim(terms, (here + distance) % heads, 0, False),
            functools.partial(around, distance=distance),
        )
        for distance in range(1, heads)
    ]
    total = lax.dynamic_index_in_dim(terms, here, 0, False).astype(f32)
    for result in results:
        total = total + result.astype(f32)
    return total


def tokens_gather(block):
    masks = far_masks()
    middle = block.shape[0] // 2
    parts = [(block[:middle], masks), (block[middle:], masks[::-1])]
    for step in range(len(masks)):
        results = yield [(part, by_seq(order[step])) for part, order in parts]
        parts = [
            (
                jnp.stack(
                    [part, result],
                    axis=sum(1 for other in order[:step] if other > order[step]),
                ),
                order,
            )
            for (part, order), result in zip(parts, results)
        ]
    whole = jnp.concatenate([part for part, _ in parts], axis=len(masks))
    return whole.reshape((lax.axis_size("seq") // 2 * block.shape[0],) + block.shape[1:])


def tokens_scatter(own, other):
    masks = far_masks()
    blocks = lax.axis_size("seq") // 2
    (result,) = yield [(other, by_seq(1))]
    whole = (own.astype(f32) + result.astype(f32)).astype(bf16)
    whole = whole.reshape((2,) * len(masks) + (own.shape[0] // blocks, own.shape[1]))
    middle = whole.shape[-2] // 2
    parts = [(whole[..., :middle, :], masks), (whole[..., middle:, :], masks[::-1])]
    for step in range(len(masks)):
        axes = [sum(1 for other in order[step + 1 :] if other > order[step]) for _, order in parts]
        results = yield [
            (lax.index_in_dim(part, 1, axis, False), by_seq(order[step]))
            for (part, order), axis in zip(parts, axes)
        ]
        last = step == len(masks) - 1
        parts = [
            (
                (
                    lax.index_in_dim(part, 0, axis, False).astype(f32) + result.astype(f32)
                ).astype(f32 if last else bf16),
                order,
            )
            for (part, order), axis, result in zip(parts, axes, results)
        ]
    return jnp.concatenate([part for part, _ in parts], axis=0)


def doc_start(doc_lengths, places):
    starts = jnp.cumsum(doc_lengths) - doc_lengths
    earlier = starts[None, :] <= places[:, None]
    return jnp.max(jnp.where(earlier, starts[None, :], 0), axis=1)


def rope_tables(places):
    frequency = jnp.exp(
        -jnp.log(10000.0) * 2.0 * jnp.arange(HALF).astype(f32) / HEAD_WIDTH
    )
    angles = places.astype(f32)[:, None] * frequency[None, :]
    cosine, sine = jnp.cos(angles), jnp.sin(angles)
    return (
        jnp.concatenate([cosine] * (LANES // HALF), axis=1),
        jnp.concatenate([-sine, sine] * PAIRED, axis=1),
    )


def turn(values, cosine, sine, sign):
    lane = lax.broadcasted_iota(jnp.int32, (values.shape[0], LANES), 1) % HEAD_WIDTH
    pieces = []
    for first in range(0, values.shape[1], LANES):
        piece = values[:, first : first + LANES]
        swapped = jnp.where(
            lane < HALF, pltpu.roll(piece, LANES - HALF, 1), pltpu.roll(piece, HALF, 1)
        )
        pieces.append(piece * cosine + (sign * swapped) * sine)
    return jnp.concatenate(pieces, axis=1)


def whole_block(shape):
    return pl.BlockSpec(shape, lambda *_: (0,) * len(shape), pipeline_mode=pl.Buffered(1))


def params():
    return pltpu.CompilerParams(vmem_limit_bytes=VMEM_BYTES)


def cost(flops, moved, transcendentals=0, weight=1):
    return pl.CostEstimate(
        flops=weight * flops,
        bytes_accessed=weight * moved,
        transcendentals=weight * transcendentals,
    )


def rms_inverse(values):
    return lax.rsqrt(jnp.mean(values * values, axis=1, keepdims=True) + EPS)


def norm_backward(values, inverse, gain, incoming):
    scaled = incoming * gain
    mean_term = jnp.mean(scaled * values, axis=1, keepdims=True)
    values_grad = inverse * scaled - values * (inverse * inverse * inverse * mean_term)
    gain_grad = jnp.sum(incoming * values * inverse, axis=0, keepdims=True)
    return (values_grad, gain_grad)


def enter(hidden_in, w_small, cosine, sine):
    tokens = hidden_in.shape[0]
    small_cols = w_small.shape[1]

    def kernel(hidden_ref, weight_ref, cosine_ref, sine_ref, normed_ref, kv_ref, gain_ref):
        extras = jnp.transpose(weight_ref[:, 2 * PAIR_COLS :].astype(f32))
        gains = extras[EXPERTS : EXPERTS + 8]
        gain_ref[...] = gains
        values = hidden_ref[...].astype(f32)
        normed = (values * rms_inverse(values) * gains[:1]).astype(bf16)
        normed_ref[...] = normed
        keys = dot(normed, weight_ref[:, :PAIR_COLS])
        kv_ref[0] = turn(keys, cosine_ref[...], sine_ref[...], 1.0).astype(bf16)
        kv_ref[1] = dot(normed, weight_ref[:, PAIR_COLS : 2 * PAIR_COLS]).astype(bf16)

    return pl.pallas_call(
        kernel,
        out_shape=[
            jax.ShapeDtypeStruct((tokens, MODEL_WIDTH), bf16),
            jax.ShapeDtypeStruct((2, tokens, PAIR_COLS), bf16),
            jax.ShapeDtypeStruct((8, MODEL_WIDTH), f32),
        ],
        compiler_params=params(),
        cost_estimate=cost(
            4 * tokens * MODEL_WIDTH * PAIR_COLS, 2 * MODEL_WIDTH * (small_cols + 2 * tokens)
        ),
        name="enter",
    )(hidden_in, w_small, cosine, sine)


def project_queries(normed, w_square, cosine, sine):
    tokens = normed.shape[0]
    width = 512

    def kernel(normed_ref, weight_ref, cosine_ref, sine_ref, out_ref):
        product = dot(normed_ref[...], weight_ref[...])
        out_ref[...] = turn(product, cosine_ref[...], sine_ref[...], 1.0).astype(bf16)

    return pl.pallas_call(
        kernel,
        grid=(QUERY_COLS // width,),
        in_specs=[
            whole_block((tokens, MODEL_WIDTH)),
            pl.BlockSpec((MODEL_WIDTH, width), lambda i: (0, i)),
            whole_block((tokens, LANES)),
            whole_block((tokens, LANES)),
        ],
        out_specs=pl.BlockSpec((tokens, width), lambda i: (0, i)),
        out_shape=jax.ShapeDtypeStruct((tokens, QUERY_COLS), bf16),
        compiler_params=params(),
        cost_estimate=cost(
            2 * tokens * MODEL_WIDTH * QUERY_COLS, 2 * MODEL_WIDTH * (QUERY_COLS + 2 * tokens)
        ),
        name="project_queries",
    )(normed, w_square, cosine, sine)


def square_block(index):
    return pl.BlockSpec(
        (MODEL_WIDTH, MODEL_WIDTH), lambda *_: (0, index), pipeline_mode=pl.Buffered(1)
    )


def leave_attention(mixture, w_square, hidden_in, gains):
    tokens = mixture.shape[0]

    def kernel(mixture_ref, weight_ref, hidden_ref, gain_ref, middle_ref, normed_ref):
        branch = dot(mixture_ref[...], weight_ref[...], NT)
        middle = hidden_ref[...].astype(f32) + RESIDUAL_SCALE * branch
        middle_ref[...] = middle
        normed_ref[...] = (middle * rms_inverse(middle) * gain_ref[1:2]).astype(bf16)

    return pl.pallas_call(
        kernel,
        grid=(1,),
        in_specs=[
            whole_block((tokens, QUERY_COLS)),
            square_block(1),
            whole_block((tokens, MODEL_WIDTH)),
            whole_block((8, MODEL_WIDTH)),
        ],
        out_specs=[whole_block((tokens, MODEL_WIDTH))] * 2,
        out_shape=[
            jax.ShapeDtypeStruct((tokens, MODEL_WIDTH), f32),
            jax.ShapeDtypeStruct((tokens, MODEL_WIDTH), bf16),
        ],
        compiler_params=params(),
        cost_estimate=cost(
            2 * tokens * MODEL_WIDTH * QUERY_COLS, 2 * MODEL_WIDTH * (QUERY_COLS + 5 * tokens)
        ),
        name="leave_attention",
    )(mixture, w_square, hidden_in, gains)


def return_to_attention(back, back_parts, code, normed_two, middle, out_grad, w_small, w_square, gains):
    tokens = middle.shape[0]
    parts = len(back_parts)

    def kernel(
        back_ref,
        code_ref,
        normed_ref,
        middle_ref,
        grad_ref,
        router_ref,
        weight_ref,
        gain_ref,
        *refs,
    ):
        logits_grad_ref, middle_grad_ref, branch_grad_ref, mixture_grad_ref, gain_grad_ref = refs[
            parts:
        ]
        total = back_ref[...]
        for ref in refs[:parts]:
            total = total + ref[...].astype(f32)
        code = code_ref[...].astype(f32)
        lane = lax.broadcasted_iota(jnp.int32, (tokens, LANES), 1)
        router = jnp.where(
            lax.broadcasted_iota(jnp.int32, (MODEL_WIDTH, LANES), 1) < EXPERTS,
            router_ref[...],
            jnp.asarray(0.0, bf16),
        )
        logits = jnp.where(code > 0.5, dot(normed_ref[...], router), MASKED)
        raised = jnp.exp(logits - jnp.max(logits, axis=1, keepdims=True))
        raised = jnp.where(code > 0.5, raised, 0.0)
        gates = raised / jnp.sum(raised, axis=1, keepdims=True)
        extra = total[:, MODEL_WIDTH:]
        gate_grad = extra + pltpu.roll(extra, LANES - EXPERTS, 1)
        gate_grad = jnp.where((lane < EXPERTS) & (code > 0.5) & (code < 1.5), gate_grad, 0.0)
        inner = jnp.sum(gates * gate_grad, axis=1, keepdims=True)
        logits_grad = (gates * (gate_grad - inner)).astype(bf16)
        logits_grad_ref[...] = logits_grad
        incoming = total[:, :MODEL_WIDTH] + dot(logits_grad, router, NT)
        middle = middle_ref[...]
        norm_grad, gain_grad = norm_backward(
            middle, rms_inverse(middle), gain_ref[1:2], incoming
        )
        middle_grad = grad_ref[...].astype(f32) + norm_grad
        middle_grad_ref[...] = middle_grad
        branch_grad = (RESIDUAL_SCALE * middle_grad).astype(bf16)
        branch_grad_ref[...] = branch_grad
        mixture_grad_ref[...] = dot(branch_grad, weight_ref[...]).astype(bf16)
        gain_grad_ref[...] = jnp.broadcast_to(gain_grad, (8, MODEL_WIDTH))

    wide = MODEL_WIDTH + LANES
    return pl.pallas_call(
        kernel,
        grid=(1,),
        in_specs=[
            whole_block((tokens, wide)),
            whole_block((tokens, LANES)),
            whole_block((tokens, MODEL_WIDTH)),
            whole_block((tokens, MODEL_WIDTH)),
            whole_block((tokens, MODEL_WIDTH)),
            pl.BlockSpec(
                (MODEL_WIDTH, LANES),
                lambda *_: (0, 2 * PAIR_COLS // LANES),
                pipeline_mode=pl.Buffered(1),
            ),
            square_block(1),
            whole_block((8, MODEL_WIDTH)),
        ]
        + [whole_block((tokens, wide))] * parts,
        out_specs=[
            whole_block((tokens, LANES)),
            whole_block((tokens, MODEL_WIDTH)),
            whole_block((tokens, MODEL_WIDTH)),
            whole_block((tokens, QUERY_COLS)),
            whole_block((8, MODEL_WIDTH)),
        ],
        out_shape=[
            jax.ShapeDtypeStruct((tokens, LANES), bf16),
            jax.ShapeDtypeStruct((tokens, MODEL_WIDTH), f32),
            jax.ShapeDtypeStruct((tokens, MODEL_WIDTH), bf16),
            jax.ShapeDtypeStruct((tokens, QUERY_COLS), bf16),
            jax.ShapeDtypeStruct((8, MODEL_WIDTH), f32),
        ],
        compiler_params=params(),
        cost_estimate=cost(
            2 * tokens * MODEL_WIDTH * QUERY_COLS, 2 * MODEL_WIDTH * (QUERY_COLS + 12 * tokens)
        ),
        name="return_to_attention",
    )(back, code, normed_two, middle, out_grad, w_small, w_square, gains, *back_parts)


def store_rows(product, columns, place, core, kept_ref, sent_ref):
    heads, far, rows = kept_ref.shape[:3]
    for mine in range(2):

        @pl.when(core == mine)
        def _():
            for head in range(heads):
                for group in range(2 * far):
                    first = (head * 2 * far + group) * rows
                    piece = product[first : first + rows]
                    target = kept_ref if group % 2 == mine else sent_ref
                    target[head, (group // 2) ^ place, :, columns] = piece


def weight_terms(lefts, rights):
    tokens = lefts[0].shape[0]
    tile = 384
    operands, in_specs, runs = [], [], []
    first = 0
    for left, parts in zip(lefts, rights):
        left_at = len(operands)
        operands.append(left)
        in_specs.append(whole_block((tokens, MODEL_WIDTH)))
        for right in parts:
            steps = right.shape[1] // tile
            runs.append((first, steps, left_at, len(operands)))
            operands.append(right)
            in_specs.append(
                pl.BlockSpec(
                    (tokens, tile),
                    functools.partial(
                        lambda i, first, steps: (0, jnp.clip(i - first, 0, steps - 1)),
                        first=first,
                        steps=steps,
                    ),
                )
            )
            first = first + steps
    width = first * tile

    def kernel(*refs):
        step = pl.program_id(0)
        for start, steps, left_at, right_at in runs:

            @pl.when((step >= start) & (step < start + steps))
            def _():
                refs[-1][...] = dot(refs[left_at][...], refs[right_at][...], TN).astype(bf16)

    return pl.pallas_call(
        kernel,
        grid=(first,),
        in_specs=in_specs,
        out_specs=pl.BlockSpec((MODEL_WIDTH, tile), lambda i: (0, i)),
        out_shape=jax.ShapeDtypeStruct((MODEL_WIDTH, width), bf16),
        compiler_params=params(),
        cost_estimate=cost(
            2 * tokens * MODEL_WIDTH * width,
            2 * width * (MODEL_WIDTH + tokens),
        ),
        name="weight_terms",
    )(*operands)


def leave(
    place,
    heads,
    groups,
    terms,
    query_grads,
    cosine,
    sine,
    hidden_in,
    normed,
    middle_grad,
    normed_two,
    logits_grad,
    gain_grad_two,
    w_small,
    w_query,
    gains,
):
    tokens = hidden_in.shape[0]
    parts = len(terms)
    count = len(terms[0])
    part_cols = PAIR_COLS // parts
    query_cols = QUERY_COLS // parts
    small_cols = w_small.shape[1]
    part_shape = (heads, groups // 2, MODEL_WIDTH // (heads * groups), small_cols)

    def kernel(
        place_ref,
        cosine_ref,
        sine_ref,
        hidden_ref,
        normed_ref,
        middle_grad_ref,
        normed_two_ref,
        logits_grad_ref,
        gain_two_ref,
        small_ref,
        query_weight_ref,
        gain_ref,
        *refs,
    ):
        query_grad_refs, term_refs = refs[:parts], refs[parts:-3]
        input_grad_ref, kept_ref, sent_ref = refs[-3:]

        def store(product, columns):
            store_rows(
                product.astype(bf16), columns, place_ref[0], place_ref[1], kept_ref, sent_ref
            )

        keys, lists = [], []
        for part in range(parts):
            total = term_refs[part * count][...]
            for ref in term_refs[part * count + 1 : (part + 1) * count]:
                total = total + ref[...].astype(f32)
            keys.append(turn(total[0], cosine_ref[...], sine_ref[...], -1.0).astype(bf16))
            lists.append(total[1].astype(bf16))
        keys = jnp.concatenate(keys, axis=1)
        lists = jnp.concatenate(lists, axis=1)
        incoming = dot(keys, small_ref[:, :PAIR_COLS], NT) + dot(
            lists, small_ref[:, PAIR_COLS : 2 * PAIR_COLS], NT
        )
        for part in range(parts):
            columns = slice(part * query_cols, (part + 1) * query_cols)
            incoming = incoming + dot(
                query_grad_refs[part][...], query_weight_ref[:, columns], NT
            )
        values = hidden_ref[...].astype(f32)
        norm_grad, gain_grad = norm_backward(
            values, rms_inverse(values), gain_ref[:1], incoming
        )
        input_grad_ref[...] = middle_grad_ref[...] + norm_grad
        normed = normed_ref[...]
        store(dot(normed, keys, TN), slice(0, PAIR_COLS))
        store(dot(normed, lists, TN), slice(PAIR_COLS, 2 * PAIR_COLS))
        two = gain_two_ref[:1]
        first_high = gain_grad.astype(bf16).astype(f32)
        second_high = two.astype(bf16).astype(f32)
        rows = jnp.concatenate(
            [
                jnp.zeros((EXPERTS, MODEL_WIDTH), f32),
                first_high,
                second_high,
                gain_grad - first_high,
                two - second_high,
                jnp.zeros((LANES - EXPERTS - 4, MODEL_WIDTH), f32),
            ],
            axis=0,
        )
        extras = dot(normed_two_ref[...], logits_grad_ref[...], TN) + jnp.transpose(rows)
        store(extras, slice(2 * PAIR_COLS, small_cols))

    return pl.pallas_call(
        kernel,
        grid=(1,),
        in_specs=[
            pl.BlockSpec(memory_space=pltpu.SMEM),
            whole_block((tokens, LANES)),
            whole_block((tokens, LANES)),
            whole_block((tokens, MODEL_WIDTH)),
            whole_block((tokens, MODEL_WIDTH)),
            whole_block((tokens, MODEL_WIDTH)),
            whole_block((tokens, MODEL_WIDTH)),
            whole_block((tokens, LANES)),
            whole_block((8, MODEL_WIDTH)),
            whole_block((MODEL_WIDTH, small_cols)),
            square_block(0),
            whole_block((8, MODEL_WIDTH)),
        ]
        + [whole_block((tokens, query_cols))] * parts
        + [whole_block((2, tokens, part_cols))] * (parts * count),
        out_specs=[
            whole_block((tokens, MODEL_WIDTH)),
            whole_block(part_shape),
            whole_block(part_shape),
        ],
        out_shape=[
            jax.ShapeDtypeStruct((tokens, MODEL_WIDTH), f32),
            jax.ShapeDtypeStruct(part_shape, bf16),
            jax.ShapeDtypeStruct(part_shape, bf16),
        ],
        compiler_params=params(),
        cost_estimate=cost(
            2 * tokens * MODEL_WIDTH * (QUERY_COLS + 4 * PAIR_COLS),
            2 * MODEL_WIDTH * (QUERY_COLS + 2 * small_cols + 8 * tokens),
        ),
        name="leave",
    )(
        place,
        cosine,
        sine,
        hidden_in,
        normed,
        middle_grad,
        normed_two,
        logits_grad,
        gain_grad_two,
        w_small,
        w_query,
        gains,
        *query_grads,
        *[array for part in terms for array in part],
    )


def stacked_heads(block, pair):
    first = pair * GROUP * HEAD_WIDTH
    return jnp.concatenate(
        [
            block[:, first + j * HEAD_WIDTH : first + (j + 1) * HEAD_WIDTH]
            for j in range(GROUP)
        ],
        axis=0,
    )


def masked_scores(keys, queries, starts, offset, causal):
    tokens = keys.shape[0]
    scores = dot(keys, queries, NT)
    key_place = lax.broadcasted_iota(jnp.int32, (tokens, tokens), 0)
    visible = key_place + offset >= starts
    if causal:
        visible = visible & (key_place <= lax.broadcasted_iota(jnp.int32, (tokens, tokens), 1))
    parts = [
        jnp.where(visible, scores[:, j * tokens : (j + 1) * tokens], MASKED) for j in range(GROUP)
    ]
    return jnp.concatenate(parts, axis=1)


def kv_spec(tokens):
    return pl.BlockSpec((2, tokens, LANES), lambda i: (0, 0, i))


def attend(queries, key_values, starts, name):
    tokens = queries.shape[0]
    blocks = len(key_values)
    pairs = KEY_VALUE_HEADS // PAIRED
    width = PAIRED * GROUP * HEAD_WIDTH

    def kernel(starts_ref, query_ref, *refs):
        kv_refs, (out_ref, lse_ref) = refs[:blocks], refs[blocks:]
        starts_row = starts_ref[...]
        turned = []
        lse_rows = []
        for pair in range(PAIRED):
            lanes = slice(pair * HEAD_WIDTH, (pair + 1) * HEAD_WIDTH)
            stacked = stacked_heads(query_ref[...], pair) * jnp.asarray(ATTN_SCALE, bf16)
            scores = [
                masked_scores(
                    kv_refs[b][0, :, lanes],
                    stacked,
                    starts_row,
                    (b - blocks + 1) * tokens,
                    b == blocks - 1,
                )
                for b in range(blocks)
            ]
            top = functools.reduce(
                jnp.maximum, [jnp.max(s, axis=0, keepdims=True) for s in scores]
            )
            total = jnp.zeros_like(top)
            mixed = jnp.zeros((HEAD_WIDTH, GROUP * tokens), f32)
            for b in range(blocks):
                weights = jnp.exp(scores[b] - top)
                total = total + jnp.sum(weights, axis=0, keepdims=True)
                mixed = mixed + dot(kv_refs[b][1, :, lanes], weights.astype(bf16), TN)
            mixed = mixed / total
            lse = top + jnp.log(total)
            for j in range(GROUP):
                columns = slice(j * tokens, (j + 1) * tokens)
                turned.append(mixed[:, columns])
                lse_rows.append(lse[:, columns])
        out_ref[...] = jnp.transpose(jnp.concatenate(turned, axis=0)).astype(bf16)
        lse_rows = lse_rows + [jnp.zeros((1, tokens), f32)] * (8 - len(lse_rows))
        lse_ref[0] = jnp.concatenate(lse_rows, axis=0)

    scores_count = QUERY_HEADS * tokens * tokens * blocks
    return pl.pallas_call(
        kernel,
        grid=(pairs,),
        in_specs=[
            whole_block((1, tokens)),
            pl.BlockSpec((tokens, width), lambda i: (0, i)),
        ]
        + [kv_spec(tokens)] * blocks,
        out_specs=[
            pl.BlockSpec((tokens, width), lambda i: (0, i)),
            pl.BlockSpec((1, 8, tokens), lambda i: (i, 0, 0)),
        ],
        out_shape=[
            jax.ShapeDtypeStruct((tokens, QUERY_COLS), bf16),
            jax.ShapeDtypeStruct((pairs, 8, tokens), f32),
        ],
        compiler_params=pltpu.CompilerParams(vmem_limit_bytes=VMEM_BYTES),
        cost_estimate=pl.CostEstimate(
            flops=4 * scores_count * HEAD_WIDTH,
            bytes_accessed=4 * tokens * (QUERY_COLS + blocks * PAIR_COLS),
            transcendentals=scores_count,
        ),
        name=name,
    )(starts, queries, *key_values)


def attend_backward(
    queries, key_values, starts, mixture_grad, lse, cosine, sine, part, parts, name
):
    tokens = queries.shape[0]
    blocks = len(key_values)
    pairs = KEY_VALUE_HEADS // PAIRED // parts
    first = part * pairs
    width = PAIRED * GROUP * HEAD_WIDTH

    def kernel(starts_ref, query_ref, grad_ref, lse_ref, cosine_ref, sine_ref, *refs):
        kv_refs = refs[:blocks]
        dq_ref = refs[blocks]
        dkv_refs = refs[blocks + 1 : 2 * blocks + 1]
        probs_ref, prob_grad_ref = refs[2 * blocks + 1 :]
        starts_row = starts_ref[...]
        turned = []
        for pair in range(PAIRED):
            lanes = slice(pair * HEAD_WIDTH, (pair + 1) * HEAD_WIDTH)
            stacked = stacked_heads(query_ref[...], pair) * jnp.asarray(ATTN_SCALE, bf16)
            incoming = stacked_heads(grad_ref[...], pair)
            lse_row = jnp.concatenate(
                [lse_ref[0, pair * GROUP + j : pair * GROUP + j + 1, :] for j in range(GROUP)],
                axis=1,
            )
            delta = jnp.zeros((1, GROUP * tokens), f32)
            for b in range(blocks):
                scores = masked_scores(
                    kv_refs[b][0, :, lanes],
                    stacked,
                    starts_row,
                    (b - blocks + 1) * tokens,
                    b == blocks - 1,
                )
                probs = jnp.exp(scores - lse_row)
                prob_grad = dot(kv_refs[b][1, :, lanes], incoming, NT)
                delta = delta + jnp.sum(probs * prob_grad, axis=0, keepdims=True)
                probs_ref[b] = probs
                prob_grad_ref[b] = prob_grad
            query_grad = jnp.zeros((HEAD_WIDTH, GROUP * tokens), f32)
            for b in range(blocks):
                probs = probs_ref[b]
                score_grad = (probs * (prob_grad_ref[b] - delta)).astype(bf16)
                query_grad = query_grad + dot(kv_refs[b][0, :, lanes], score_grad, TN)
                key_part = dot(score_grad, stacked)
                value_part = dot(probs.astype(bf16), incoming)
                dkv_refs[b][0, :, lanes] = key_part.astype(dkv_refs[b].dtype)
                dkv_refs[b][1, :, lanes] = value_part.astype(dkv_refs[b].dtype)
            query_grad = query_grad * ATTN_SCALE
            for j in range(GROUP):
                turned.append(query_grad[:, j * tokens : (j + 1) * tokens])
        query_grad = jnp.transpose(jnp.concatenate(turned, axis=0))
        dq_ref[...] = turn(query_grad, cosine_ref[...], sine_ref[...], -1.0).astype(bf16)

    scores_count = QUERY_HEADS // parts * tokens * tokens * blocks
    return pl.pallas_call(
        kernel,
        grid=(pairs,),
        in_specs=[
            whole_block((1, tokens)),
            pl.BlockSpec((tokens, width), lambda i: (0, first + i)),
            pl.BlockSpec((tokens, width), lambda i: (0, first + i)),
            pl.BlockSpec((1, 8, tokens), lambda i: (first + i, 0, 0)),
            whole_block((tokens, LANES)),
            whole_block((tokens, LANES)),
        ]
        + [pl.BlockSpec((2, tokens, LANES), lambda i: (0, 0, first + i))] * blocks,
        out_specs=[pl.BlockSpec((tokens, width), lambda i: (0, i))] + [kv_spec(tokens)] * blocks,
        out_shape=[jax.ShapeDtypeStruct((tokens, QUERY_COLS // parts), bf16)]
        + [jax.ShapeDtypeStruct((2, tokens, PAIR_COLS // parts), bf16)] * (blocks - 1)
        + [jax.ShapeDtypeStruct((2, tokens, PAIR_COLS // parts), f32)],
        scratch_shapes=[pltpu.VMEM((blocks, tokens, GROUP * tokens), f32)] * 2,
        compiler_params=pltpu.CompilerParams(vmem_limit_bytes=VMEM_BYTES),
        cost_estimate=pl.CostEstimate(
            flops=10 * scores_count * HEAD_WIDTH,
            bytes_accessed=4 * tokens * (2 * QUERY_COLS + 2 * blocks * PAIR_COLS),
            transcendentals=scores_count,
        ),
        name=name,
    )(starts, queries, mixture_grad, lse, cosine, sine, *key_values)


def expert_block(index):
    return pl.BlockSpec((MODEL_WIDTH, FF), lambda *_: (0, index), pipeline_mode=pl.Buffered(1))


def experts(order, inputs, grads, scaled, w_small, w_up, w_down, expert, tokens):
    rows = inputs.shape[0]
    wide = MODEL_WIDTH + LANES
    fresh = scaled is None

    def kernel(
        order_ref, expert_ref, input_ref, grad_ref, router_ref, gate_ref, up_ref, down_ref, *refs
    ):
        scaled_ref, hidden_grad_ref, input_grad_ref = refs if fresh else refs[1:]
        block = input_ref[...]
        code = grad_ref[:, MODEL_WIDTH:].astype(f32)
        lane = lax.broadcasted_iota(jnp.int32, (tokens, LANES), 1)
        logits = jnp.where(code > 0.5, dot(block, router_ref[...]), MASKED)
        raised = jnp.exp(logits - jnp.max(logits, axis=1, keepdims=True))
        raised = jnp.where(code > 0.5, raised, 0.0)
        gates = raised / jnp.sum(raised, axis=1, keepdims=True)
        kept = (lane == expert_ref[0]) & (code > 0.5) & (code < 1.5)
        gate = jnp.sum(jnp.where(kept, gates, 0.0), axis=1, keepdims=True)
        gate_part = dot(block, gate_ref[...])
        up_part = dot(block, up_ref[...])
        sigmoid = 1.0 / (1.0 + jnp.exp(-gate_part))
        silu = gate_part * sigmoid
        activation = silu * up_part
        scaled_ref[...] = (activation * gate).astype(bf16)
        pulled = dot(grad_ref[:, :MODEL_WIDTH], down_ref[...])
        gate_grad = RESIDUAL_SCALE * jnp.sum(activation * pulled, axis=1, keepdims=True)
        high = gate_grad.astype(bf16).astype(f32)
        columns = jnp.where(
            lane == expert_ref[0],
            high,
            jnp.where(lane == expert_ref[0] + EXPERTS, gate_grad - high, 0.0),
        )
        input_grad_ref[:, MODEL_WIDTH:] = columns.astype(bf16)
        activation_grad = pulled * (RESIDUAL_SCALE * gate)
        slope = sigmoid * (1.0 + gate_part * (1.0 - sigmoid))
        gate_part_grad = (activation_grad * up_part * slope).astype(bf16)
        up_part_grad = (activation_grad * silu).astype(bf16)
        hidden_grad_ref[:, :FF] = gate_part_grad
        hidden_grad_ref[:, FF:] = up_part_grad
        input_grad_ref[:, :MODEL_WIDTH] = (
            dot(gate_part_grad, gate_ref[...], NT) + dot(up_part_grad, up_ref[...], NT)
        ).astype(bf16)

    in_specs = [
        pl.BlockSpec(memory_space=pltpu.SMEM),
        pl.BlockSpec((tokens, MODEL_WIDTH), lambda i, order_ref: (i, 0)),
        pl.BlockSpec((tokens, wide), lambda i, order_ref: (order_ref[i], 0)),
        pl.BlockSpec(
            (MODEL_WIDTH, LANES),
            lambda *_: (0, 2 * PAIR_COLS // LANES),
            pipeline_mode=pl.Buffered(1),
        ),
        expert_block(0),
        expert_block(1),
        expert_block(0),
    ]
    operands = [order, expert, inputs, grads, w_small, w_up, w_up, w_down]
    if not fresh:
        in_specs.append(pl.BlockSpec(memory_space=pl.ANY))
        operands.append(scaled)
    return pl.pallas_call(
        kernel,
        grid_spec=pltpu.PrefetchScalarGridSpec(
            num_scalar_prefetch=1,
            grid=(rows // tokens,),
            in_specs=in_specs,
            out_specs=[
                pl.BlockSpec((tokens, FF), lambda i, order_ref: (order_ref[i], 0)),
                pl.BlockSpec((tokens, 2 * FF), lambda i, order_ref: (i, 0)),
                pl.BlockSpec((tokens, wide), lambda i, order_ref: (i, 0)),
            ],
        ),
        out_shape=[
            jax.ShapeDtypeStruct((grads.shape[0], FF), bf16),
            jax.ShapeDtypeStruct((rows, 2 * FF), bf16),
            jax.ShapeDtypeStruct((rows, wide), bf16),
        ],
        input_output_aliases={} if fresh else {8: 0},
        compiler_params=params(),
        cost_estimate=cost(
            10 * rows * MODEL_WIDTH * FF,
            2 * MODEL_WIDTH * (3 * rows + EXPERT_COLS),
            rows * FF,
        ),
        name="experts",
    )(*operands)


def expert_shares(orders, scaled, weights, tokens, groups):
    count = len(scaled)

    def kernel(orders_ref, *refs):
        weight_ref, out_ref = refs[count:]
        for k in range(count):

            @pl.when(pl.program_id(1) == k)
            def _():
                out_ref[...] = dot(refs[k][...], weight_ref[...], NT).astype(bf16)

    def piece_spec(piece):
        return pl.BlockSpec(
            (tokens, FF), lambda i, k, orders_ref: (orders_ref[piece * groups + i], 0)
        )

    rows = groups * count * tokens
    return pl.pallas_call(
        kernel,
        grid_spec=pltpu.PrefetchScalarGridSpec(
            num_scalar_prefetch=1,
            grid=(groups, count),
            in_specs=[piece_spec(k) for k in range(count)] + [expert_block(0)],
            out_specs=pl.BlockSpec(
                (tokens, MODEL_WIDTH), lambda i, k, orders_ref: (i * count + k, 0)
            ),
        ),
        out_shape=jax.ShapeDtypeStruct((rows, MODEL_WIDTH), bf16),
        compiler_params=params(),
        cost_estimate=cost(
            2 * rows * MODEL_WIDTH * FF, 2 * MODEL_WIDTH * (rows + FF) + 2 * rows * FF
        ),
        name="expert_shares",
    )(orders, *scaled, weights)


def expert_terms(pieces, scale, name):
    width = pieces[0][1].shape[1]
    tile = 384
    rows = sum(left.shape[0] for left, _ in pieces)

    def kernel(*refs):
        total = None
        for k in range(len(pieces)):
            term = dot(refs[2 * k][...], refs[2 * k + 1][...], TN)
            total = term if total is None else total + term
        refs[-1][...] = (scale * total).astype(bf16)

    in_specs = []
    for left, right in pieces:
        in_specs.append(pl.BlockSpec((left.shape[0], tile), lambda i: (0, i)))
        in_specs.append(whole_block(right.shape))
    return pl.pallas_call(
        kernel,
        grid=(MODEL_WIDTH // tile,),
        in_specs=in_specs,
        out_specs=pl.BlockSpec((tile, width), lambda i: (i, 0)),
        out_shape=jax.ShapeDtypeStruct((MODEL_WIDTH, width), bf16),
        compiler_params=params(),
        cost_estimate=cost(
            2 * rows * MODEL_WIDTH * width, 2 * (rows + width) * MODEL_WIDTH + 2 * rows * width
        ),
        name=name,
    )(*[array for piece in pieces for array in piece])


def shards(
    hidden_in,
    out_grad,
    doc_lengths,
    expert_ids,
    attention_norm,
    query_weight,
    key_matrix,
    value_matrix,
    output_weight,
    expert_norm,
    router_weight,
    expert_input,
    expert_output,
):
    tokens = hidden_in.shape[0]
    heads = lax.axis_size("head")
    groups = lax.axis_size("seq")
    own_rows = query_weight.shape[0]
    head_index = lax.axis_index("head")
    seq_index = lax.axis_index("seq")
    shared = EXPERTS // groups
    first_row = (seq_index * heads + head_index) * tokens
    expert = (seq_index * shared + head_index % shared).astype(jnp.int32)[None]

    places = first_row + jnp.arange(tokens)
    starts = doc_start(doc_lengths, places)
    cosine, sine = rope_tables(places - starts)
    starts_row = (starts - first_row).astype(jnp.int32)[None, :]

    hot = (expert_ids[:, :, None] == jnp.arange(EXPERTS)[None, None, :]).astype(f32)
    chosen = jnp.sum(hot, axis=1)
    before = (jnp.arange(tokens)[:, None] > jnp.arange(tokens)[None, :]).astype(bf16)
    earlier = dot(before, chosen.astype(bf16))
    code = jnp.where(chosen > 0.5, jnp.where(earlier < CAP - 0.5, 1.0, 2.0), 0.0)
    code = jnp.concatenate(
        [code.astype(bf16), jnp.zeros((tokens, LANES - EXPERTS), bf16)], axis=1
    )
    coded_grad = jnp.concatenate([out_grad, code], axis=1)

    def spread(block, axes):
        return lax.all_to_all(block, axes, split_axis=0, concat_axis=0, tiled=True)

    clock = Clock()
    small = jnp.concatenate(
        [
            key_matrix,
            value_matrix,
            router_weight,
            attention_norm[:, None],
            expert_norm[:, None],
            jnp.zeros((own_rows, LANES - EXPERTS - 2), bf16),
        ],
        axis=1,
    )
    w_small = lax.all_gather(small, ("head", "seq"), axis=0, tiled=True)

    def expert_rows(weight):
        weight = weight.reshape(own_rows, groups, shared, weight.shape[2])
        weight = jnp.tile(jnp.transpose(weight, (2, 1, 0, 3)), (heads // shared, 1, 1, 1))
        return Flow(
            one_move(
                weight.reshape(heads * groups, own_rows, weight.shape[3]),
                functools.partial(spread, axes=("head", "seq")),
            )
        )

    up_flow = expert_rows(expert_input)
    far_grads = [Flow(one_move(coded_grad, by_head(step))) for step in range(1, shared)]
    pending = clock.begin(up_flow, *far_grads)

    normed, own_kv, gains = enter(hidden_in, w_small, cosine, sine)
    clock.end(pending, own_kv)
    kv_flows = [
        Flow(one_move(own_kv, functools.partial(along_stream, distance=distance)))
        for distance in range(1, heads + 1)
    ]
    w_large = lax.all_gather(
        jnp.concatenate([query_weight, output_weight], axis=1),
        ("head", "seq"),
        axis=0,
        tiled=True,
    )
    grad_flows = [Flow(tokens_gather(flow.value)) for flow in far_grads]
    clock.tick(kv_flows[0], kv_flows[-1], *grad_flows)
    clock.tick(*kv_flows[1:-1], *grad_flows)
    key_values = [flow.value for flow in kv_flows[::-1]] + [own_kv]
    down_flow = expert_rows(after(expert_output, kv_flows[-1].value))
    Clock().tick(down_flow)
    w_up = up_flow.value.reshape(MODEL_WIDTH, 2 * FF)
    w_down = down_flow.value.reshape(MODEL_WIDTH, FF)
    queries = project_queries(normed, w_large, cosine, sine)
    mixture, lse = attend(queries, key_values, starts_row, "attend")
    middle, normed_two = leave_attention(mixture, w_large, hidden_in, gains)

    input_flows = [Flow(tokens_gather(normed_two))]
    far_tokens = [Flow(one_move(normed_two, by_head(step))) for step in range(1, shared)]
    for flow in grad_flows:
        clock.finish(flow)
    grad_cores = [Flow(one_move(flow.value, by_seq(1))) for flow in grad_flows]
    clock.tick(input_flows[0], *far_tokens, *grad_cores, ready=(down_flow.value,))

    def seq_gather(block):
        return lax.all_gather(block, "seq", axis=0, tiled=True)

    grads = [seq_gather(after(coded_grad, *key_values))] + [
        jnp.concatenate([flow.value, core.value], axis=0)
        for flow, core in zip(grad_flows, grad_cores)
    ]
    input_flows = input_flows + [Flow(tokens_gather(flow.value)) for flow in far_tokens]
    clock.tick(input_flows[0])
    core_flows = [Flow(one_move(clock.finish(input_flows[0]), by_seq(1)))]

    back = []
    inputs = {}
    hidden_grads = {}
    scaled = [None] * shared
    turn_of = expert
    blocks = jnp.arange(groups // 2, dtype=jnp.int32) * 2
    for step in range(shared):
        terms = []
        inputs[step, 0] = clock.finish(input_flows[step])
        if step > 0:
            core_flows.append(Flow(one_move(inputs[step, 0], by_seq(1))))
        pending = clock.begin(*core_flows[step:], *input_flows[step + 1 :], *back)
        for core in range(2):
            if core == 1:
                clock.end(pending, turn_of)
                pending = clock.begin(*input_flows[step + 1 :], *back)
                inputs[step, 1] = clock.finish(core_flows[step])
            if step == 0:
                order = (blocks + core) ^ seq_index
            else:
                order = core * (groups // 2) + jnp.arange(groups // 2)
            scaled[step], hidden_grads[step, core], input_grad = experts(
                order.astype(jnp.int32),
                inputs[step, core],
                grads[step],
                scaled[step],
                w_small,
                w_up,
                w_down,
                turn_of,
                tokens,
            )
            turn_of = after(expert, input_grad)
            terms.append(input_grad)
        clock.end(pending, turn_of)
        back.append(Flow(tokens_scatter(*terms)))

    everyone = jnp.arange(groups)
    place_of = everyone ^ seq_index
    place_of = (place_of % 2) * (groups // 2) + place_of // 2
    orders = jnp.concatenate([everyone] + [place_of] * (shared - 1)).astype(jnp.int32)
    work = [
        lambda first: expert_shares(
            orders, [after(part, first) for part in scaled], w_down, tokens, groups
        ),
        lambda first: expert_terms(
            [(inputs[key], after(hidden_grads[key], first)) for key in inputs], 1.0, "up_terms"
        ),
        lambda first: expert_terms(
            [(grad, after(part, first)) for grad, part in zip(grads, scaled)],
            RESIDUAL_SCALE,
            "down_terms",
        ),
    ]
    made = []
    while not all(flow.done for flow in back):
        pending = clock.begin(*back)
        held = ()
        if len(made) < len(work):
            made.append(work[len(made)](after(turn_of, *clock.last)))
            turn_of = after(expert, made[-1])
            held = (turn_of,)
        clock.end(pending, *held)
    back_parts = [
        Flow(one_move(back[step].value.astype(bf16), by_head(step))) for step in range(1, shared)
    ]
    pending = clock.begin(*back_parts)
    while len(made) < len(work):
        made.append(work[len(made)](after(turn_of, *clock.last)))
        turn_of = after(expert, made[-1])
    clock.end(pending, turn_of)
    shares, up_part, down_part = made
    shares = lax.psum_scatter(shares, "seq", scatter_dimension=0, tiled=True)
    expert_part = jnp.concatenate([up_part, down_part], axis=1)
    expert_part = expert_part.reshape(heads * groups, own_rows, EXPERT_COLS)
    expert_flow = Flow(
        one_move(expert_part, functools.partial(spread, axes=("head", "seq")))
    )
    pending = clock.begin(expert_flow)
    logits_grad, middle_grad, branch_grad, mixture_grad, gain_grad_two = return_to_attention(
        back[0].value,
        [flow.value for flow in back_parts],
        code,
        normed_two,
        middle,
        out_grad,
        w_small,
        w_large,
        gains,
    )

    place = jnp.stack([seq_index // 2, seq_index % 2]).astype(jnp.int32)
    query_grad, *kv_terms = attend_backward(
        queries,
        key_values,
        starts_row,
        mixture_grad,
        lse,
        cosine,
        sine,
        0,
        1,
        "attend_backward",
    )
    query_grads = [query_grad]
    large_part = weight_terms(
        [normed, after(branch_grad, query_grad)], [query_grads, [mixture]]
    )
    clock.end(pending, large_part)
    large_part = lax.psum_scatter(large_part, ("head", "seq"), scatter_dimension=0, tiled=True)
    kv_flows = [
        Flow(one_move(term, functools.partial(along_stream, distance=-distance)))
        for term, distance in zip(kv_terms[:-1], range(heads, 0, -1))
    ]
    share_flows = [
        Flow(one_move(shares[step * tokens : (step + 1) * tokens], by_head(step)))
        for step in range(1, shared)
    ]
    clock.tick(*kv_flows, *share_flows)
    terms = [(kv_terms[-1], kv_flows)]
    input_grad, *small_parts = leave(
        place,
        heads,
        groups,
        [[own] + [flow.value for flow in flows] for own, flows in terms],
        query_grads,
        cosine,
        sine,
        after(hidden_in, shares),
        normed,
        middle_grad,
        normed_two,
        logits_grad,
        gain_grad_two,
        w_small,
        w_large,
        gains,
    )

    small_flow = Flow(rows_scatter(*small_parts))
    small_flow = Flow(line_scatter(clock.finish(small_flow)))
    clock.finish(small_flow)
    moe_out = shares[:tokens].astype(f32)
    for flow in share_flows:
        moe_out = moe_out + flow.value.astype(f32)
    block_out = (middle + RESIDUAL_SCALE * moe_out).astype(bf16)

    expert_sum = expert_flow.value.reshape(
        heads // shared, shared, groups, own_rows, EXPERT_COLS
    )
    expert_sum = jnp.sum(expert_sum.astype(f32), axis=0)

    def expert_output_of(first, last):
        columns = jnp.transpose(expert_sum[..., first:last], (2, 1, 0, 3))
        return columns.reshape(own_rows, EXPERTS, last - first)

    expert_input_grad = expert_output_of(0, 2 * FF)
    expert_output_grad = expert_output_of(2 * FF, EXPERT_COLS)
    large_sum = after(large_part, small_flow.value).astype(f32)
    query_weight_grad = large_sum[:, :QUERY_COLS]
    output_grad = large_sum[:, QUERY_COLS:]
    small_sum = small_flow.value
    key_grad = small_sum[:, :PAIR_COLS]
    value_grad = small_sum[:, PAIR_COLS : 2 * PAIR_COLS]
    rest = small_sum[:, 2 * PAIR_COLS :]
    router_grad = rest[:, :EXPERTS]
    attention_norm_grad = rest[:, EXPERTS] + rest[:, EXPERTS + 2]
    expert_norm_grad = rest[:, EXPERTS + 1] + rest[:, EXPERTS + 3]
    return (
        block_out,
        input_grad,
        attention_norm_grad,
        query_weight_grad,
        key_grad,
        value_grad,
        output_grad,
        expert_norm_grad,
        router_grad,
        expert_input_grad,
        expert_output_grad,
    )


def solution(mesh):
    return jax.shard_map(
        shards,
        mesh=mesh,
        in_specs=(
            P(("seq", "head"), None),
            P(("seq", "head"), None),
            P(),
            P(("seq", "head"), None),
            P(("head", "seq")),
            P(("head", "seq"), None),
            P(("head", "seq"), None),
            P(("head", "seq"), None),
            P(("head", "seq"), None),
            P(("head", "seq")),
            P(("head", "seq"), None),
            P(("head", "seq"), None, None),
            P(("head", "seq"), None, None),
        ),
        out_specs=(
            P(("seq", "head"), None),
            P(("seq", "head"), None),
            P(("head", "seq")),
            P(("head", "seq"), None),
            P(("head", "seq"), None),
            P(("head", "seq"), None),
            P(("head", "seq"), None),
            P(("head", "seq")),
            P(("head", "seq"), None),
            P(("head", "seq"), None, None),
            P(("head", "seq"), None, None),
        ),
        check_vma=False,
    )
```

```python
import functools

import jax
import jax.numpy as jnp
from jax import lax
from jax.experimental import pallas as pl
from jax.experimental.pallas import tpu as pltpu
from jax.sharding import PartitionSpec as P

MODEL_WIDTH = 1536
QUERY_HEADS = 24
KEY_VALUE_HEADS = 8
HEAD_WIDTH = 64
FF = 512
EXPERTS = 16
CAP = 160

EPS = 1e-06
ATTN_SCALE = 1.0 / 64.0
RESIDUAL_SCALE = 0.22
MASKED = -1e30

GROUP = QUERY_HEADS // KEY_VALUE_HEADS
QUERY_COLS = QUERY_HEADS * HEAD_WIDTH
PAIR_COLS = KEY_VALUE_HEADS * HEAD_WIDTH
LANES = 128
HALF = HEAD_WIDTH // 2
PAIRED = LANES // HEAD_WIDTH
EXPERT_COLS = 3 * FF

bf16 = jnp.bfloat16
f32 = jnp.float32

NT = (((1,), (1,)), ((), ()))
TN = (((0,), (0,)), ((), ()))
VMEM_BYTES = 56 * 1024 * 1024


def dot(left, right, dims=(((1,), (0,)), ((), ()))):
    return lax.dot_general(left, right, dims, preferred_element_type=f32)


def swap(block, mask):
    count = lax.axis_size("seq")
    return lax.ppermute(block, "seq", [(i, i ^ mask) for i in range(count)])


def around(block, distance):
    count = lax.axis_size("head")
    return lax.ppermute(block, "head", [(i, (i + distance) % count) for i in range(count)])


def along_stream(block, distance):
    heads, groups = lax.axis_size("head"), lax.axis_size("seq")
    route = []
    for group in range(groups):
        for head in range(heads):
            target = group * heads + head + distance
            if 0 <= target < heads * groups:
                route.append((head * groups + group, (target % heads) * groups + target // heads))
    return lax.ppermute(block, ("head", "seq"), route)


def side(mask):
    return (lax.axis_index("seq") // mask) % 2


def far_masks():
    masks, mask = [], 2
    while mask < lax.axis_size("seq"):
        masks.append(mask)
        mask = mask * 2
    return masks


def join(own, other, bit, axis):
    return jnp.where(
        bit == 0, jnp.stack([own, other], axis=axis), jnp.stack([other, own], axis=axis)
    )


def swap_head(block, mask):
    count = lax.axis_size("head")
    return lax.ppermute(block, "head", [(i, i ^ mask) for i in range(count)])


def head_side(mask):
    return (lax.axis_index("head") // mask) % 2


def after(value, *others):
    return lax.optimization_barrier((value,) + others)[0]


class Flow:
    def __init__(self, steps):
        self.steps = steps
        self.value = None
        self.moves = []
        self.done = False
        self.feed(None)

    def feed(self, results):
        try:
            self.moves = self.steps.send(results)
        except StopIteration as stop:
            self.value, self.moves, self.done = stop.value, [], True


class Clock:
    def __init__(self):
        self.last = ()

    def begin(self, *flows, ready=()):
        flows = [flow for flow in flows if not flow.done]
        blocks = tuple(block for flow in flows for block, _ in flow.moves)
        if not blocks:
            return [], []
        tied = lax.optimization_barrier(blocks + tuple(self.last) + tuple(ready))
        movers = [move for flow in flows for _, move in flow.moves]
        return flows, [move(block) for move, block in zip(movers, tied)]

    def end(self, pending, *held):
        flows, results = pending
        if not results:
            return
        if held:
            results = list(lax.optimization_barrier(tuple(results) + held)[: len(results)])
        self.last = tuple(results)
        for flow in flows:
            count = len(flow.moves)
            flow.feed(results[:count])
            results = results[count:]

    def tick(self, *flows, ready=()):
        self.end(self.begin(*flows, ready=ready))

    def finish(self, *flows):
        while not all(flow.done for flow in flows):
            self.tick(*flows)
        return flows[0].value if len(flows) == 1 else [flow.value for flow in flows]


def by_seq(mask):
    return lambda block: swap(block, mask)


def by_head(mask):
    return lambda block: swap_head(block, mask)


def one_move(block, move):
    (result,) = yield [(block, move)]
    return result


def line_gather(block):
    heads = lax.axis_size("head")
    here = lax.axis_index("head")
    whole = jnp.zeros((heads,) + block.shape, block.dtype)
    whole = lax.dynamic_update_index_in_dim(whole, block, here, 0)
    results = yield [
        (block, functools.partial(around, distance=distance)) for distance in range(1, heads)
    ]
    for distance, result in enumerate(results, 1):
        whole = lax.dynamic_update_index_in_dim(whole, result, (here - distance) % heads, 0)
    return whole


def rows_gather(block):
    lines = yield from line_gather(block)
    masks = far_masks()
    middle = lines.shape[0] // 2
    parts = [(lines[:middle], masks), (lines[middle:], masks[::-1])]
    for step in range(len(masks)):
        results = yield [(part, by_seq(order[step])) for part, order in parts]
        parts = [
            (
                join(
                    part,
                    result,
                    side(order[step]),
                    1 + sum(1 for other in order[:step] if other > order[step]),
                ),
                order,
            )
            for (part, order), result in zip(parts, results)
        ]
    whole = jnp.concatenate([part for part, _ in parts], axis=0)
    (result,) = yield [(whole, by_seq(1))]
    whole = join(whole, result, side(1), 1 + len(masks))
    return whole.reshape(MODEL_WIDTH, block.shape[1])


def rows_scatter(kept, sent):
    masks = far_masks()
    (result,) = yield [(sent, by_seq(1))]
    whole = (kept.astype(f32) + result.astype(f32)).astype(bf16)
    whole = whole.reshape(whole.shape[:1] + (2,) * len(masks) + whole.shape[2:])
    middle = whole.shape[0] // 2
    parts = [(whole[:middle], masks), (whole[middle:], masks[::-1])]
    for step in range(len(masks)):
        axes = [
            1 + sum(1 for other in order[step + 1 :] if other > order[step])
            for _, order in parts
        ]
        results = yield [
            (lax.index_in_dim(part, 1, axis, False), by_seq(order[step]))
            for (part, order), axis in zip(parts, axes)
        ]
        parts = [
            (
                (
                    lax.index_in_dim(part, 0, axis, False).astype(f32) + result.astype(f32)
                ).astype(bf16),
                order,
            )
            for (part, order), axis, result in zip(parts, axes, results)
        ]
    return jnp.concatenate([part for part, _ in parts], axis=0)


def line_scatter(terms):
    heads = lax.axis_size("head")
    here = lax.axis_index("head")
    results = yield [
        (
            lax.dynamic_index_in_dim(terms, (here + distance) % heads, 0, False),
            functools.partial(around, distance=distance),
        )
        for distance in range(1, heads)
    ]
    total = lax.dynamic_index_in_dim(terms, here, 0, False).astype(f32)
    for result in results:
        total = total + result.astype(f32)
    return total


def tokens_gather(block):
    masks = far_masks()
    middle = block.shape[0] // 2
    parts = [(block[:middle], masks), (block[middle:], masks[::-1])]
    for step in range(len(masks)):
        results = yield [(part, by_seq(order[step])) for part, order in parts]
        parts = [
            (
                jnp.stack(
                    [part, result],
                    axis=sum(1 for other in order[:step] if other > order[step]),
                ),
                order,
            )
            for (part, order), result in zip(parts, results)
        ]
    whole = jnp.concatenate([part for part, _ in parts], axis=len(masks))
    return whole.reshape((lax.axis_size("seq") // 2 * block.shape[0],) + block.shape[1:])


def tokens_scatter(own, other):
    masks = far_masks()
    blocks = lax.axis_size("seq") // 2
    (result,) = yield [(other, by_seq(1))]
    whole = (own.astype(f32) + result.astype(f32)).astype(bf16)
    whole = whole.reshape((2,) * len(masks) + (own.shape[0] // blocks, own.shape[1]))
    middle = whole.shape[-2] // 2
    parts = [(whole[..., :middle, :], masks), (whole[..., middle:, :], masks[::-1])]
    for step in range(len(masks)):
        axes = [sum(1 for other in order[step + 1 :] if other > order[step]) for _, order in parts]
        results = yield [
            (lax.index_in_dim(part, 1, axis, False), by_seq(order[step]))
            for (part, order), axis in zip(parts, axes)
        ]
        last = step == len(masks) - 1
        parts = [
            (
                (
                    lax.index_in_dim(part, 0, axis, False).astype(f32) + result.astype(f32)
                ).astype(f32 if last else bf16),
                order,
            )
            for (part, order), axis, result in zip(parts, axes, results)
        ]
    return jnp.concatenate([part for part, _ in parts], axis=0)


def doc_start(doc_lengths, places):
    starts = jnp.cumsum(doc_lengths) - doc_lengths
    earlier = starts[None, :] <= places[:, None]
    return jnp.max(jnp.where(earlier, starts[None, :], 0), axis=1)


def rope_tables(places):
    frequency = jnp.exp(
        -jnp.log(10000.0) * 2.0 * jnp.arange(HALF).astype(f32) / HEAD_WIDTH
    )
    angles = places.astype(f32)[:, None] * frequency[None, :]
    cosine, sine = jnp.cos(angles), jnp.sin(angles)
    return (
        jnp.concatenate([cosine] * (LANES // HALF), axis=1),
        jnp.concatenate([-sine, sine] * PAIRED, axis=1),
    )


def turn(values, cosine, sine, sign):
    lane = lax.broadcasted_iota(jnp.int32, (values.shape[0], LANES), 1) % HEAD_WIDTH
    pieces = []
    for first in range(0, values.shape[1], LANES):
        piece = values[:, first : first + LANES]
        swapped = jnp.where(
            lane < HALF, pltpu.roll(piece, LANES - HALF, 1), pltpu.roll(piece, HALF, 1)
        )
        pieces.append(piece * cosine + (sign * swapped) * sine)
    return jnp.concatenate(pieces, axis=1)


def whole_block(shape):
    return pl.BlockSpec(shape, lambda *_: (0,) * len(shape), pipeline_mode=pl.Buffered(1))


def params():
    return pltpu.CompilerParams(vmem_limit_bytes=VMEM_BYTES)


def cost(flops, moved, transcendentals=0, weight=1):
    return pl.CostEstimate(
        flops=weight * flops,
        bytes_accessed=weight * moved,
        transcendentals=weight * transcendentals,
    )


def rms_inverse(values):
    return lax.rsqrt(jnp.mean(values * values, axis=1, keepdims=True) + EPS)


def norm_backward(values, inverse, gain, incoming):
    scaled = incoming * gain
    mean_term = jnp.mean(scaled * values, axis=1, keepdims=True)
    values_grad = inverse * scaled - values * (inverse * inverse * inverse * mean_term)
    gain_grad = jnp.sum(incoming * values * inverse, axis=0, keepdims=True)
    return (values_grad, gain_grad)


def enter(hidden_in, w_small, cosine, sine):
    tokens = hidden_in.shape[0]
    small_cols = w_small.shape[1]

    def kernel(hidden_ref, weight_ref, cosine_ref, sine_ref, normed_ref, kv_ref, gain_ref):
        extras = jnp.transpose(weight_ref[:, 2 * PAIR_COLS :].astype(f32))
        gains = extras[EXPERTS : EXPERTS + 8]
        gain_ref[...] = gains
        values = hidden_ref[...].astype(f32)
        normed = (values * rms_inverse(values) * gains[:1]).astype(bf16)
        normed_ref[...] = normed
        keys = dot(normed, weight_ref[:, :PAIR_COLS])
        kv_ref[0] = turn(keys, cosine_ref[...], sine_ref[...], 1.0).astype(bf16)
        kv_ref[1] = dot(normed, weight_ref[:, PAIR_COLS : 2 * PAIR_COLS]).astype(bf16)

    return pl.pallas_call(
        kernel,
        out_shape=[
            jax.ShapeDtypeStruct((tokens, MODEL_WIDTH), bf16),
            jax.ShapeDtypeStruct((2, tokens, PAIR_COLS), bf16),
            jax.ShapeDtypeStruct((8, MODEL_WIDTH), f32),
        ],
        compiler_params=params(),
        cost_estimate=cost(
            4 * tokens * MODEL_WIDTH * PAIR_COLS, 2 * MODEL_WIDTH * (small_cols + 2 * tokens)
        ),
        name="enter",
    )(hidden_in, w_small, cosine, sine)


def project_queries(normed, w_square, cosine, sine):
    tokens = normed.shape[0]
    width = 512

    def kernel(normed_ref, weight_ref, cosine_ref, sine_ref, out_ref):
        product = dot(normed_ref[...], weight_ref[...])
        out_ref[...] = turn(product, cosine_ref[...], sine_ref[...], 1.0).astype(bf16)

    return pl.pallas_call(
        kernel,
        grid=(QUERY_COLS // width,),
        in_specs=[
            whole_block((tokens, MODEL_WIDTH)),
            pl.BlockSpec((MODEL_WIDTH, width), lambda i: (0, i)),
            whole_block((tokens, LANES)),
            whole_block((tokens, LANES)),
        ],
        out_specs=pl.BlockSpec((tokens, width), lambda i: (0, i)),
        out_shape=jax.ShapeDtypeStruct((tokens, QUERY_COLS), bf16),
        compiler_params=params(),
        cost_estimate=cost(
            2 * tokens * MODEL_WIDTH * QUERY_COLS, 2 * MODEL_WIDTH * (QUERY_COLS + 2 * tokens)
        ),
        name="project_queries",
    )(normed, w_square, cosine, sine)


def square_block(index):
    return pl.BlockSpec(
        (MODEL_WIDTH, MODEL_WIDTH), lambda *_: (0, index), pipeline_mode=pl.Buffered(1)
    )


def leave_attention(mixture, w_square, hidden_in, gains):
    tokens = mixture.shape[0]

    def kernel(mixture_ref, weight_ref, hidden_ref, gain_ref, middle_ref, normed_ref):
        branch = dot(mixture_ref[...], weight_ref[...], NT)
        middle = hidden_ref[...].astype(f32) + RESIDUAL_SCALE * branch
        middle_ref[...] = middle
        normed_ref[...] = (middle * rms_inverse(middle) * gain_ref[1:2]).astype(bf16)

    return pl.pallas_call(
        kernel,
        grid=(1,),
        in_specs=[
            whole_block((tokens, QUERY_COLS)),
            square_block(1),
            whole_block((tokens, MODEL_WIDTH)),
            whole_block((8, MODEL_WIDTH)),
        ],
        out_specs=[whole_block((tokens, MODEL_WIDTH))] * 2,
        out_shape=[
            jax.ShapeDtypeStruct((tokens, MODEL_WIDTH), f32),
            jax.ShapeDtypeStruct((tokens, MODEL_WIDTH), bf16),
        ],
        compiler_params=params(),
        cost_estimate=cost(
            2 * tokens * MODEL_WIDTH * QUERY_COLS, 2 * MODEL_WIDTH * (QUERY_COLS + 5 * tokens)
        ),
        name="leave_attention",
    )(mixture, w_square, hidden_in, gains)


def return_to_attention(back, back_parts, code, normed_two, middle, out_grad, w_small, w_square, gains):
    tokens = middle.shape[0]
    parts = len(back_parts)

    def kernel(
        back_ref,
        code_ref,
        normed_ref,
        middle_ref,
        grad_ref,
        router_ref,
        weight_ref,
        gain_ref,
        *refs,
    ):
        logits_grad_ref, middle_grad_ref, branch_grad_ref, mixture_grad_ref, gain_grad_ref = refs[
            parts:
        ]
        total = back_ref[...]
        for ref in refs[:parts]:
            total = total + ref[...].astype(f32)
        code = code_ref[...].astype(f32)
        lane = lax.broadcasted_iota(jnp.int32, (tokens, LANES), 1)
        router = jnp.where(
            lax.broadcasted_iota(jnp.int32, (MODEL_WIDTH, LANES), 1) < EXPERTS,
            router_ref[...],
            jnp.asarray(0.0, bf16),
        )
        logits = jnp.where(code > 0.5, dot(normed_ref[...], router), MASKED)
        raised = jnp.exp(logits - jnp.max(logits, axis=1, keepdims=True))
        raised = jnp.where(code > 0.5, raised, 0.0)
        gates = raised / jnp.sum(raised, axis=1, keepdims=True)
        extra = total[:, MODEL_WIDTH:]
        gate_grad = extra + pltpu.roll(extra, LANES - EXPERTS, 1)
        gate_grad = jnp.where((lane < EXPERTS) & (code > 0.5) & (code < 1.5), gate_grad, 0.0)
        inner = jnp.sum(gates * gate_grad, axis=1, keepdims=True)
        logits_grad = (gates * (gate_grad - inner)).astype(bf16)
        logits_grad_ref[...] = logits_grad
        incoming = total[:, :MODEL_WIDTH] + dot(logits_grad, router, NT)
        middle = middle_ref[...]
        norm_grad, gain_grad = norm_backward(
            middle, rms_inverse(middle), gain_ref[1:2], incoming
        )
        middle_grad = grad_ref[...].astype(f32) + norm_grad
        middle_grad_ref[...] = middle_grad
        branch_grad = (RESIDUAL_SCALE * middle_grad).astype(bf16)
        branch_grad_ref[...] = branch_grad
        mixture_grad_ref[...] = dot(branch_grad, weight_ref[...]).astype(bf16)
        gain_grad_ref[...] = jnp.broadcast_to(gain_grad, (8, MODEL_WIDTH))

    wide = MODEL_WIDTH + LANES
    return pl.pallas_call(
        kernel,
        grid=(1,),
        in_specs=[
            whole_block((tokens, wide)),
            whole_block((tokens, LANES)),
            whole_block((tokens, MODEL_WIDTH)),
            whole_block((tokens, MODEL_WIDTH)),
            whole_block((tokens, MODEL_WIDTH)),
            pl.BlockSpec(
                (MODEL_WIDTH, LANES),
                lambda *_: (0, 2 * PAIR_COLS // LANES),
                pipeline_mode=pl.Buffered(1),
            ),
            square_block(1),
            whole_block((8, MODEL_WIDTH)),
        ]
        + [whole_block((tokens, wide))] * parts,
        out_specs=[
            whole_block((tokens, LANES)),
            whole_block((tokens, MODEL_WIDTH)),
            whole_block((tokens, MODEL_WIDTH)),
            whole_block((tokens, QUERY_COLS)),
            whole_block((8, MODEL_WIDTH)),
        ],
        out_shape=[
            jax.ShapeDtypeStruct((tokens, LANES), bf16),
            jax.ShapeDtypeStruct((tokens, MODEL_WIDTH), f32),
            jax.ShapeDtypeStruct((tokens, MODEL_WIDTH), bf16),
            jax.ShapeDtypeStruct((tokens, QUERY_COLS), bf16),
            jax.ShapeDtypeStruct((8, MODEL_WIDTH), f32),
        ],
        compiler_params=params(),
        cost_estimate=cost(
            2 * tokens * MODEL_WIDTH * QUERY_COLS, 2 * MODEL_WIDTH * (QUERY_COLS + 12 * tokens)
        ),
        name="return_to_attention",
    )(back, code, normed_two, middle, out_grad, w_small, w_square, gains, *back_parts)


def store_rows(product, columns, place, core, kept_ref, sent_ref):
    heads, far, rows = kept_ref.shape[:3]
    for mine in range(2):

        @pl.when(core == mine)
        def _():
            for head in range(heads):
                for group in range(2 * far):
                    first = (head * 2 * far + group) * rows
                    piece = product[first : first + rows]
                    target = kept_ref if group % 2 == mine else sent_ref
                    target[head, (group // 2) ^ place, :, columns] = piece


def weight_terms(lefts, rights):
    tokens = lefts[0].shape[0]
    tile = 384
    operands, in_specs, runs = [], [], []
    first = 0
    for left, parts in zip(lefts, rights):
        left_at = len(operands)
        operands.append(left)
        in_specs.append(whole_block((tokens, MODEL_WIDTH)))
        for right in parts:
            steps = right.shape[1] // tile
            runs.append((first, steps, left_at, len(operands)))
            operands.append(right)
            in_specs.append(
                pl.BlockSpec(
                    (tokens, tile),
                    functools.partial(
                        lambda i, first, steps: (0, jnp.clip(i - first, 0, steps - 1)),
                        first=first,
                        steps=steps,
                    ),
                )
            )
            first = first + steps
    width = first * tile

    def kernel(*refs):
        step = pl.program_id(0)
        for start, steps, left_at, right_at in runs:

            @pl.when((step >= start) & (step < start + steps))
            def _():
                refs[-1][...] = dot(refs[left_at][...], refs[right_at][...], TN).astype(bf16)

    return pl.pallas_call(
        kernel,
        grid=(first,),
        in_specs=in_specs,
        out_specs=pl.BlockSpec((MODEL_WIDTH, tile), lambda i: (0, i)),
        out_shape=jax.ShapeDtypeStruct((MODEL_WIDTH, width), bf16),
        compiler_params=params(),
        cost_estimate=cost(
            2 * tokens * MODEL_WIDTH * width,
            2 * width * (MODEL_WIDTH + tokens),
        ),
        name="weight_terms",
    )(*operands)


def leave(
    place,
    heads,
    groups,
    terms,
    query_grads,
    cosine,
    sine,
    hidden_in,
    normed,
    middle_grad,
    normed_two,
    logits_grad,
    gain_grad_two,
    w_small,
    w_query,
    gains,
):
    tokens = hidden_in.shape[0]
    parts = len(terms)
    count = len(terms[0])
    part_cols = PAIR_COLS // parts
    query_cols = QUERY_COLS // parts
    small_cols = w_small.shape[1]
    part_shape = (heads, groups // 2, MODEL_WIDTH // (heads * groups), small_cols)

    def kernel(
        place_ref,
        cosine_ref,
        sine_ref,
        hidden_ref,
        normed_ref,
        middle_grad_ref,
        normed_two_ref,
        logits_grad_ref,
        gain_two_ref,
        small_ref,
        query_weight_ref,
        gain_ref,
        *refs,
    ):
        query_grad_refs, term_refs = refs[:parts], refs[parts:-3]
        input_grad_ref, kept_ref, sent_ref = refs[-3:]

        def store(product, columns):
            store_rows(
                product.astype(bf16), columns, place_ref[0], place_ref[1], kept_ref, sent_ref
            )

        keys, lists = [], []
        for part in range(parts):
            total = term_refs[part * count][...]
            for ref in term_refs[part * count + 1 : (part + 1) * count]:
                total = total + ref[...].astype(f32)
            keys.append(turn(total[0], cosine_ref[...], sine_ref[...], -1.0).astype(bf16))
            lists.append(total[1].astype(bf16))
        keys = jnp.concatenate(keys, axis=1)
        lists = jnp.concatenate(lists, axis=1)
        incoming = dot(keys, small_ref[:, :PAIR_COLS], NT) + dot(
            lists, small_ref[:, PAIR_COLS : 2 * PAIR_COLS], NT
        )
        for part in range(parts):
            columns = slice(part * query_cols, (part + 1) * query_cols)
            incoming = incoming + dot(
                query_grad_refs[part][...], query_weight_ref[:, columns], NT
            )
        values = hidden_ref[...].astype(f32)
        norm_grad, gain_grad = norm_backward(
            values, rms_inverse(values), gain_ref[:1], incoming
        )
        input_grad_ref[...] = middle_grad_ref[...] + norm_grad
        normed = normed_ref[...]
        store(dot(normed, keys, TN), slice(0, PAIR_COLS))
        store(dot(normed, lists, TN), slice(PAIR_COLS, 2 * PAIR_COLS))
        two = gain_two_ref[:1]
        first_high = gain_grad.astype(bf16).astype(f32)
        second_high = two.astype(bf16).astype(f32)
        rows = jnp.concatenate(
            [
                jnp.zeros((EXPERTS, MODEL_WIDTH), f32),
                first_high,
                second_high,
                gain_grad - first_high,
                two - second_high,
                jnp.zeros((LANES - EXPERTS - 4, MODEL_WIDTH), f32),
            ],
            axis=0,
        )
        extras = dot(normed_two_ref[...], logits_grad_ref[...], TN) + jnp.transpose(rows)
        store(extras, slice(2 * PAIR_COLS, small_cols))

    return pl.pallas_call(
        kernel,
        grid=(1,),
        in_specs=[
            pl.BlockSpec(memory_space=pltpu.SMEM),
            whole_block((tokens, LANES)),
            whole_block((tokens, LANES)),
            whole_block((tokens, MODEL_WIDTH)),
            whole_block((tokens, MODEL_WIDTH)),
            whole_block((tokens, MODEL_WIDTH)),
            whole_block((tokens, MODEL_WIDTH)),
            whole_block((tokens, LANES)),
            whole_block((8, MODEL_WIDTH)),
            whole_block((MODEL_WIDTH, small_cols)),
            square_block(0),
            whole_block((8, MODEL_WIDTH)),
        ]
        + [whole_block((tokens, query_cols))] * parts
        + [whole_block((2, tokens, part_cols))] * (parts * count),
        out_specs=[
            whole_block((tokens, MODEL_WIDTH)),
            whole_block(part_shape),
            whole_block(part_shape),
        ],
        out_shape=[
            jax.ShapeDtypeStruct((tokens, MODEL_WIDTH), f32),
            jax.ShapeDtypeStruct(part_shape, bf16),
            jax.ShapeDtypeStruct(part_shape, bf16),
        ],
        compiler_params=params(),
        cost_estimate=cost(
            2 * tokens * MODEL_WIDTH * (QUERY_COLS + 4 * PAIR_COLS),
            2 * MODEL_WIDTH * (QUERY_COLS + 2 * small_cols + 8 * tokens),
        ),
        name="leave",
    )(
        place,
        cosine,
        sine,
        hidden_in,
        normed,
        middle_grad,
        normed_two,
        logits_grad,
        gain_grad_two,
        w_small,
        w_query,
        gains,
        *query_grads,
        *[array for part in terms for array in part],
    )


def stacked_heads(block, pair):
    first = pair * GROUP * HEAD_WIDTH
    return jnp.concatenate(
        [
            block[:, first + j * HEAD_WIDTH : first + (j + 1) * HEAD_WIDTH]
            for j in range(GROUP)
        ],
        axis=0,
    )


def masked_scores(keys, queries, starts, offset, causal):
    tokens = keys.shape[0]
    scores = dot(keys, queries, NT)
    key_place = lax.broadcasted_iota(jnp.int32, (tokens, tokens), 0)
    visible = key_place + offset >= starts
    if causal:
        visible = visible & (key_place <= lax.broadcasted_iota(jnp.int32, (tokens, tokens), 1))
    parts = [
        jnp.where(visible, scores[:, j * tokens : (j + 1) * tokens], MASKED) for j in range(GROUP)
    ]
    return jnp.concatenate(parts, axis=1)


def kv_spec(tokens):
    return pl.BlockSpec((2, tokens, LANES), lambda i: (0, 0, i))


def attend(queries, key_values, starts, name):
    tokens = queries.shape[0]
    blocks = len(key_values)
    pairs = KEY_VALUE_HEADS // PAIRED
    width = PAIRED * GROUP * HEAD_WIDTH

    def kernel(starts_ref, query_ref, *refs):
        kv_refs, (out_ref, lse_ref) = refs[:blocks], refs[blocks:]
        starts_row = starts_ref[...]
        turned = []
        lse_rows = []
        for pair in range(PAIRED):
            lanes = slice(pair * HEAD_WIDTH, (pair + 1) * HEAD_WIDTH)
            stacked = stacked_heads(query_ref[...], pair) * jnp.asarray(ATTN_SCALE, bf16)
            scores = [
                masked_scores(
                    kv_refs[b][0, :, lanes],
                    stacked,
                    starts_row,
                    (b - blocks + 1) * tokens,
                    b == blocks - 1,
                )
                for b in range(blocks)
            ]
            top = functools.reduce(
                jnp.maximum, [jnp.max(s, axis=0, keepdims=True) for s in scores]
            )
            total = jnp.zeros_like(top)
            mixed = jnp.zeros((HEAD_WIDTH, GROUP * tokens), f32)
            for b in range(blocks):
                weights = jnp.exp(scores[b] - top)
                total = total + jnp.sum(weights, axis=0, keepdims=True)
                mixed = mixed + dot(kv_refs[b][1, :, lanes], weights.astype(bf16), TN)
            mixed = mixed / total
            lse = top + jnp.log(total)
            for j in range(GROUP):
                columns = slice(j * tokens, (j + 1) * tokens)
                turned.append(mixed[:, columns])
                lse_rows.append(lse[:, columns])
        out_ref[...] = jnp.transpose(jnp.concatenate(turned, axis=0)).astype(bf16)
        lse_rows = lse_rows + [jnp.zeros((1, tokens), f32)] * (8 - len(lse_rows))
        lse_ref[0] = jnp.concatenate(lse_rows, axis=0)

    scores_count = QUERY_HEADS * tokens * tokens * blocks
    return pl.pallas_call(
        kernel,
        grid=(pairs,),
        in_specs=[
            whole_block((1, tokens)),
            pl.BlockSpec((tokens, width), lambda i: (0, i)),
        ]
        + [kv_spec(tokens)] * blocks,
        out_specs=[
            pl.BlockSpec((tokens, width), lambda i: (0, i)),
            pl.BlockSpec((1, 8, tokens), lambda i: (i, 0, 0)),
        ],
        out_shape=[
            jax.ShapeDtypeStruct((tokens, QUERY_COLS), bf16),
            jax.ShapeDtypeStruct((pairs, 8, tokens), f32),
        ],
        compiler_params=pltpu.CompilerParams(vmem_limit_bytes=VMEM_BYTES),
        cost_estimate=pl.CostEstimate(
            flops=4 * scores_count * HEAD_WIDTH,
            bytes_accessed=4 * tokens * (QUERY_COLS + blocks * PAIR_COLS),
            transcendentals=scores_count,
        ),
        name=name,
    )(starts, queries, *key_values)


def attend_backward(
    queries, key_values, starts, mixture_grad, lse, cosine, sine, part, parts, name
):
    tokens = queries.shape[0]
    blocks = len(key_values)
    pairs = KEY_VALUE_HEADS // PAIRED // parts
    first = part * pairs
    width = PAIRED * GROUP * HEAD_WIDTH

    def kernel(starts_ref, query_ref, grad_ref, lse_ref, cosine_ref, sine_ref, *refs):
        kv_refs = refs[:blocks]
        dq_ref = refs[blocks]
        dkv_refs = refs[blocks + 1 : 2 * blocks + 1]
        probs_ref, prob_grad_ref = refs[2 * blocks + 1 :]
        starts_row = starts_ref[...]
        turned = []
        for pair in range(PAIRED):
            lanes = slice(pair * HEAD_WIDTH, (pair + 1) * HEAD_WIDTH)
            stacked = stacked_heads(query_ref[...], pair) * jnp.asarray(ATTN_SCALE, bf16)
            incoming = stacked_heads(grad_ref[...], pair)
            lse_row = jnp.concatenate(
                [lse_ref[0, pair * GROUP + j : pair * GROUP + j + 1, :] for j in range(GROUP)],
                axis=1,
            )
            delta = jnp.zeros((1, GROUP * tokens), f32)
            for b in range(blocks):
                scores = masked_scores(
                    kv_refs[b][0, :, lanes],
                    stacked,
                    starts_row,
                    (b - blocks + 1) * tokens,
                    b == blocks - 1,
                )
                probs = jnp.exp(scores - lse_row)
                prob_grad = dot(kv_refs[b][1, :, lanes], incoming, NT)
                delta = delta + jnp.sum(probs * prob_grad, axis=0, keepdims=True)
                probs_ref[b] = probs
                prob_grad_ref[b] = prob_grad
            query_grad = jnp.zeros((HEAD_WIDTH, GROUP * tokens), f32)
            for b in range(blocks):
                probs = probs_ref[b]
                score_grad = (probs * (prob_grad_ref[b] - delta)).astype(bf16)
                query_grad = query_grad + dot(kv_refs[b][0, :, lanes], score_grad, TN)
                key_part = dot(score_grad, stacked)
                value_part = dot(probs.astype(bf16), incoming)
                dkv_refs[b][0, :, lanes] = key_part.astype(dkv_refs[b].dtype)
                dkv_refs[b][1, :, lanes] = value_part.astype(dkv_refs[b].dtype)
            query_grad = query_grad * ATTN_SCALE
            for j in range(GROUP):
                turned.append(query_grad[:, j * tokens : (j + 1) * tokens])
        query_grad = jnp.transpose(jnp.concatenate(turned, axis=0))
        dq_ref[...] = turn(query_grad, cosine_ref[...], sine_ref[...], -1.0).astype(bf16)

    scores_count = QUERY_HEADS // parts * tokens * tokens * blocks
    return pl.pallas_call(
        kernel,
        grid=(pairs,),
        in_specs=[
            whole_block((1, tokens)),
            pl.BlockSpec((tokens, width), lambda i: (0, first + i)),
            pl.BlockSpec((tokens, width), lambda i: (0, first + i)),
            pl.BlockSpec((1, 8, tokens), lambda i: (first + i, 0, 0)),
            whole_block((tokens, LANES)),
            whole_block((tokens, LANES)),
        ]
        + [pl.BlockSpec((2, tokens, LANES), lambda i: (0, 0, first + i))] * blocks,
        out_specs=[pl.BlockSpec((tokens, width), lambda i: (0, i))] + [kv_spec(tokens)] * blocks,
        out_shape=[jax.ShapeDtypeStruct((tokens, QUERY_COLS // parts), bf16)]
        + [jax.ShapeDtypeStruct((2, tokens, PAIR_COLS // parts), bf16)] * (blocks - 1)
        + [jax.ShapeDtypeStruct((2, tokens, PAIR_COLS // parts), f32)],
        scratch_shapes=[pltpu.VMEM((blocks, tokens, GROUP * tokens), f32)] * 2,
        compiler_params=pltpu.CompilerParams(vmem_limit_bytes=VMEM_BYTES),
        cost_estimate=pl.CostEstimate(
            flops=10 * scores_count * HEAD_WIDTH,
            bytes_accessed=4 * tokens * (2 * QUERY_COLS + 2 * blocks * PAIR_COLS),
            transcendentals=scores_count,
        ),
        name=name,
    )(starts, queries, mixture_grad, lse, cosine, sine, *key_values)


def expert_block(index):
    return pl.BlockSpec((MODEL_WIDTH, FF), lambda *_: (0, index), pipeline_mode=pl.Buffered(1))


def experts(order, inputs, grads, scaled, w_small, w_up, w_down, expert, tokens):
    rows = inputs.shape[0]
    wide = MODEL_WIDTH + LANES
    fresh = scaled is None

    def kernel(
        order_ref, expert_ref, input_ref, grad_ref, router_ref, gate_ref, up_ref, down_ref, *refs
    ):
        scaled_ref, hidden_grad_ref, input_grad_ref = refs if fresh else refs[1:]
        block = input_ref[...]
        code = grad_ref[:, MODEL_WIDTH:].astype(f32)
        lane = lax.broadcasted_iota(jnp.int32, (tokens, LANES), 1)
        logits = jnp.where(code > 0.5, dot(block, router_ref[...]), MASKED)
        raised = jnp.exp(logits - jnp.max(logits, axis=1, keepdims=True))
        raised = jnp.where(code > 0.5, raised, 0.0)
        gates = raised / jnp.sum(raised, axis=1, keepdims=True)
        kept = (lane == expert_ref[0]) & (code > 0.5) & (code < 1.5)
        gate = jnp.sum(jnp.where(kept, gates, 0.0), axis=1, keepdims=True)
        gate_part = dot(block, gate_ref[...])
        up_part = dot(block, up_ref[...])
        sigmoid = 1.0 / (1.0 + jnp.exp(-gate_part))
        silu = gate_part * sigmoid
        activation = silu * up_part
        scaled_ref[...] = (activation * gate).astype(bf16)
        pulled = dot(grad_ref[:, :MODEL_WIDTH], down_ref[...])
        gate_grad = RESIDUAL_SCALE * jnp.sum(activation * pulled, axis=1, keepdims=True)
        high = gate_grad.astype(bf16).astype(f32)
        columns = jnp.where(
            lane == expert_ref[0],
            high,
            jnp.where(lane == expert_ref[0] + EXPERTS, gate_grad - high, 0.0),
        )
        input_grad_ref[:, MODEL_WIDTH:] = columns.astype(bf16)
        activation_grad = pulled * (RESIDUAL_SCALE * gate)
        slope = sigmoid * (1.0 + gate_part * (1.0 - sigmoid))
        gate_part_grad = (activation_grad * up_part * slope).astype(bf16)
        up_part_grad = (activation_grad * silu).astype(bf16)
        hidden_grad_ref[:, :FF] = gate_part_grad
        hidden_grad_ref[:, FF:] = up_part_grad
        input_grad_ref[:, :MODEL_WIDTH] = (
            dot(gate_part_grad, gate_ref[...], NT) + dot(up_part_grad, up_ref[...], NT)
        ).astype(bf16)

    in_specs = [
        pl.BlockSpec(memory_space=pltpu.SMEM),
        pl.BlockSpec((tokens, MODEL_WIDTH), lambda i, order_ref: (i, 0)),
        pl.BlockSpec((tokens, wide), lambda i, order_ref: (order_ref[i], 0)),
        pl.BlockSpec(
            (MODEL_WIDTH, LANES),
            lambda *_: (0, 2 * PAIR_COLS // LANES),
            pipeline_mode=pl.Buffered(1),
        ),
        expert_block(0),
        expert_block(1),
        expert_block(0),
    ]
    operands = [order, expert, inputs, grads, w_small, w_up, w_up, w_down]
    if not fresh:
        in_specs.append(pl.BlockSpec(memory_space=pl.ANY))
        operands.append(scaled)
    return pl.pallas_call(
        kernel,
        grid_spec=pltpu.PrefetchScalarGridSpec(
            num_scalar_prefetch=1,
            grid=(rows // tokens,),
            in_specs=in_specs,
            out_specs=[
                pl.BlockSpec((tokens, FF), lambda i, order_ref: (order_ref[i], 0)),
                pl.BlockSpec((tokens, 2 * FF), lambda i, order_ref: (i, 0)),
                pl.BlockSpec((tokens, wide), lambda i, order_ref: (i, 0)),
            ],
        ),
        out_shape=[
            jax.ShapeDtypeStruct((grads.shape[0], FF), bf16),
            jax.ShapeDtypeStruct((rows, 2 * FF), bf16),
            jax.ShapeDtypeStruct((rows, wide), bf16),
        ],
        input_output_aliases={} if fresh else {8: 0},
        compiler_params=params(),
        cost_estimate=cost(
            10 * rows * MODEL_WIDTH * FF,
            2 * MODEL_WIDTH * (3 * rows + EXPERT_COLS),
            rows * FF,
        ),
        name="experts",
    )(*operands)


def expert_shares(orders, scaled, weights, tokens, groups):
    count = len(scaled)

    def kernel(orders_ref, *refs):
        weight_ref, out_ref = refs[count:]
        for k in range(count):

            @pl.when(pl.program_id(1) == k)
            def _():
                out_ref[...] = dot(refs[k][...], weight_ref[...], NT).astype(bf16)

    def piece_spec(piece):
        return pl.BlockSpec(
            (tokens, FF), lambda i, k, orders_ref: (orders_ref[piece * groups + i], 0)
        )

    rows = groups * count * tokens
    return pl.pallas_call(
        kernel,
        grid_spec=pltpu.PrefetchScalarGridSpec(
            num_scalar_prefetch=1,
            grid=(groups, count),
            in_specs=[piece_spec(k) for k in range(count)] + [expert_block(0)],
            out_specs=pl.BlockSpec(
                (tokens, MODEL_WIDTH), lambda i, k, orders_ref: (i * count + k, 0)
            ),
        ),
        out_shape=jax.ShapeDtypeStruct((rows, MODEL_WIDTH), bf16),
        compiler_params=params(),
        cost_estimate=cost(
            2 * rows * MODEL_WIDTH * FF, 2 * MODEL_WIDTH * (rows + FF) + 2 * rows * FF
        ),
        name="expert_shares",
    )(orders, *scaled, weights)


def expert_terms(pieces, scale, name):
    width = pieces[0][1].shape[1]
    tile = 384
    rows = sum(left.shape[0] for left, _ in pieces)

    def kernel(*refs):
        total = None
        for k in range(len(pieces)):
            term = dot(refs[2 * k][...], refs[2 * k + 1][...], TN)
            total = term if total is None else total + term
        refs[-1][...] = (scale * total).astype(bf16)

    in_specs = []
    for left, right in pieces:
        in_specs.append(pl.BlockSpec((left.shape[0], tile), lambda i: (0, i)))
        in_specs.append(whole_block(right.shape))
    return pl.pallas_call(
        kernel,
        grid=(MODEL_WIDTH // tile,),
        in_specs=in_specs,
        out_specs=pl.BlockSpec((tile, width), lambda i: (i, 0)),
        out_shape=jax.ShapeDtypeStruct((MODEL_WIDTH, width), bf16),
        compiler_params=params(),
        cost_estimate=cost(
            2 * rows * MODEL_WIDTH * width, 2 * (rows + width) * MODEL_WIDTH + 2 * rows * width
        ),
        name=name,
    )(*[array for piece in pieces for array in piece])


def shards(
    hidden_in,
    out_grad,
    doc_lengths,
    expert_ids,
    attention_norm,
    query_weight,
    key_matrix,
    value_matrix,
    output_weight,
    expert_norm,
    router_weight,
    expert_input,
    expert_output,
):
    tokens = hidden_in.shape[0]
    heads = lax.axis_size("head")
    groups = lax.axis_size("seq")
    own_rows = query_weight.shape[0]
    head_index = lax.axis_index("head")
    seq_index = lax.axis_index("seq")
    shared = EXPERTS // groups
    first_row = (seq_index * heads + head_index) * tokens
    expert = (seq_index * shared + head_index % shared).astype(jnp.int32)[None]

    places = first_row + jnp.arange(tokens)
    starts = doc_start(doc_lengths, places)
    cosine, sine = rope_tables(places - starts)
    starts_row = (starts - first_row).astype(jnp.int32)[None, :]

    hot = (expert_ids[:, :, None] == jnp.arange(EXPERTS)[None, None, :]).astype(f32)
    chosen = jnp.sum(hot, axis=1)
    before = (jnp.arange(tokens)[:, None] > jnp.arange(tokens)[None, :]).astype(bf16)
    earlier = dot(before, chosen.astype(bf16))
    code = jnp.where(chosen > 0.5, jnp.where(earlier < CAP - 0.5, 1.0, 2.0), 0.0)
    code = jnp.concatenate(
        [code.astype(bf16), jnp.zeros((tokens, LANES - EXPERTS), bf16)], axis=1
    )
    coded_grad = jnp.concatenate([out_grad, code], axis=1)

    def spread(block, axes):
        return lax.all_to_all(block, axes, split_axis=0, concat_axis=0, tiled=True)

    clock = Clock()
    small = jnp.concatenate(
        [
            key_matrix,
            value_matrix,
            router_weight,
            attention_norm[:, None],
            expert_norm[:, None],
            jnp.zeros((own_rows, LANES - EXPERTS - 2), bf16),
        ],
        axis=1,
    )
    w_small = lax.all_gather(small, ("head", "seq"), axis=0, tiled=True)

    def expert_rows(weight):
        weight = weight.reshape(own_rows, groups, shared, weight.shape[2])
        weight = jnp.tile(jnp.transpose(weight, (2, 1, 0, 3)), (heads // shared, 1, 1, 1))
        return Flow(
            one_move(
                weight.reshape(heads * groups, own_rows, weight.shape[3]),
                functools.partial(spread, axes=("head", "seq")),
            )
        )

    up_flow = expert_rows(expert_input)
    far_grads = [Flow(one_move(coded_grad, by_head(step))) for step in range(1, shared)]
    pending = clock.begin(up_flow, *far_grads)

    normed, own_kv, gains = enter(hidden_in, w_small, cosine, sine)
    clock.end(pending, own_kv)
    kv_flows = [
        Flow(one_move(own_kv, functools.partial(along_stream, distance=distance)))
        for distance in range(1, heads + 1)
    ]
    w_large = lax.all_gather(
        jnp.concatenate([query_weight, output_weight], axis=1),
        ("head", "seq"),
        axis=0,
        tiled=True,
    )
    grad_flows = [Flow(tokens_gather(flow.value)) for flow in far_grads]
    clock.tick(kv_flows[0], kv_flows[-1], *grad_flows)
    clock.tick(*kv_flows[1:-1], *grad_flows)
    key_values = [flow.value for flow in kv_flows[::-1]] + [own_kv]
    down_flow = expert_rows(after(expert_output, *clock.last))
    Clock().tick(down_flow)
    w_up = up_flow.value.reshape(MODEL_WIDTH, 2 * FF)
    w_down = down_flow.value.reshape(MODEL_WIDTH, FF)
    queries = project_queries(normed, w_large, cosine, sine)
    mixture, lse = attend(queries, key_values, starts_row, "attend")
    middle, normed_two = leave_attention(mixture, w_large, hidden_in, gains)

    input_flows = [Flow(tokens_gather(normed_two))]
    far_tokens = [Flow(one_move(normed_two, by_head(step))) for step in range(1, shared)]
    for flow in grad_flows:
        clock.finish(flow)
    grad_cores = [Flow(one_move(flow.value, by_seq(1))) for flow in grad_flows]
    clock.tick(input_flows[0], *far_tokens, *grad_cores, ready=(down_flow.value,))

    def seq_gather(block):
        return lax.all_gather(block, "seq", axis=0, tiled=True)

    grads = [seq_gather(after(coded_grad, *key_values))] + [
        jnp.concatenate([flow.value, core.value], axis=0)
        for flow, core in zip(grad_flows, grad_cores)
    ]
    input_flows = input_flows + [Flow(tokens_gather(flow.value)) for flow in far_tokens]
    clock.tick(input_flows[0])
    core_flows = [Flow(one_move(clock.finish(input_flows[0]), by_seq(1)))]

    back = []
    inputs = {}
    hidden_grads = {}
    scaled = [None] * shared
    turn_of = expert
    blocks = jnp.arange(groups // 2, dtype=jnp.int32) * 2
    for step in range(shared):
        terms = []
        inputs[step, 0] = clock.finish(input_flows[step])
        if step > 0:
            core_flows.append(Flow(one_move(inputs[step, 0], by_seq(1))))
        pending = clock.begin(*core_flows[step:], *input_flows[step + 1 :], *back)
        for core in range(2):
            if core == 1:
                clock.end(pending, turn_of)
                pending = clock.begin(*input_flows[step + 1 :], *back)
                inputs[step, 1] = clock.finish(core_flows[step])
            if step == 0:
                order = (blocks + core) ^ seq_index
            else:
                order = core * (groups // 2) + jnp.arange(groups // 2)
            scaled[step], hidden_grads[step, core], input_grad = experts(
                order.astype(jnp.int32),
                inputs[step, core],
                grads[step],
                scaled[step],
                w_small,
                w_up,
                w_down,
                turn_of,
                tokens,
            )
            turn_of = after(expert, input_grad)
            terms.append(input_grad)
        clock.end(pending, turn_of)
        back.append(Flow(tokens_scatter(*terms)))

    everyone = jnp.arange(groups)
    place_of = everyone ^ seq_index
    place_of = (place_of % 2) * (groups // 2) + place_of // 2
    orders = jnp.concatenate([everyone] + [place_of] * (shared - 1)).astype(jnp.int32)
    work = [
        lambda first: expert_shares(
            orders, [after(part, first) for part in scaled], w_down, tokens, groups
        ),
        lambda first: expert_terms(
            [(inputs[key], after(hidden_grads[key], first)) for key in inputs], 1.0, "up_terms"
        ),
        lambda first: expert_terms(
            [(grad, after(part, first)) for grad, part in zip(grads, scaled)],
            RESIDUAL_SCALE,
            "down_terms",
        ),
    ]
    made = []
    while not all(flow.done for flow in back):
        pending = clock.begin(*back)
        held = ()
        if len(made) < len(work):
            made.append(work[len(made)](after(turn_of, *clock.last)))
            turn_of = after(expert, made[-1])
            held = (turn_of,)
        clock.end(pending, *held)
    back_parts = [
        Flow(one_move(back[step].value.astype(bf16), by_head(step))) for step in range(1, shared)
    ]
    pending = clock.begin(*back_parts)
    while len(made) < len(work):
        made.append(work[len(made)](after(turn_of, *clock.last)))
        turn_of = after(expert, made[-1])
    clock.end(pending, turn_of)
    shares, up_part, down_part = made
    shares = lax.psum_scatter(shares, "seq", scatter_dimension=0, tiled=True)
    expert_part = jnp.concatenate([up_part, down_part], axis=1)
    expert_part = expert_part.reshape(heads * groups, own_rows, EXPERT_COLS)
    expert_flow = Flow(
        one_move(expert_part, functools.partial(spread, axes=("head", "seq")))
    )
    pending = clock.begin(expert_flow)
    logits_grad, middle_grad, branch_grad, mixture_grad, gain_grad_two = return_to_attention(
        back[0].value,
        [flow.value for flow in back_parts],
        code,
        normed_two,
        middle,
        out_grad,
        w_small,
        w_large,
        gains,
    )

    place = jnp.stack([seq_index // 2, seq_index % 2]).astype(jnp.int32)
    query_grad, *kv_terms = attend_backward(
        queries,
        key_values,
        starts_row,
        mixture_grad,
        lse,
        cosine,
        sine,
        0,
        1,
        "attend_backward",
    )
    query_grads = [query_grad]
    large_part = weight_terms(
        [normed, after(branch_grad, query_grad)], [query_grads, [mixture]]
    )
    clock.end(pending, large_part)
    large_part = lax.psum_scatter(large_part, ("head", "seq"), scatter_dimension=0, tiled=True)
    kv_flows = [
        Flow(one_move(term, functools.partial(along_stream, distance=-distance)))
        for term, distance in zip(kv_terms[:-1], range(heads, 0, -1))
    ]
    share_flows = [
        Flow(one_move(shares[step * tokens : (step + 1) * tokens], by_head(step)))
        for step in range(1, shared)
    ]
    clock.tick(*kv_flows, *share_flows)
    terms = [(kv_terms[-1], kv_flows)]
    input_grad, *small_parts = leave(
        place,
        heads,
        groups,
        [[own] + [flow.value for flow in flows] for own, flows in terms],
        query_grads,
        cosine,
        sine,
        after(hidden_in, shares),
        normed,
        middle_grad,
        normed_two,
        logits_grad,
        gain_grad_two,
        w_small,
        w_large,
        gains,
    )

    small_flow = Flow(rows_scatter(*small_parts))
    small_flow = Flow(line_scatter(clock.finish(small_flow)))
    clock.finish(small_flow)
    moe_out = shares[:tokens].astype(f32)
    for flow in share_flows:
        moe_out = moe_out + flow.value.astype(f32)
    block_out = (middle + RESIDUAL_SCALE * moe_out).astype(bf16)

    expert_sum = expert_flow.value.reshape(
        heads // shared, shared, groups, own_rows, EXPERT_COLS
    )
    expert_sum = jnp.sum(expert_sum.astype(f32), axis=0)

    def expert_output_of(first, last):
        columns = jnp.transpose(expert_sum[..., first:last], (2, 1, 0, 3))
        return columns.reshape(own_rows, EXPERTS, last - first)

    expert_input_grad = expert_output_of(0, 2 * FF)
    expert_output_grad = expert_output_of(2 * FF, EXPERT_COLS)
    large_sum = after(large_part, small_flow.value).astype(f32)
    query_weight_grad = large_sum[:, :QUERY_COLS]
    output_grad = large_sum[:, QUERY_COLS:]
    small_sum = small_flow.value
    key_grad = small_sum[:, :PAIR_COLS]
    value_grad = small_sum[:, PAIR_COLS : 2 * PAIR_COLS]
    rest = small_sum[:, 2 * PAIR_COLS :]
    router_grad = rest[:, :EXPERTS]
    attention_norm_grad = rest[:, EXPERTS] + rest[:, EXPERTS + 2]
    expert_norm_grad = rest[:, EXPERTS + 1] + rest[:, EXPERTS + 3]
    return (
        block_out,
        input_grad,
        attention_norm_grad,
        query_weight_grad,
        key_grad,
        value_grad,
        output_grad,
        expert_norm_grad,
        router_grad,
        expert_input_grad,
        expert_output_grad,
    )


def solution(mesh):
    return jax.shard_map(
        shards,
        mesh=mesh,
        in_specs=(
            P(("seq", "head"), None),
            P(("seq", "head"), None),
            P(),
            P(("seq", "head"), None),
            P(("head", "seq")),
            P(("head", "seq"), None),
            P(("head", "seq"), None),
            P(("head", "seq"), None),
            P(("head", "seq"), None),
            P(("head", "seq")),
            P(("head", "seq"), None),
            P(("head", "seq"), None, None),
            P(("head", "seq"), None, None),
        ),
        out_specs=(
            P(("seq", "head"), None),
            P(("seq", "head"), None),
            P(("head", "seq")),
            P(("head", "seq"), None),
            P(("head", "seq"), None),
            P(("head", "seq"), None),
            P(("head", "seq"), None),
            P(("head", "seq")),
            P(("head", "seq"), None),
            P(("head", "seq"), None, None),
            P(("head", "seq"), None, None),
        ),
        check_vma=False,
    )
```
